32 devices in a mesh: region: 2 (over x), owner: 16 (over z, y, core).
Axes of the slice: x: 2, y: 2, z: 4, core: 2. Of those that a mesh axis runs over, the one named last changes fastest.
Arguments:
- voxels: bfloat16 [2, 16, 1, 256, 1024], P('region', 'owner'), may hold values from -6 to 6
- norm_gain: float32 [1024], replicated, may hold values from 0.5 to 1.5
- qkv_weight: bfloat16 [1024, 3072], P(('region', 'owner')), may hold values from -0.14453125 to 0.14453125
- out_weight: bfloat16 [1024, 1024], P(('region', 'owner')), may hold values from -0.1875 to 0.1875
- neighbours: int32 [2, 16, 1, 8], P('region', 'owner'), may hold values from -1 to 31, as said below
Outputs:
- attended_voxels: bfloat16 [2, 16, 1, 256, 1024], P('region', 'owner')
The draws below stay inside these ranges and needn't reach their ends.
Inputs may be any that keep to these rules, and one draw needn't show every extreme that they name: `neighbours`: each entry is -1 or the number (r * 16 + o) + c of a block c held by the device at region r and owner o, where r and o each differ by at most one from those of the list's own block; a list never names its own block and names no block twice.
All inputs are finite; a program needn't handle non-finite values.
Results may differ from the reference program's by a relative error of at most 0.0057.
Values may be sent and summed in bfloat16 or wider, within the bound.
A program may use at most 64 MiB of HBM per device.

```python
import jax
import jax.numpy as jnp
from jax import lax

D = 1024
HEADS = 16
HEAD_DIM = 64
S = 256
CAP = 1
NBR = 8
REGIONS = 2
OWNERS = 16


def common_direction(key):
    base = jax.random.normal(jax.random.fold_in(key, 501), (D,), jnp.float32)
    base = jnp.clip(base, -2.2, 2.2)
    base = base - jnp.mean(base)
    return base / jnp.sqrt(jnp.mean(base * base))


def draw_voxels(key, part):
    shape = (REGIONS, OWNERS, CAP, S, D)
    return jax.random.truncated_normal(jax.random.fold_in(key, 504), -6.0, 6.0, shape, jnp.float32).astype(jnp.bfloat16)


def draw_qkv_weight(key, part):
    direction = common_direction(key)
    random_part = jax.random.truncated_normal(jax.random.fold_in(key, 511), -4.0, 4.0, (D, 3 * D), jnp.float32) * D ** (-0.5)
    levels = jax.random.permutation(jax.random.fold_in(key, 512), HEADS).astype(jnp.float32) / (HEADS - 1)
    strength = 7.0 ** levels
    signs = jnp.where(jax.random.bernoulli(jax.random.fold_in(key, 513), 0.5, (HEADS, HEAD_DIM)), 1.0, -1.0)
    pattern = (strength[:, None] * signs).reshape(D) / D
    aligned = direction[:, None] * pattern[None, :]
    blank = jnp.zeros((D, D), jnp.float32)
    return (random_part + jnp.concatenate([aligned, aligned, blank], axis=1)).astype(jnp.bfloat16)


def draw_neighbours(key, part):
    candidate_count = 9 * CAP
    region_ids = jnp.arange(REGIONS, dtype=jnp.int32)[:, None, None, None]
    owner_ids = jnp.arange(OWNERS, dtype=jnp.int32)[None, :, None, None]
    slot_ids = jnp.arange(CAP, dtype=jnp.int32)[None, None, :, None]
    candidate_ids = jnp.arange(candidate_count, dtype=jnp.int32)[None, None, None, :]
    noise = jax.random.randint(jax.random.fold_in(key, 11), (REGIONS, OWNERS, CAP, candidate_count), 0, 1 << 20)
    ranking = noise * 64 + candidate_ids
    ranking = jnp.where(candidate_ids == 4 * CAP + slot_ids, 1 << 30, ranking)
    chosen = jnp.argsort(ranking, axis=-1, stable=True)[..., :NBR].astype(jnp.int32)
    device_pos = chosen // CAP
    other_slot = chosen % CAP
    far_region = region_ids + device_pos // 3 - 1
    far_owner = owner_ids + device_pos % 3 - 1
    inside = (far_region >= 0) & (far_region < REGIONS) & (far_owner >= 0) & (far_owner < OWNERS)
    keeping = jax.random.randint(jax.random.fold_in(key, 12), (REGIONS, OWNERS, CAP, NBR), 0, 10) < 7
    numbers = (far_region * OWNERS + far_owner) * CAP + other_slot
    return jnp.where(inside & keeping, numbers, -1).astype(jnp.int32)


def level_of(rng, extent, cuts, least, high):
    loudness, own = 1.0, jax.random.fold_in(rng, 6)
    for axis_at, blocks in cuts:
        draws = jnp.exp(jax.random.uniform(jax.random.fold_in(own, axis_at), (blocks,), jnp.float32, least / len(cuts), high / len(cuts)))
        loudness = loudness * jnp.repeat(draws, extent[axis_at] // blocks).reshape([-1 if axis == axis_at else 1 for axis in range(len(extent))])
    return loudness


def centred(key, dims, deviation, most, cuts=(), held_as=jnp.bfloat16):
    values = jax.random.normal(key, dims, jnp.float32) * deviation
    if len(cuts) > 0:
        values = level_of(key, dims, cuts, -0.22, 0.18) * values
    return jnp.clip(values, min=-most, max=most).astype(held_as)


def setup_inputs(seed: int = 0) -> dict:
    seeds = jax.random.split(jax.random.key(seed), 6)
    return {
        "voxels": draw_voxels(jax.random.fold_in(seeds[5], 71), 0),
        "norm_gain": jnp.clip(1.0 + 0.1 * jax.random.normal(seeds[1], (D,), jnp.float32), 0.5, 1.5),
        "qkv_weight": draw_qkv_weight(jax.random.fold_in(seeds[5], 71), 0),
        "out_weight": centred(seeds[3], (D, D), D ** -0.5, 0.1875, ((0, 32),)),
        "neighbours": draw_neighbours(jax.random.fold_in(seeds[5], 71), 0),
    }


def layer_norm(inputs, norm_gain):
    widened = inputs.astype(jnp.float32)
    average = lax.optimization_barrier(jnp.mean(widened, axis=-1, keepdims=True))
    spread = lax.optimization_barrier(jnp.mean((widened - average) ** 2, axis=-1, keepdims=True))
    return ((widened - average) * lax.rsqrt(spread + 1e-06) * norm_gain).astype(jnp.bfloat16)

def reference(voxels, norm_gain, qkv_weight, out_weight, neighbours):
    model_width = voxels.shape[-1]
    block_size = voxels.shape[3]
    flat_tokens = voxels.reshape(-1, model_width)
    normed = layer_norm(flat_tokens, norm_gain)
    qkv = jnp.dot(normed, qkv_weight, preferred_element_type=jnp.float32).astype(jnp.bfloat16)
    queries = qkv[:, :model_width].reshape(-1, block_size, HEADS, HEAD_DIM)
    key_table = qkv[:, model_width:2 * model_width].reshape(-1, block_size, HEADS, HEAD_DIM)
    value_table = qkv[:, 2 * model_width:].reshape(-1, block_size, HEADS, HEAD_DIM)
    block_count = queries.shape[0]
    block_ids = jnp.arange(block_count, dtype=jnp.int32)
    key_lists = jnp.concatenate([block_ids[:, None], neighbours.reshape(block_count, NBR).astype(jnp.int32)], axis=1)
    score_scale = HEAD_DIM ** (-0.5)

    def attend(operands):
        query_block, key_list = operands
        present = key_list >= 0
        clamped = jnp.where(present, key_list, 0).astype(jnp.int32)
        key_rows = key_table[clamped].reshape(-1, HEADS, HEAD_DIM).astype(jnp.float32)
        value_rows = value_table[clamped].reshape(-1, HEADS, HEAD_DIM).astype(jnp.float32)
        scores = jnp.einsum('shd,khd->hsk', query_block.astype(jnp.float32), key_rows) * score_scale
        key_mask = jnp.repeat(present, block_size)
        scores = jnp.where(key_mask[None, None, :], scores, -1e+30)
        attn_probs = jax.nn.softmax(scores, axis=-1).astype(jnp.bfloat16)
        attended = jnp.einsum('hsk,khd->shd', attn_probs.astype(jnp.float32), value_rows)
        return attended.reshape(block_size, model_width).astype(jnp.bfloat16)
    mixed = lax.map(attend, (queries, key_lists))
    projected = jnp.dot(mixed.reshape(-1, model_width), out_weight, preferred_element_type=jnp.float32)
    result = flat_tokens.astype(jnp.float32) + projected
    return result.astype(jnp.bfloat16).reshape(voxels.shape)
```

```python
import functools

import jax
import jax.numpy as jnp
from jax import lax
from jax.experimental import pallas as pl
from jax.experimental.pallas import tpu as pltpu
from jax.sharding import PartitionSpec as P

HEAD_DIM = 64
MESH = pl.DeviceIdType.MESH
PLANE = 8
CHUNKS = 4
MASKED = -1e30


def padded(value, sides, width):
    for axis, dim in sides:
        devices, length = (lax.axis_size(axis), value.shape[dim])
        up = [(i, (i + 1) % devices) for i in range(devices - 1)]
        down = [(j, i) for i, j in up]
        last = lax.slice_in_dim(value, length - width, length, axis=dim)
        first = lax.slice_in_dim(value, 0, width, axis=dim)
        before = lax.ppermute(last, axis, up)
        after = lax.ppermute(first, axis, down)
        value = jnp.concatenate([before, value, after], axis=dim)
    return value


def layer_norm(inputs, norm_gain):
    widened = inputs.astype(jnp.float32)
    average = jnp.mean(widened, axis=-1, keepdims=True)
    spread = jnp.mean((widened - average) ** 2, axis=-1, keepdims=True)
    return ((widened - average) * lax.rsqrt(spread + 1e-06) * norm_gain).astype(jnp.bfloat16)


def fused_kernel(owners, x_ref, wq_ref, wo_ref, gain_ref, near_ref, out_ref,
                 cut_ref, w_ref, go_ref, blocks_ref, own_tab_ref, tabs_ref,
                 ql_ref, qh_ref, kl_ref, kh_ref, vl_ref, vh_ref,
                 edge_out_ref, edge_in_ref, staged_ref, mixed_ref,
                 send_w, recv_w, send_t, recv_t, send_z, recv_z, send_oz, recv_oz,
                 send_b, recv_b, send_o, recv_o, send_e, recv_e, send_m, recv_m):
    tokens, width = x_ref.shape
    depth = wo_ref.shape[0]
    share = 2 * HEAD_DIM
    planes = owners // 4
    region = lax.axis_index("region")
    owner = lax.axis_index("owner")
    core = lax.rem(owner, 2)
    row = lax.rem(owner // 2, 2)
    plane = owner // 4
    bf16, f32 = jnp.bfloat16, jnp.float32

    def place(r, y, c):
        return (2 * y + c) * 2 + r

    def device(r, z, y, c):
        return (r, z * 4 + y * 2 + c)

    me = place(region, row, core)
    mine = region * owners + owner
    peers = [
        (dr, dy, dc) for dr in (0, 1) for dy in (0, 1) for dc in (0, 1) if dr or dy or dc
    ]

    def flip(value, change):
        return 1 - value if change else value

    def moved(change):
        dr, dy, dc = change
        return flip(region, dr), flip(row, dy), flip(core, dc)

    def peer_device(change):
        r, y, c = moved(change)
        return device(r, plane, y, c)

    X, Y, SIB = (1, 0, 0), (0, 1, 0), (0, 0, 1)
    has_up = plane < planes - 1
    has_down = plane > 0
    above = device(region, plane + 1, row, core)
    below = device(region, plane - 1, row, core)

    def run(cond, fn):
        if cond is None:
            fn()
        else:
            pl.when(cond)(fn)

    def both(a, b):
        if a is None:
            return b
        return a if b is None else jnp.logical_and(a, b)

    barrier = pltpu.get_barrier_semaphore()

    def greet(target):
        pl.semaphore_signal(barrier, inc=1, device_id=target, device_id_type=MESH)

    for change in peers:
        greet(peer_device(change))
    run(has_up, lambda: greet(above))
    run(has_down, lambda: greet(below))

    shard_rows = pl.ds(pl.multiple_of(mine * depth, depth), depth)
    for p in range(PLANE):
        for part in range(3):
            at = part * width + p * share
            cut_ref[p, :, part * share:(part + 1) * share] = wq_ref[:, at:at + share]
    w_ref[shard_rows, :] = cut_ref[me]
    go_ref[shard_rows, :] = wo_ref[...]
    own_rows = pl.ds(pl.multiple_of(me * tokens, tokens), tokens)
    blocks_ref[own_rows, :] = layer_norm(x_ref[...], gain_ref[...])
    entries, lanes = own_tab_ref.shape
    entry = lax.broadcasted_iota(jnp.int32, (entries, lanes), 0)
    lane = lax.broadcasted_iota(jnp.int32, (entries, lanes), 1)
    far_region = entry % 2
    far_owner = plane * 4 - 1 + entry // 2
    number = far_region * owners + far_owner
    listed = number == mine
    for k in range(near_ref.shape[1]):
        listed = jnp.logical_or(listed, number == near_ref[0, k])
    inside = jnp.logical_and(far_owner >= 0, far_owner < owners)
    listed = jnp.logical_and(listed, inside)
    marked = jnp.logical_or(lane == me, lane == me + HEAD_DIM)
    own_tab_ref[...] = jnp.where(
        jnp.logical_and(marked, jnp.logical_not(listed)), MASKED, 0.0
    ).astype(bf16)
    tabs_ref[me] = own_tab_ref[...]

    pl.semaphore_wait(
        barrier, len(peers) + has_up.astype(jnp.int32) + has_down.astype(jnp.int32)
    )

    pending = []

    def remote(src, dst, send_sem, recv_sem, target):
        return pltpu.make_async_remote_copy(
            src_ref=src, dst_ref=dst, send_sem=send_sem, recv_sem=recv_sem,
            device_id=target, device_id_type=MESH,
        )

    def start(cond, make):
        run(cond, lambda: make().start())
        pending.append((cond, lambda: make().wait_send()))

    def arrive(cond, make):
        run(cond, lambda: make().wait_recv())

    sib_target = peer_device(SIB)

    for i, change in enumerate(peers):
        to = place(*moved(change))
        start(None, functools.partial(
            remote, cut_ref.at[to], w_ref.at[shard_rows, :], send_w.at[i], recv_w.at[me],
            peer_device(change)))

    def wait_shard(change):
        r, y, c = moved(change)
        source = r * owners + plane * 4 + y * 2 + c
        rows = pl.ds(pl.multiple_of(source * depth, depth), depth)
        arrive(None, functools.partial(
            remote, w_ref.at[rows, :], w_ref.at[rows, :], send_w.at[0],
            recv_w.at[place(r, y, c)], sib_target))

    def send_tables():
        for i, change in enumerate(peers):
            start(None, functools.partial(
                remote, own_tab_ref, tabs_ref.at[me], send_t.at[i], recv_t.at[me],
                peer_device(change)))

    def wait_tables():
        for change in peers:
            p = place(*moved(change))
            arrive(None, functools.partial(
                remote, tabs_ref.at[p], tabs_ref.at[p], send_t.at[0], recv_t.at[p], sib_target))

    class Gather:
        def __init__(self, pieces, view, send, recv):
            self.pieces, self.view, self.recv = pieces, view, recv
            self.send_sems, self.used = send, 0
            self.first = list(range(pieces // 2))
            self.second = list(range(pieces // 2, pieces))

        def send(self, change, piece, source):
            p = place(*moved(source))
            ref = self.view(source, piece)
            sem = self.send_sems.at[self.used]
            self.used += 1
            start(None, functools.partial(
                remote, ref, ref, sem, self.recv.at[p, piece], peer_device(change)))

        def wait(self, source, piece):
            p = place(*moved(source))
            ref = self.view(source, piece)
            arrive(None, functools.partial(
                remote, ref, ref, self.send_sems.at[0], self.recv.at[p, piece], sib_target))

        def own(self, ks):
            for k in ks:
                self.send(X, (self.first + self.second)[k], (0, 0, 0))
                self.send(Y, (self.second + self.first)[k], (0, 0, 0))

        def own_sib(self):
            for piece in range(self.pieces):
                self.send(SIB, piece, (0, 0, 0))

        def direct(self, k):
            a, b = (self.first + self.second)[k], (self.second + self.first)[k]
            onward = k < self.pieces // 2
            self.wait(X, a)
            if onward:
                self.send(Y, a, X)
            self.send(SIB, a, X)
            self.wait(Y, b)
            if onward:
                self.send(X, b, Y)
            self.send(SIB, b, Y)

        def diagonal(self, k):
            for piece in (self.first[k], self.second[k]):
                self.wait((1, 1, 0), piece)
                self.send(SIB, piece, (1, 1, 0))

        def finish(self, sources):
            for source in sources:
                for piece in range(self.pieces):
                    self.wait(source, piece)

    piece_rows = tokens // CHUNKS

    def block_piece(source, piece):
        at = place(*moved(source)) * tokens + piece * piece_rows
        return blocks_ref.at[pl.ds(pl.multiple_of(at, piece_rows), piece_rows), :]

    def out_piece(source, piece):
        r, y, c = moved(source)
        at = (r * owners + piece * 4 + y * 2 + c) * depth
        return go_ref.at[pl.ds(pl.multiple_of(at, depth), depth), :]

    blocks = Gather(CHUNKS, block_piece, send_b, recv_b)
    outs = Gather(planes, out_piece, send_o, recv_o)

    def line(d):
        return [(plane - d, plane - d >= 0), (plane + d, plane + d < planes)]

    def w_half(z, r):
        at = (r * owners + z * 4) * depth
        return w_ref.at[pl.ds(pl.multiple_of(at, 4 * depth), 4 * depth), :]

    def send_w_half(z, r, up, cond):
        ref = w_half(z, r)
        start(both(cond, has_up if up else has_down), functools.partial(
            remote, ref, ref, send_z.at[int(up), z, r], recv_z.at[z, r], above if up else below))

    def wait_w_half(z, r, cond):
        ref = w_half(z, r)
        arrive(cond, functools.partial(
            remote, ref, ref, send_z.at[0, z, r], recv_z.at[z, r], sib_target))

    def own_w():
        for flipped in (0, 1):
            for change in peers:
                if change[0] == flipped:
                    wait_shard(change)
            for up in (True, False):
                send_w_half(plane, flip(region, flipped), up, None)

    def relay_w(d):
        for flipped in (0, 1):
            for (z, cond), up in zip(line(d), (True, False)):
                wait_w_half(z, flip(region, flipped), cond)
                send_w_half(z, flip(region, flipped), up, cond)

    def out_shard(z):
        at = (region * owners + z * 4 + row * 2 + core) * depth
        return go_ref.at[pl.ds(pl.multiple_of(at, depth), depth), :]

    def send_out(z, up, cond):
        ref = out_shard(z)
        start(both(cond, has_up if up else has_down), functools.partial(
            remote, ref, ref, send_oz.at[int(up), z], recv_oz.at[z], above if up else below))

    def own_out():
        for up in (True, False):
            send_out(plane, up, None)

    def relay_out(d):
        for (z, cond), up in zip(line(d), (True, False)):
            ref = out_shard(z)
            arrive(cond, functools.partial(
                remote, ref, ref, send_oz.at[0, z], recv_oz.at[z], sib_target))
            send_out(z, up, cond)

    pair_rows = 2 * tokens
    low = lax.broadcasted_iota(jnp.int32, (tokens, share), 1) < HEAD_DIM
    at_lane = lax.broadcasted_iota(jnp.int32, (tokens, share), 1)
    ones = jnp.ones((tokens, share), bf16)

    def keep_keys(slot, keys, values):
        table = tabs_ref[0].astype(f32)
        for p in range(1, PLANE):
            table = table + tabs_ref[p].astype(f32)
        which = lax.broadcasted_iota(jnp.int32, table.shape, 0)
        for r in (0, 1):
            absent = jnp.sum(
                jnp.where(which == slot * 2 + r, table, 0.0), axis=0, keepdims=True
            )
            absent = jnp.broadcast_to(absent, (tokens, share)).astype(bf16)
            rows = pl.ds(pl.multiple_of(slot * pair_rows + r * tokens, tokens), tokens)
            part = slice(r * tokens, (r + 1) * tokens)
            kl_ref[rows, :] = jnp.where(low, keys[part], absent)
            kh_ref[rows, :] = jnp.where(low, absent, keys[part])
            vl_ref[rows, :] = jnp.where(low, values[part], ones)
            vh_ref[rows, :] = jnp.where(low, ones, values[part])

    def project(j, edge):
        rows = pl.ds(pl.multiple_of(j * pair_rows, pair_rows), pair_rows)
        part = jnp.dot(blocks_ref[rows, :], w_ref[...], preferred_element_type=f32).astype(bf16)
        queries = part[:, 0:share] * bf16(HEAD_DIM ** (-0.5))
        keys, values = part[:, share:2 * share], part[:, 2 * share:]
        if edge is not None:
            edge_out_ref[edge, :, 0:share] = keys
            edge_out_ref[edge, :, share:] = values
        for r in (0, 1):
            q = 2 * j + r
            q_rows = pl.ds(pl.multiple_of(q * tokens, tokens), tokens)
            mark_low = jnp.where(at_lane == q, 1.0, 0.0).astype(bf16)
            mark_high = jnp.where(at_lane == q + HEAD_DIM, 1.0, 0.0).astype(bf16)
            piece = queries[r * tokens:(r + 1) * tokens]
            ql_ref[q_rows, :] = jnp.where(low, piece, mark_high)
            qh_ref[q_rows, :] = jnp.where(low, mark_low, piece)
        keep_keys(j + 1, keys, values)

    def send_edge(e):
        z = plane + 2 * e - 1
        start(jnp.logical_and(z >= 0, z < planes), functools.partial(
            remote, edge_out_ref.at[e], edge_in_ref.at[1 - e], send_e.at[e], recv_e.at[1 - e],
            device(region, z, row, core)))

    def take_edge(e):
        z = plane + 2 * e - 1
        there = jnp.logical_and(z >= 0, z < planes)
        arrive(there, functools.partial(
            remote, edge_in_ref.at[e], edge_in_ref.at[e], send_e.at[e], recv_e.at[e], sib_target))

        @pl.when(jnp.logical_not(there))
        def _():
            edge_in_ref[e] = jnp.zeros(edge_in_ref.shape[1:], bf16)

        keep_keys(e * 5, edge_in_ref[e, :, 0:share], edge_in_ref[e, :, share:])

    def order(i):
        g = i // 2
        late = g // 2
        a = (1 - late) * (2 - g) + late * (9 - 3 * g)
        j = a + row * (3 - 2 * a)
        r = (i % 2) * region + (1 - i % 2) * (1 - region)
        return j, r

    def mixed_copy(i):
        j, r = order(i)
        return remote(
            staged_ref.at[i], mixed_ref.at[me], send_m.at[i], recv_m.at[me],
            device(r, plane, j // 2, j % 2))

    def attend_block(i):
        j, r = order(i)
        q = 2 * j + r
        rows = pl.ds(pl.multiple_of(q * tokens, tokens), tokens)
        keys = pl.ds(pl.multiple_of(j * pair_rows, pair_rows), 3 * pair_rows)
        mixes = []
        for q_ref, k_ref, v_ref in ((ql_ref, kl_ref, vl_ref), (qh_ref, kh_ref, vh_ref)):
            scores = lax.dot_general(
                q_ref[rows, :], k_ref[keys, :], (((1,), (1,)), ((), ())),
                preferred_element_type=f32,
            )
            shifted = jnp.exp(scores - jnp.max(scores, axis=-1, keepdims=True)).astype(bf16)
            mixes.append(jnp.dot(shifted, v_ref[keys, :], preferred_element_type=f32))
        total = jnp.where(low, mixes[1], mixes[0])
        total = pltpu.roll(total, HEAD_DIM, 1)
        out = (jnp.where(low, mixes[0], mixes[1]) / total).astype(bf16)
        staged_ref[i] = out

        @pl.when(q == me)
        def _():
            mixed_ref[me] = out

        @pl.when(q != me)
        def _():
            mixed_copy(i).start()

    blocks.own([0])
    own_w()
    blocks.own(range(1, CHUNKS))
    blocks.own_sib()
    send_tables()
    own_out()
    blocks.direct(0)
    relay_w(1)
    blocks.direct(1)
    relay_w(2)
    blocks.direct(2)
    blocks.direct(3)
    for d in range(3, planes):
        relay_w(d)
    relay_out(1)
    wait_tables()
    blocks.finish([SIB, (1, 0, 1)])
    project(3 * row, row)
    send_edge(row)
    project(1 + row, None)
    blocks.diagonal(0)
    for d in range(2, planes):
        relay_out(d)
    blocks.diagonal(1)
    outs.own(range(planes))
    outs.own_sib()
    blocks.finish([(0, 1, 1), (1, 1, 1)])
    project(3 - 3 * row, 1 - row)
    send_edge(1 - row)
    project(2 - row, None)

    def out_early():
        for k in range(planes // 2):
            outs.direct(k)

    def out_middle():
        for k in range(planes // 2, planes):
            outs.direct(k)

    def out_late():
        for k in range(planes // 2):
            outs.diagonal(k)

    def attend_blocks(first, last):
        def step(i, carry):
            attend_block(i)
            return carry

        lax.fori_loop(first, last, step, 0)

    attend_blocks(0, 3)
    out_early()
    attend_blocks(3, 4)
    take_edge(1 - row)
    attend_blocks(4, 5)
    out_middle()
    attend_blocks(5, 6)
    take_edge(row)
    attend_blocks(6, 7)
    out_late()
    attend_blocks(7, 8)
    outs.finish([SIB, (1, 0, 1), (0, 1, 1), (1, 1, 1)])
    for change in peers:
        p = place(*moved(change))
        arrive(None, functools.partial(
            remote, mixed_ref.at[p], mixed_ref.at[p], send_m.at[0], recv_m.at[p], sib_target))
    mixed = jnp.concatenate([mixed_ref[p] for p in range(PLANE)], axis=1)
    tile = min(512, width)
    for at in range(0, width, tile):
        projected = jnp.dot(mixed, go_ref[:, at:at + tile], preferred_element_type=f32)
        out_ref[:, at:at + tile] = (
            x_ref[:, at:at + tile].astype(f32) + projected
        ).astype(out_ref.dtype)
    for cond, wait in pending:
        run(cond, wait)
    for i in range(PLANE):
        j, r = order(i)
        run(2 * j + r != me, functools.partial(lambda i: mixed_copy(i).wait_send(), i))


def fused(block, qkv_weight, out_weight, norm_gain, near):
    owners = lax.axis_size("owner")
    devices = lax.axis_size("region") * owners
    planes = owners // 4
    tokens, width = block.shape
    depth = qkv_weight.shape[0]
    share = 2 * HEAD_DIM
    bf16 = jnp.bfloat16
    vmem = pl.BlockSpec(memory_space=pltpu.VMEM)
    dma = pltpu.SemaphoreType.DMA
    return pl.pallas_call(
        functools.partial(fused_kernel, owners),
        out_shape=jax.ShapeDtypeStruct(block.shape, block.dtype),
        in_specs=[vmem] * 4 + [pl.BlockSpec(memory_space=pltpu.SMEM)],
        out_specs=vmem,
        scratch_shapes=[
            pltpu.VMEM((PLANE, depth, 3 * share), bf16),
            pltpu.VMEM((devices * depth, 3 * share), bf16),
            pltpu.VMEM((devices * depth, width), bf16),
            pltpu.VMEM((PLANE * tokens, width), bf16),
            pltpu.VMEM((16, share), bf16),
            pltpu.VMEM((PLANE, 16, share), bf16),
        ] + [pltpu.VMEM((PLANE * tokens, share), bf16)] * 2
        + [pltpu.VMEM((12 * tokens, share), bf16)] * 4
        + [pltpu.VMEM((2, 2 * tokens, 2 * share), bf16)] * 2
        + [pltpu.VMEM((PLANE, tokens, share), bf16)] * 2
        + [
            dma((PLANE,)), dma((PLANE,)),
            dma((PLANE,)), dma((PLANE,)),
            dma((2, planes, 2)), dma((planes, 2)),
            dma((2, planes)), dma((planes,)),
            dma((7 * CHUNKS,)), dma((PLANE, CHUNKS)),
            dma((7 * planes,)), dma((PLANE, planes)),
            dma((2,)), dma((2,)),
            dma((PLANE,)), dma((PLANE,)),
        ],
        compiler_params=pltpu.CompilerParams(
            collective_id=0, has_side_effects=True, vmem_limit_bytes=60 * 1024 * 1024
        ),
        name="fused",
    )(block, qkv_weight, out_weight, norm_gain, near)


def attend_kernel(listed_ref, x_ref, xs_ref, gain_ref, bias_ref, wq_ref, wo_ref, out_ref,
                  normed_ref, q_ref, kv_ref, mixed_ref):
    tokens, width = x_ref.shape
    others = xs_ref.shape[0]
    gain = gain_ref[...]
    normed_ref[0:tokens, :] = layer_norm(x_ref[...], gain)

    @pl.loop(0, others)
    def _(slot):
        rows = pl.ds(pl.multiple_of((slot + 1) * tokens, tokens), tokens)
        block = xs_ref[slot].astype(jnp.float32)
        block = jnp.where(listed_ref[slot] > 0, block, 0.0)
        normed_ref[rows, :] = layer_norm(block, gain)

    tile = min(512, width)

    @pl.loop(0, width // tile)
    def _(step):
        cols = pl.ds(pl.multiple_of(step * tile, tile), tile)
        part = jnp.dot(normed_ref[0:tokens, :], wq_ref[:, cols], preferred_element_type=jnp.float32)
        q_ref[:, cols] = part.astype(jnp.bfloat16) * jnp.bfloat16(HEAD_DIM ** (-0.5))

    @pl.loop(0, 2 * width // tile)
    def _(step):
        cols = pl.ds(pl.multiple_of(step * tile, tile), tile)
        from_cols = pl.ds(pl.multiple_of(width + step * tile, tile), tile)
        kv_ref[:, cols] = jnp.dot(
            normed_ref[...], wq_ref[:, from_cols], preferred_element_type=jnp.float32
        ).astype(jnp.bfloat16)

    pair = 2 * HEAD_DIM
    low = lax.broadcasted_iota(jnp.int32, (tokens, pair), 1) < HEAD_DIM
    bias = bias_ref[...]

    @pl.loop(0, width // pair)
    def _(group):
        cols = pl.ds(pl.multiple_of(group * pair, pair), pair)
        value_cols = pl.ds(pl.multiple_of(width + group * pair, pair), pair)
        queries = q_ref[:, cols]
        keys = kv_ref[:, cols]
        values = kv_ref[:, value_cols]
        halves = []
        for mine in (low, jnp.logical_not(low)):
            query = jnp.where(mine, queries, jnp.zeros_like(queries))
            scores = lax.dot_general(
                query, keys, (((1,), (1,)), ((), ())), preferred_element_type=jnp.float32
            ) + bias
            shifted = jnp.exp(scores - jnp.max(scores, axis=-1, keepdims=True))
            total = jnp.sum(shifted, axis=-1, keepdims=True)
            mixed = jnp.dot(shifted.astype(jnp.bfloat16), values, preferred_element_type=jnp.float32)
            halves.append(mixed / total)
        mixed_ref[:, cols] = jnp.where(low, halves[0], halves[1]).astype(jnp.bfloat16)

    @pl.loop(0, width // tile)
    def _(step):
        cols = pl.ds(pl.multiple_of(step * tile, tile), tile)
        projected = jnp.dot(mixed_ref[...], wo_ref[:, cols], preferred_element_type=jnp.float32)
        out_ref[:, cols] = (x_ref[:, cols].astype(jnp.float32) + projected).astype(out_ref.dtype)


def attend(listed, block, others, norm_gain, bias, qkv_weight, out_weight):
    tokens, width = block.shape
    count = (others.shape[0] + 1) * tokens
    vmem = pl.BlockSpec(memory_space=pltpu.VMEM)
    return pl.pallas_call(
        attend_kernel,
        out_shape=jax.ShapeDtypeStruct(block.shape, block.dtype),
        in_specs=[pl.BlockSpec(memory_space=pltpu.SMEM)] + [vmem] * 6,
        out_specs=vmem,
        scratch_shapes=[
            pltpu.VMEM((count, width), jnp.bfloat16),
            pltpu.VMEM((tokens, width), jnp.bfloat16),
            pltpu.VMEM((count, 2 * width), jnp.bfloat16),
            pltpu.VMEM((tokens, width), jnp.bfloat16),
        ],
        compiler_params=pltpu.CompilerParams(vmem_limit_bytes=60 * 1024 * 1024),
        name="attend",
    )(listed, block, others, norm_gain, bias, qkv_weight, out_weight)


def shards(voxels, norm_gain, qkv_weight, out_weight, neighbours):
    block_size, model_width = voxels.shape[-2:]
    block = voxels.reshape(block_size, model_width)
    regions, owners = (lax.axis_size("region"), lax.axis_size("owner"))
    region, owner = (lax.axis_index("region"), lax.axis_index("owner"))
    share = 2 * HEAD_DIM
    together = regions == 2 and owners % 8 == 0 and model_width == PLANE * share
    together = together and block_size % (16 * CHUNKS) == 0 and voxels.shape[2] == 1
    if together:
        out = fused(block, qkv_weight, out_weight, norm_gain[None, :], neighbours.reshape(1, -1))
        return out.reshape(voxels.shape)
    wide = padded(voxels[:, :, 0], (("owner", 1), ("region", 0)), 1)
    wide = wide.reshape(-1, block_size, model_width)
    middle = wide.shape[0] // 2
    others = jnp.concatenate([wide[:middle], wide[middle + 1:]], axis=0)
    full_qkv = lax.all_gather(qkv_weight, ("region", "owner"), axis=0, tiled=True)
    full_out = lax.all_gather(out_weight, ("region", "owner"), axis=0, tiled=True)
    offsets = [(i, j) for i in (-1, 0, 1) for j in (-1, 0, 1) if i or j]
    numbers = []
    for up, along in offsets:
        inside = (owner + along >= 0) & (owner + along < owners)
        number = (region + up) * owners + owner + along
        numbers.append(jnp.where(inside & (number >= 0), number, -2))
    listed = jnp.any(neighbours.reshape(1, -1) == jnp.stack(numbers)[:, None], axis=1)
    present = jnp.concatenate([jnp.ones((1,), bool), listed])
    bias = jnp.repeat(jnp.where(present, 0.0, MASKED).astype(jnp.float32), block_size)[None, :]
    out = attend(
        listed.astype(jnp.int32), block, others, norm_gain[None, :], bias, full_qkv, full_out
    )
    return out.reshape(voxels.shape)


def solution(mesh):
    return jax.shard_map(
        shards,
        mesh=mesh,
        in_specs=(
            P("region", "owner", None, None, None),
            P(),
            P(("region", "owner"), None),
            P(("region", "owner"), None),
            P("region", "owner", None, None),
        ),
        out_specs=P("region", "owner", None, None, None),
        check_vma=False,
    )
```

```python
import functools

import jax
import jax.numpy as jnp
from jax import lax
from jax.experimental import pallas as pl
from jax.experimental.pallas import tpu as pltpu
from jax.sharding import PartitionSpec as P

HEAD_DIM = 64
MESH = pl.DeviceIdType.MESH
PLANE = 8
CHUNKS = 4
MASKED = -1e30


def padded(value, sides, width):
    for axis, dim in sides:
        devices, length = (lax.axis_size(axis), value.shape[dim])
        up = [(i, (i + 1) % devices) for i in range(devices - 1)]
        down = [(j, i) for i, j in up]
        last = lax.slice_in_dim(value, length - width, length, axis=dim)
        first = lax.slice_in_dim(value, 0, width, axis=dim)
        before = lax.ppermute(last, axis, up)
        after = lax.ppermute(first, axis, down)
        value = jnp.concatenate([before, value, after], axis=dim)
    return value


def layer_norm(inputs, norm_gain):
    widened = inputs.astype(jnp.float32)
    average = jnp.mean(widened, axis=-1, keepdims=True)
    spread = jnp.mean((widened - average) ** 2, axis=-1, keepdims=True)
    return ((widened - average) * lax.rsqrt(spread + 1e-06) * norm_gain).astype(jnp.bfloat16)


def fused_kernel(owners, x_hbm, wq_hbm, wo_hbm, gain_ref, near_ref, out_ref,
                 x_ref, wq_ref, cut_ref, w_ref, go_ref, blocks_ref, own_tab_ref, tabs_ref,
                 ql_ref, qh_ref, kl_ref, kh_ref, vl_ref, vh_ref,
                 edge_out_ref, edge_in_ref, staged_ref, mixed_ref,
                 send_w, recv_w, send_t, recv_t, send_z, recv_z, send_l, send_b, recv_b,
                 send_o, recv_o, send_e, recv_e, send_m, recv_m, local_sem):
    tokens, width = x_ref.shape
    depth = wo_hbm.shape[0]
    share = 2 * HEAD_DIM
    planes = owners // 4
    region = lax.axis_index("region")
    owner = lax.axis_index("owner")
    core = lax.rem(owner, 2)
    row = lax.rem(owner // 2, 2)
    plane = owner // 4
    bf16, f32 = jnp.bfloat16, jnp.float32

    def place(r, y, c):
        return (2 * y + c) * 2 + r

    def device(r, z, y, c):
        return (r, z * 4 + y * 2 + c)

    me = place(region, row, core)
    mine = region * owners + owner
    peers = [
        (dr, dy, dc) for dr in (1, 0) for dy in (1, 0) for dc in (1, 0) if dr or dy or dc
    ]

    def flip(value, change):
        return 1 - value if change else value

    def moved(change):
        dr, dy, dc = change
        return flip(region, dr), flip(row, dy), flip(core, dc)

    def peer_device(change):
        r, y, c = moved(change)
        return device(r, plane, y, c)

    X, Y, SIB = (1, 0, 0), (0, 1, 0), (0, 0, 1)
    has_up = plane < planes - 1
    has_down = plane > 0
    above = device(region, plane + 1, row, core)
    below = device(region, plane - 1, row, core)

    def run(cond, fn):
        if cond is None:
            fn()
        else:
            pl.when(cond)(fn)

    def both(a, b):
        if a is None:
            return b
        return a if b is None else jnp.logical_and(a, b)

    shard_rows = pl.ds(pl.multiple_of(mine * depth, depth), depth)
    local = [
        pltpu.make_async_copy(wq_hbm, wq_ref, local_sem.at[0]),
        pltpu.make_async_copy(x_hbm, x_ref, local_sem.at[1]),
        pltpu.make_async_copy(wo_hbm, go_ref.at[shard_rows, :], local_sem.at[2]),
    ]
    for copy in local:
        copy.start()
    barrier = pltpu.get_barrier_semaphore()

    def greet(target):
        pl.semaphore_signal(barrier, inc=1, device_id=target, device_id_type=MESH)

    for change in peers:
        greet(peer_device(change))
    run(has_up, lambda: greet(above))
    run(has_down, lambda: greet(below))

    local[0].wait()
    for p in range(PLANE):
        for part in range(3):
            at = part * width + p * share
            cut_ref[p, :, part * share:(part + 1) * share] = wq_ref[:, at:at + share]
    w_ref[shard_rows, :] = cut_ref[me]
    local[1].wait()
    own_rows = pl.ds(pl.multiple_of(me * tokens, tokens), tokens)
    blocks_ref[own_rows, :] = layer_norm(x_ref[...], gain_ref[...])
    entries, lanes = own_tab_ref.shape
    entry = lax.broadcasted_iota(jnp.int32, (entries, lanes), 0)
    lane = lax.broadcasted_iota(jnp.int32, (entries, lanes), 1)
    far_region = entry % 2
    far_owner = plane * 4 - 1 + entry // 2
    number = far_region * owners + far_owner
    listed = number == mine
    for k in range(near_ref.shape[1]):
        listed = jnp.logical_or(listed, number == near_ref[0, k])
    inside = jnp.logical_and(far_owner >= 0, far_owner < owners)
    listed = jnp.logical_and(listed, inside)
    marked = jnp.logical_or(lane == me, lane == me + HEAD_DIM)
    own_tab_ref[...] = jnp.where(
        jnp.logical_and(marked, jnp.logical_not(listed)), MASKED, 0.0
    ).astype(bf16)
    tabs_ref[me] = own_tab_ref[...]
    local[2].wait()

    pl.semaphore_wait(
        barrier, len(peers) + has_up.astype(jnp.int32) + has_down.astype(jnp.int32)
    )

    pending = []
    sib_target = peer_device(SIB)

    def remote(src, dst, send_sem, recv_sem, target):
        return pltpu.make_async_remote_copy(
            src_ref=src, dst_ref=dst, send_sem=send_sem, recv_sem=recv_sem,
            device_id=target, device_id_type=MESH,
        )

    def start(cond, make):
        run(cond, lambda: make().start())

    def sent(ref, sem, cond=None):
        pending.append((cond, lambda: remote(ref, ref, sem, sem, sib_target).wait_send()))

    def arrive(cond, make):
        run(cond, lambda: make().wait_recv())

    for change in peers:
        to = place(*moved(change))
        start(None, functools.partial(
            remote, cut_ref.at[to], w_ref.at[shard_rows, :], send_w, recv_w.at[change[0]],
            peer_device(change)))
    sent(cut_ref.at[0:PLANE - 1], send_w)

    def wait_shards(flipped):
        count = sum(change[0] == flipped for change in peers)
        ref = cut_ref.at[0:count]
        arrive(None, functools.partial(
            remote, ref, ref, send_w, recv_w.at[flipped], sib_target))

    for change in peers:
        start(None, functools.partial(
            remote, own_tab_ref, tabs_ref.at[me], send_t, recv_t, peer_device(change)))
    sent(tabs_ref.at[0:PLANE - 1], send_t)

    def wait_tables():
        ref = tabs_ref.at[0:PLANE - 1]
        arrive(None, functools.partial(remote, ref, ref, send_t, recv_t, sib_target))

    OWN, DIAGONAL = (0, 0, 0), (1, 1, 0)
    LINE, BY_X, BY_Y, BY_BOTH, BY_SIB = range(5)

    def slot(sems, source, to, piece):
        way = tuple(int(a != b) for a, b in zip(source, to))
        if way[2]:
            return sems.at[BY_SIB, way[0] + 2 * way[1]]
        return sems.at[way[0] + 2 * way[1], piece]

    def lane_of(to, source):
        if to != SIB:
            return 0 if to == X else 1
        return 2 if source in (OWN, X) else 3

    class Gather:
        def __init__(self, pieces, view, send, recv):
            self.pieces, self.view, self.send_sem, self.recv = pieces, view, send, recv
            self.first = list(range(pieces // 2))
            self.second = list(range(pieces // 2, pieces))

        def send(self, change, piece, source):
            ref = self.view(source, piece)
            start(None, functools.partial(
                remote, ref, ref, self.send_sem.at[lane_of(change, source)],
                slot(self.recv, source, change, piece), peer_device(change)))

        def wait(self, source, piece):
            ref = self.view(source, piece)
            arrive(None, functools.partial(
                remote, ref, ref, self.send_sem.at[0], slot(self.recv, source, OWN, piece),
                sib_target))

        def own(self, ks):
            for k in ks:
                self.send(X, (self.first + self.second)[k], (0, 0, 0))
                self.send(Y, (self.second + self.first)[k], (0, 0, 0))

        def own_sib(self):
            for piece in range(self.pieces):
                self.send(SIB, piece, (0, 0, 0))

        def direct(self, k):
            a, b = (self.first + self.second)[k], (self.second + self.first)[k]
            onward = k < self.pieces // 2
            self.wait(X, a)
            if onward:
                self.send(Y, a, X)
            self.send(SIB, a, X)
            self.wait(Y, b)
            if onward:
                self.send(X, b, Y)
            self.send(SIB, b, Y)

        def diagonal(self, k):
            for piece in (self.first[k], self.second[k]):
                self.wait((1, 1, 0), piece)
                self.send(SIB, piece, (1, 1, 0))

        def finish(self, sources):
            for source in sources:
                at = pl.multiple_of(place(*moved(source)) * tokens, tokens)
                ref = blocks_ref.at[pl.ds(at, tokens), :]
                arrive(None, functools.partial(
                    remote, ref, ref, self.send_sem.at[0], slot(self.recv, source, OWN, None),
                    sib_target))

    piece_rows = tokens // CHUNKS

    def block_piece(source, piece):
        at = place(*moved(source)) * tokens + piece * piece_rows
        return blocks_ref.at[pl.ds(pl.multiple_of(at, piece_rows), piece_rows), :]

    blocks = Gather(CHUNKS, block_piece, send_b, recv_b)
    for way, count in ((0, 3), (1, 3), (2, 4), (3, 4)):
        sent(blocks_ref.at[0:count * tokens // 2, :], send_b.at[way])

    def line(d):
        return [(plane - d, plane - d >= 0), (plane + d, plane + d < planes)]

    def w_half(z, r):
        at = (r * owners + z * 4) * depth
        return w_ref.at[pl.ds(pl.multiple_of(at, 4 * depth), 4 * depth), :]

    def send_w_half(z, r, up, cond, d):
        ref = w_half(z, r)
        start(both(cond, has_up if up else has_down), functools.partial(
            remote, ref, ref, send_z.at[int(up), d], recv_z.at[z, r], above if up else below))

    def wait_w_half(z, r, cond):
        ref = w_half(z, r)
        arrive(cond, functools.partial(
            remote, ref, ref, send_z.at[0, 0], recv_z.at[z, r], sib_target))

    for d in range(planes - 1):
        for up, cond in ((1, plane - d >= 0), (0, plane + d < planes)):
            cond = jnp.logical_and(cond, has_up if up else has_down)
            sent(w_ref.at[0:8 * depth, :], send_z.at[up, d], cond)
            sent(go_ref.at[0:depth, :], send_l.at[up, d], cond)

    def own_w():
        for flipped in (0, 1):
            wait_shards(flipped)
            for up in (True, False):
                send_w_half(plane, flip(region, flipped), up, None, 0)

    def relay_w(d):
        for flipped in (0, 1):
            for (z, cond), up in zip(line(d), (True, False)):
                wait_w_half(z, flip(region, flipped), cond)
                if d < planes - 1:
                    send_w_half(z, flip(region, flipped), up, cond, d)

    def out_rows(source, z, half=None):
        r, y, c = moved(source)
        at = (r * owners + z * 4 + y * 2 + c) * depth
        if half is None:
            return go_ref.at[pl.ds(pl.multiple_of(at, depth), depth), :]
        at = at + half * (depth // 2)
        return go_ref.at[pl.ds(pl.multiple_of(at, depth // 2), depth // 2), :]

    def send_out(source, z, to, cond, half=None):
        ref = out_rows(source, z, half)
        start(cond, functools.partial(
            remote, ref, ref, send_o.at[lane_of(to, source)], slot(recv_o, source, to, z),
            peer_device(to)))

    def wait_out(source, z, cond):
        ref = out_rows(source, z)
        arrive(cond, functools.partial(
            remote, ref, ref, send_o.at[0], slot(recv_o, source, OWN, z), sib_target))

    for way, count in ((0, 3), (1, 3), (2, 4), (3, 4)):
        sent(go_ref.at[0:count * planes * depth // 2, :], send_o.at[way])

    def line_out(z, up, cond, d):
        ref = out_rows(OWN, z)
        start(both(cond, has_up if up else has_down), functools.partial(
            remote, ref, ref, send_l.at[int(up), d], recv_o.at[LINE, z], above if up else below))

    def own_out():
        for up in (True, False):
            line_out(plane, up, None, 0)

    def relay_out(d):
        for (z, cond), up in zip(line(d), (True, False)):
            wait_out(OWN, z, cond)
            if d < planes - 1:
                line_out(z, up, cond, d)

    def ring(d):
        return [(plane, None)] if d == 0 else line(d)

    def spread_out(d):
        for z, cond in ring(d):
            send_out(OWN, z, X, cond)
            send_out(OWN, z, Y, cond)

    def spread_out_sib(d):
        for z, cond in ring(d):
            send_out(OWN, z, SIB, cond)

    def onward_out(d):
        for z, cond in ring(d):
            wait_out(X, z, cond)
            send_out(X, z, Y, cond, 0)
            send_out(X, z, SIB, cond)
            wait_out(Y, z, cond)
            send_out(Y, z, X, cond, 1)
            send_out(Y, z, SIB, cond)

    def diagonal_out(d):
        for z, cond in ring(d):
            wait_out(DIAGONAL, z, cond)
            send_out(DIAGONAL, z, SIB, cond)

    def finish_out():
        ref = go_ref.at[0:planes * depth, :]
        for source in (SIB, (1, 0, 1), (0, 1, 1), (1, 1, 1)):
            arrive(None, functools.partial(
                remote, ref, ref, send_o.at[0], slot(recv_o, source, OWN, None), sib_target))

    pair_rows = 2 * tokens
    low = lax.broadcasted_iota(jnp.int32, (tokens, share), 1) < HEAD_DIM
    at_lane = lax.broadcasted_iota(jnp.int32, (tokens, share), 1)
    ones = jnp.ones((tokens, share), bf16)

    def keep_keys(slot, keys, values):
        table = tabs_ref[0].astype(f32)
        for p in range(1, PLANE):
            table = table + tabs_ref[p].astype(f32)
        which = lax.broadcasted_iota(jnp.int32, table.shape, 0)
        for r in (0, 1):
            absent = jnp.sum(
                jnp.where(which == slot * 2 + r, table, 0.0), axis=0, keepdims=True
            )
            absent = jnp.broadcast_to(absent, (tokens, share)).astype(bf16)
            rows = pl.ds(pl.multiple_of(slot * pair_rows + r * tokens, tokens), tokens)
            part = slice(r * tokens, (r + 1) * tokens)
            kl_ref[rows, :] = jnp.where(low, keys[part], absent)
            kh_ref[rows, :] = jnp.where(low, absent, keys[part])
            vl_ref[rows, :] = jnp.where(low, values[part], ones)
            vh_ref[rows, :] = jnp.where(low, ones, values[part])

    def project(j, edge):
        rows = pl.ds(pl.multiple_of(j * pair_rows, pair_rows), pair_rows)
        part = jnp.dot(blocks_ref[rows, :], w_ref[...], preferred_element_type=f32).astype(bf16)
        queries = part[:, 0:share] * bf16(HEAD_DIM ** (-0.5))
        keys, values = part[:, share:2 * share], part[:, 2 * share:]
        if edge is not None:
            edge_out_ref[edge, :, 0:share] = keys
            edge_out_ref[edge, :, share:] = values
        for r in (0, 1):
            q = 2 * j + r
            q_rows = pl.ds(pl.multiple_of(q * tokens, tokens), tokens)
            mark_low = jnp.where(at_lane == q, 1.0, 0.0).astype(bf16)
            mark_high = jnp.where(at_lane == q + HEAD_DIM, 1.0, 0.0).astype(bf16)
            piece = queries[r * tokens:(r + 1) * tokens]
            ql_ref[q_rows, :] = jnp.where(low, piece, mark_high)
            qh_ref[q_rows, :] = jnp.where(low, mark_low, piece)
        keep_keys(j + 1, keys, values)

    def send_edge(e):
        z = plane + 2 * e - 1
        there = jnp.logical_and(z >= 0, z < planes)
        sent(edge_out_ref.at[e], send_e.at[e], there)
        start(there, functools.partial(
            remote, edge_out_ref.at[e], edge_in_ref.at[1 - e], send_e.at[e], recv_e.at[1 - e],
            device(region, z, row, core)))

    def take_edge(e):
        z = plane + 2 * e - 1
        there = jnp.logical_and(z >= 0, z < planes)
        arrive(there, functools.partial(
            remote, edge_in_ref.at[e], edge_in_ref.at[e], send_e.at[e], recv_e.at[e], sib_target))

        @pl.when(jnp.logical_not(there))
        def _():
            edge_in_ref[e] = jnp.zeros(edge_in_ref.shape[1:], bf16)

        keep_keys(e * 5, edge_in_ref[e, :, 0:share], edge_in_ref[e, :, share:])

    def order(i):
        g = i // 2
        late = g // 2
        a = (1 - late) * (2 - g) + late * (9 - 3 * g)
        j = a + row * (3 - 2 * a)
        r = (i % 2) * region + (1 - i % 2) * (1 - region)
        return j, r

    def mixed_copy(i):
        j, r = order(i)
        return remote(
            staged_ref.at[i], mixed_ref.at[me], send_m, recv_m,
            device(r, plane, j // 2, j % 2))

    def attend_block(i):
        j, r = order(i)
        q = 2 * j + r
        rows = pl.ds(pl.multiple_of(q * tokens, tokens), tokens)
        keys = pl.ds(pl.multiple_of(j * pair_rows, pair_rows), 3 * pair_rows)
        mixes = []
        for q_ref, k_ref, v_ref in ((ql_ref, kl_ref, vl_ref), (qh_ref, kh_ref, vh_ref)):
            scores = lax.dot_general(
                q_ref[rows, :], k_ref[keys, :], (((1,), (1,)), ((), ())),
                preferred_element_type=f32,
            )
            shifted = jnp.exp(scores - jnp.max(scores, axis=-1, keepdims=True)).astype(bf16)
            mixes.append(jnp.dot(shifted, v_ref[keys, :], preferred_element_type=f32))
        total = jnp.where(low, mixes[1], mixes[0])
        total = pltpu.roll(total, HEAD_DIM, 1)
        out = (jnp.where(low, mixes[0], mixes[1]) / total).astype(bf16)
        staged_ref[i] = out

        @pl.when(q == me)
        def _():
            mixed_ref[me] = out

        @pl.when(q != me)
        def _():
            mixed_copy(i).start()

    blocks.own(range(CHUNKS))
    blocks.own_sib()
    own_w()
    own_out()
    blocks.direct(0)
    relay_w(1)
    relay_out(1)
    blocks.direct(1)
    spread_out(0)
    spread_out(1)
    relay_w(2)
    relay_out(2)
    spread_out(2)
    blocks.direct(2)
    blocks.direct(3)
    relay_w(planes - 1)
    wait_tables()
    blocks.finish([SIB, (1, 0, 1)])
    project(3 * row, row)
    send_edge(row)
    project(1 + row, None)
    blocks.diagonal(0)
    blocks.diagonal(1)
    blocks.finish([(0, 1, 1), (1, 1, 1)])
    project(3 - 3 * row, 1 - row)
    send_edge(1 - row)
    relay_out(planes - 1)
    spread_out(planes - 1)
    project(2 - row, None)

    def attend_blocks(first, last):
        def step(i, carry):
            attend_block(i)
            return carry

        lax.fori_loop(first, last, step, 0)

    for d in range(planes):
        spread_out_sib(d)
    attend_blocks(0, 2)
    onward_out(0)
    onward_out(1)
    attend_blocks(2, 4)
    onward_out(2)
    take_edge(1 - row)
    attend_blocks(4, 5)
    onward_out(3)
    attend_blocks(5, 6)
    take_edge(row)
    attend_blocks(6, 7)
    diagonal_out(0)
    diagonal_out(1)
    attend_blocks(7, 8)
    diagonal_out(2)
    diagonal_out(3)
    finish_out()
    pieces = staged_ref.at[0:PLANE - 1]
    arrive(None, functools.partial(remote, pieces, pieces, send_m, recv_m, sib_target))
    sent(pieces, send_m)
    mixed = jnp.concatenate([mixed_ref[p] for p in range(PLANE)], axis=1)
    tile = min(512, width)
    for at in range(0, width, tile):
        projected = jnp.dot(mixed, go_ref[:, at:at + tile], preferred_element_type=f32)
        out_ref[:, at:at + tile] = (
            x_ref[:, at:at + tile].astype(f32) + projected
        ).astype(out_ref.dtype)
    for cond, wait in pending:
        run(cond, wait)


def fused(block, qkv_weight, out_weight, norm_gain, near):
    owners = lax.axis_size("owner")
    devices = lax.axis_size("region") * owners
    planes = owners // 4
    tokens, width = block.shape
    depth = qkv_weight.shape[0]
    share = 2 * HEAD_DIM
    bf16 = jnp.bfloat16
    vmem = pl.BlockSpec(memory_space=pltpu.VMEM)
    dma = pltpu.SemaphoreType.DMA
    return pl.pallas_call(
        functools.partial(fused_kernel, owners),
        out_shape=jax.ShapeDtypeStruct(block.shape, block.dtype),
        in_specs=[pl.BlockSpec(memory_space=pl.ANY)] * 3 + [vmem] + [pl.BlockSpec(memory_space=pltpu.SMEM)],
        out_specs=vmem,
        scratch_shapes=[
            pltpu.VMEM(block.shape, bf16),
            pltpu.VMEM(qkv_weight.shape, bf16),
            pltpu.VMEM((PLANE, depth, 3 * share), bf16),
            pltpu.VMEM((devices * depth, 3 * share), bf16),
            pltpu.VMEM((devices * depth, width), bf16),
            pltpu.VMEM((PLANE * tokens, width), bf16),
            pltpu.VMEM((16, share), bf16),
            pltpu.VMEM((PLANE, 16, share), bf16),
        ] + [pltpu.VMEM((PLANE * tokens, share), bf16)] * 2
        + [pltpu.VMEM((12 * tokens, share), bf16)] * 4
        + [pltpu.VMEM((2, 2 * tokens, 2 * share), bf16)] * 2
        + [pltpu.VMEM((PLANE, tokens, share), bf16)] * 2
        + [
            dma, dma((2,)), dma, dma,
            dma((2, planes - 1)), dma((planes, 2)), dma((2, planes - 1)),
            dma((4,)), dma((5, CHUNKS)), dma((4,)), dma((5, max(planes, 4))),
            dma((2,)), dma((2,)), dma, dma, dma((3,)),
        ],
        compiler_params=pltpu.CompilerParams(
            collective_id=0, has_side_effects=True, vmem_limit_bytes=60 * 1024 * 1024
        ),
        name="fused",
    )(block, qkv_weight, out_weight, norm_gain, near)


def attend_kernel(listed_ref, x_ref, xs_ref, gain_ref, bias_ref, wq_ref, wo_ref, out_ref,
                  normed_ref, q_ref, kv_ref, mixed_ref):
    tokens, width = x_ref.shape
    others = xs_ref.shape[0]
    gain = gain_ref[...]
    normed_ref[0:tokens, :] = layer_norm(x_ref[...], gain)

    @pl.loop(0, others)
    def _(slot):
        rows = pl.ds(pl.multiple_of((slot + 1) * tokens, tokens), tokens)
        block = xs_ref[slot].astype(jnp.float32)
        block = jnp.where(listed_ref[slot] > 0, block, 0.0)
        normed_ref[rows, :] = layer_norm(block, gain)

    tile = min(512, width)

    @pl.loop(0, width // tile)
    def _(step):
        cols = pl.ds(pl.multiple_of(step * tile, tile), tile)
        part = jnp.dot(normed_ref[0:tokens, :], wq_ref[:, cols], preferred_element_type=jnp.float32)
        q_ref[:, cols] = part.astype(jnp.bfloat16) * jnp.bfloat16(HEAD_DIM ** (-0.5))

    @pl.loop(0, 2 * width // tile)
    def _(step):
        cols = pl.ds(pl.multiple_of(step * tile, tile), tile)
        from_cols = pl.ds(pl.multiple_of(width + step * tile, tile), tile)
        kv_ref[:, cols] = jnp.dot(
            normed_ref[...], wq_ref[:, from_cols], preferred_element_type=jnp.float32
        ).astype(jnp.bfloat16)

    pair = 2 * HEAD_DIM
    low = lax.broadcasted_iota(jnp.int32, (tokens, pair), 1) < HEAD_DIM
    bias = bias_ref[...]

    @pl.loop(0, width // pair)
    def _(group):
        cols = pl.ds(pl.multiple_of(group * pair, pair), pair)
        value_cols = pl.ds(pl.multiple_of(width + group * pair, pair), pair)
        queries = q_ref[:, cols]
        keys = kv_ref[:, cols]
        values = kv_ref[:, value_cols]
        halves = []
        for mine in (low, jnp.logical_not(low)):
            query = jnp.where(mine, queries, jnp.zeros_like(queries))
            scores = lax.dot_general(
                query, keys, (((1,), (1,)), ((), ())), preferred_element_type=jnp.float32
            ) + bias
            shifted = jnp.exp(scores - jnp.max(scores, axis=-1, keepdims=True))
            total = jnp.sum(shifted, axis=-1, keepdims=True)
            mixed = jnp.dot(shifted.astype(jnp.bfloat16), values, preferred_element_type=jnp.float32)
            halves.append(mixed / total)
        mixed_ref[:, cols] = jnp.where(low, halves[0], halves[1]).astype(jnp.bfloat16)

    @pl.loop(0, width // tile)
    def _(step):
        cols = pl.ds(pl.multiple_of(step * tile, tile), tile)
        projected = jnp.dot(mixed_ref[...], wo_ref[:, cols], preferred_element_type=jnp.float32)
        out_ref[:, cols] = (x_ref[:, cols].astype(jnp.float32) + projected).astype(out_ref.dtype)


def attend(listed, block, others, norm_gain, bias, qkv_weight, out_weight):
    tokens, width = block.shape
    count = (others.shape[0] + 1) * tokens
    vmem = pl.BlockSpec(memory_space=pltpu.VMEM)
    return pl.pallas_call(
        attend_kernel,
        out_shape=jax.ShapeDtypeStruct(block.shape, block.dtype),
        in_specs=[pl.BlockSpec(memory_space=pltpu.SMEM)] + [vmem] * 6,
        out_specs=vmem,
        scratch_shapes=[
            pltpu.VMEM((count, width), jnp.bfloat16),
            pltpu.VMEM((tokens, width), jnp.bfloat16),
            pltpu.VMEM((count, 2 * width), jnp.bfloat16),
            pltpu.VMEM((tokens, width), jnp.bfloat16),
        ],
        compiler_params=pltpu.CompilerParams(vmem_limit_bytes=60 * 1024 * 1024),
        name="attend",
    )(listed, block, others, norm_gain, bias, qkv_weight, out_weight)


def shards(voxels, norm_gain, qkv_weight, out_weight, neighbours):
    block_size, model_width = voxels.shape[-2:]
    block = voxels.reshape(block_size, model_width)
    regions, owners = (lax.axis_size("region"), lax.axis_size("owner"))
    region, owner = (lax.axis_index("region"), lax.axis_index("owner"))
    share = 2 * HEAD_DIM
    together = regions == 2 and owners % 8 == 0 and model_width == PLANE * share
    together = together and block_size % (16 * CHUNKS) == 0 and voxels.shape[2] == 1
    if together:
        out = fused(block, qkv_weight, out_weight, norm_gain[None, :], neighbours.reshape(1, -1))
        return out.reshape(voxels.shape)
    wide = padded(voxels[:, :, 0], (("owner", 1), ("region", 0)), 1)
    wide = wide.reshape(-1, block_size, model_width)
    middle = wide.shape[0] // 2
    others = jnp.concatenate([wide[:middle], wide[middle + 1:]], axis=0)
    full_qkv = lax.all_gather(qkv_weight, ("region", "owner"), axis=0, tiled=True)
    full_out = lax.all_gather(out_weight, ("region", "owner"), axis=0, tiled=True)
    offsets = [(i, j) for i in (-1, 0, 1) for j in (-1, 0, 1) if i or j]
    numbers = []
    for up, along in offsets:
        inside = (owner + along >= 0) & (owner + along < owners)
        number = (region + up) * owners + owner + along
        numbers.append(jnp.where(inside & (number >= 0), number, -2))
    listed = jnp.any(neighbours.reshape(1, -1) == jnp.stack(numbers)[:, None], axis=1)
    present = jnp.concatenate([jnp.ones((1,), bool), listed])
    bias = jnp.repeat(jnp.where(present, 0.0, MASKED).astype(jnp.float32), block_size)[None, :]
    out = attend(
        listed.astype(jnp.int32), block, others, norm_gain[None, :], bias, full_qkv, full_out
    )
    return out.reshape(voxels.shape)


def solution(mesh):
    return jax.shard_map(
        shards,
        mesh=mesh,
        in_specs=(
            P("region", "owner", None, None, None),
            P(),
            P(("region", "owner"), None),
            P(("region", "owner"), None),
            P("region", "owner", None, None),
        ),
        out_specs=P("region", "owner", None, None, None),
        check_vma=False,
    )
```

```python
import functools

import jax
import jax.numpy as jnp
from jax import lax
from jax.experimental import pallas as pl
from jax.experimental.pallas import tpu as pltpu
from jax.sharding import PartitionSpec as P

HEAD_DIM = 64
MESH = pl.DeviceIdType.MESH
PLANE = 8
CHUNKS = 4
MASKED = -1e30


def padded(value, sides, width):
    for axis, dim in sides:
        devices, length = (lax.axis_size(axis), value.shape[dim])
        up = [(i, (i + 1) % devices) for i in range(devices - 1)]
        down = [(j, i) for i, j in up]
        last = lax.slice_in_dim(value, length - width, length, axis=dim)
        first = lax.slice_in_dim(value, 0, width, axis=dim)
        before = lax.ppermute(last, axis, up)
        after = lax.ppermute(first, axis, down)
        value = jnp.concatenate([before, value, after], axis=dim)
    return value


def layer_norm(inputs, norm_gain):
    widened = inputs.astype(jnp.float32)
    average = jnp.mean(widened, axis=-1, keepdims=True)
    spread = jnp.mean((widened - average) ** 2, axis=-1, keepdims=True)
    return ((widened - average) * lax.rsqrt(spread + 1e-06) * norm_gain).astype(jnp.bfloat16)


def fused_kernel(owners, x_hbm, wq_hbm, wo_hbm, gain_ref, near_ref, out_ref,
                 x_ref, wq_ref, cut_ref, w_ref, go_ref, blocks_ref, own_tab_ref, tabs_ref,
                 ql_ref, qh_ref, kl_ref, kh_ref, vl_ref, vh_ref,
                 edge_out_ref, edge_in_ref, staged_ref, mixed_ref,
                 send_w, recv_w, send_t, recv_t, send_z, recv_z, recv_l, send_b, recv_b,
                 send_o, recv_o, recv_s, send_e, recv_e, send_m, recv_m, local_sem):
    tokens, width = x_ref.shape
    depth = wo_hbm.shape[0]
    share = 2 * HEAD_DIM
    planes = owners // 4
    region = lax.axis_index("region")
    owner = lax.axis_index("owner")
    core = lax.rem(owner, 2)
    row = lax.rem(owner // 2, 2)
    plane = owner // 4
    bf16, f32 = jnp.bfloat16, jnp.float32

    def place(r, y, c):
        return (2 * y + c) * 2 + r

    def device(r, z, y, c):
        return (r, z * 4 + y * 2 + c)

    me = place(region, row, core)
    mine = region * owners + owner
    peers = [
        (dr, dy, dc) for dr in (1, 0) for dy in (1, 0) for dc in (1, 0) if dr or dy or dc
    ]

    def flip(value, change):
        return 1 - value if change else value

    def moved(change):
        dr, dy, dc = change
        return flip(region, dr), flip(row, dy), flip(core, dc)

    def peer_device(change):
        r, y, c = moved(change)
        return device(r, plane, y, c)

    X, Y, SIB = (1, 0, 0), (0, 1, 0), (0, 0, 1)
    has_up = plane < planes - 1
    has_down = plane > 0
    above = device(region, plane + 1, row, core)
    below = device(region, plane - 1, row, core)

    def run(cond, fn):
        if cond is None:
            fn()
        else:
            pl.when(cond)(fn)

    def both(a, b):
        if a is None:
            return b
        return a if b is None else jnp.logical_and(a, b)

    shard_rows = pl.ds(pl.multiple_of(mine * depth, depth), depth)
    local = [
        pltpu.make_async_copy(wq_hbm, wq_ref, local_sem.at[0]),
        pltpu.make_async_copy(x_hbm, x_ref, local_sem.at[1]),
        pltpu.make_async_copy(
            wo_hbm,
            go_ref.at[region * planes + plane, pl.ds(
                pl.multiple_of((2 * row + core) * depth, depth), depth), :],
            local_sem.at[2],
        ),
    ]
    for copy in local:
        copy.start()
    barrier = pltpu.get_barrier_semaphore()

    def greet(target):
        pl.semaphore_signal(barrier, inc=1, device_id=target, device_id_type=MESH)

    for change in peers:
        greet(peer_device(change))
    run(has_up, lambda: greet(above))
    run(has_down, lambda: greet(below))

    local[0].wait()
    for p in range(PLANE):
        for part in range(3):
            at = part * width + p * share
            cut_ref[p, :, part * share:(part + 1) * share] = wq_ref[:, at:at + share]
    w_ref[shard_rows, :] = cut_ref[me]
    local[1].wait()
    own_rows = pl.ds(pl.multiple_of(me * tokens, tokens), tokens)
    blocks_ref[own_rows, :] = layer_norm(x_ref[...], gain_ref[...])
    entries, lanes = own_tab_ref.shape
    entry = lax.broadcasted_iota(jnp.int32, (entries, lanes), 0)
    lane = lax.broadcasted_iota(jnp.int32, (entries, lanes), 1)
    far_region = entry % 2
    far_owner = plane * 4 - 1 + entry // 2
    number = far_region * owners + far_owner
    listed = number == mine
    for k in range(near_ref.shape[1]):
        listed = jnp.logical_or(listed, number == near_ref[0, k])
    inside = jnp.logical_and(far_owner >= 0, far_owner < owners)
    listed = jnp.logical_and(listed, inside)
    marked = jnp.logical_or(lane == me, lane == me + HEAD_DIM)
    own_tab_ref[...] = jnp.where(
        jnp.logical_and(marked, jnp.logical_not(listed)), MASKED, 0.0
    ).astype(bf16)
    tabs_ref[me] = own_tab_ref[...]
    local[2].wait()

    pl.semaphore_wait(
        barrier, len(peers) + has_up.astype(jnp.int32) + has_down.astype(jnp.int32)
    )

    pending = []
    sib_target = peer_device(SIB)

    def remote(src, dst, send_sem, recv_sem, target):
        return pltpu.make_async_remote_copy(
            src_ref=src, dst_ref=dst, send_sem=send_sem, recv_sem=recv_sem,
            device_id=target, device_id_type=MESH,
        )

    def start(cond, make):
        run(cond, lambda: make().start())

    def sent(ref, sem, cond=None, early=False):
        pending.append((cond, lambda: remote(ref, ref, sem, sem, sib_target).wait_send(), early))

    def arrive(cond, make):
        run(cond, lambda: make().wait_recv())

    for change in peers:
        to = place(*moved(change))
        start(None, functools.partial(
            remote, cut_ref.at[to], w_ref.at[shard_rows, :], send_w, recv_w.at[change[0]],
            peer_device(change)))
    sent(cut_ref.at[0:PLANE - 1], send_w, early=True)

    def wait_shards(flipped):
        count = sum(change[0] == flipped for change in peers)
        ref = cut_ref.at[0:count]
        arrive(None, functools.partial(
            remote, ref, ref, send_w, recv_w.at[flipped], sib_target))

    for change in peers:
        start(None, functools.partial(
            remote, own_tab_ref, tabs_ref.at[me], send_t, recv_t, peer_device(change)))
    sent(tabs_ref.at[0:PLANE - 1], send_t, early=True)

    def wait_tables():
        ref = tabs_ref.at[0:PLANE - 1]
        arrive(None, functools.partial(remote, ref, ref, send_t, recv_t, sib_target))

    OWN, DIAGONAL = (0, 0, 0), (1, 1, 0)
    LINE, BY_X, BY_Y, BY_BOTH, BY_SIB = range(5)

    def slot(sems, source, to, piece):
        way = tuple(int(a != b) for a, b in zip(source, to))
        if way[2]:
            return sems.at[BY_SIB, way[0] + 2 * way[1]]
        return sems.at[way[0] + 2 * way[1], piece]

    def lane_of(to, source):
        if to != SIB:
            return 0 if to == X else 1
        return 2 if source in (OWN, X) else 3

    class Gather:
        def __init__(self, pieces, view, send, recv):
            self.pieces, self.view, self.send_sem, self.recv = pieces, view, send, recv
            self.first = list(range(pieces // 2))
            self.second = list(range(pieces // 2, pieces))

        def send(self, change, piece, source):
            ref = self.view(source, piece)
            start(None, functools.partial(
                remote, ref, ref, self.send_sem.at[lane_of(change, source)],
                slot(self.recv, source, change, piece), peer_device(change)))

        def wait(self, source, piece):
            ref = self.view(source, piece)
            arrive(None, functools.partial(
                remote, ref, ref, self.send_sem.at[0], slot(self.recv, source, OWN, piece),
                sib_target))

        def own(self, ks):
            for k in ks:
                self.send(X, (self.first + self.second)[k], (0, 0, 0))
                self.send(Y, (self.second + self.first)[k], (0, 0, 0))

        def own_sib(self):
            for piece in range(self.pieces):
                self.send(SIB, piece, (0, 0, 0))

        def direct(self, k):
            a, b = (self.first + self.second)[k], (self.second + self.first)[k]
            onward = k < self.pieces // 2
            self.wait(X, a)
            if onward:
                self.send(Y, a, X)
            self.send(SIB, a, X)
            self.wait(Y, b)
            if onward:
                self.send(X, b, Y)
            self.send(SIB, b, Y)

        def diagonal(self, k):
            for piece in (self.first[k], self.second[k]):
                self.wait((1, 1, 0), piece)
                self.send(SIB, piece, (1, 1, 0))

        def finish(self, sources):
            for source in sources:
                at = pl.multiple_of(place(*moved(source)) * tokens, tokens)
                ref = blocks_ref.at[pl.ds(at, tokens), :]
                arrive(None, functools.partial(
                    remote, ref, ref, self.send_sem.at[0], slot(self.recv, source, OWN, None),
                    sib_target))

    piece_rows = tokens // CHUNKS

    def block_piece(source, piece):
        at = place(*moved(source)) * tokens + piece * piece_rows
        return blocks_ref.at[pl.ds(pl.multiple_of(at, piece_rows), piece_rows), :]

    blocks = Gather(CHUNKS, block_piece, send_b, recv_b)
    for way, count in ((0, 3), (1, 3), (2, 4), (3, 4)):
        sent(blocks_ref.at[0:count * tokens // 2, :], send_b.at[way])

    def line(d):
        return [(plane - d, plane - d >= 0), (plane + d, plane + d < planes)]

    def w_half(z, r):
        at = (r * owners + z * 4) * depth
        return w_ref.at[pl.ds(pl.multiple_of(at, 4 * depth), 4 * depth), :]

    def send_w_half(z, r, up, cond, d):
        ref = w_half(z, r)
        start(both(cond, has_up if up else has_down), functools.partial(
            remote, ref, ref, send_z.at[int(up), d], recv_z.at[z, r], above if up else below))

    def wait_w_half(z, r, cond):
        ref = w_half(z, r)
        arrive(cond, functools.partial(
            remote, ref, ref, send_z.at[0, 0], recv_z.at[z, r], sib_target))

    for d in range(planes - 1):
        for up, cond in ((1, plane - d >= 0), (0, plane + d < planes)):
            cond = jnp.logical_and(cond, has_up if up else has_down)
            sent(go_ref.at[0], send_z.at[up, d], cond, early=True)

    def own_w():
        for flipped in (0, 1):
            wait_shards(flipped)
            for up in (True, False):
                send_w_half(plane, flip(region, flipped), up, None, 0)

    def relay_w(d):
        for flipped in (0, 1):
            for (z, cond), up in zip(line(d), (True, False)):
                wait_w_half(z, flip(region, flipped), cond)
                if d < planes - 1:
                    send_w_half(z, flip(region, flipped), up, cond, d)

    near_planes = planes // 2

    def out_piece(source, first, count, half=None):
        r, y, c = moved(source)
        at, size = (2 * y + c) * depth, depth
        if half is not None:
            size = depth // 2
            at = at + half * size
        return go_ref.at[
            pl.ds(r * planes + first, count), pl.ds(pl.multiple_of(at, size), size), :]

    def line_out(z, up, cond, d):
        ref = out_piece(OWN, z, 1)
        start(both(cond, has_up if up else has_down), functools.partial(
            remote, ref, ref, send_z.at[int(up), d], recv_l.at[z], above if up else below))

    def own_out():
        for up in (True, False):
            line_out(plane, up, None, 0)

    def relay_out(d):
        for (z, cond), up in zip(line(d), (True, False)):
            ref = out_piece(OWN, z, 1)
            arrive(cond, functools.partial(
                remote, ref, ref, send_o.at[0], recv_l.at[z], sib_target))
            if d < planes - 1:
                line_out(z, up, cond, d)

    def ring(d):
        return [(plane, None)] if d == 0 else line(d)

    def spread_out(d):
        for z, cond in ring(d):
            ref = out_piece(OWN, z, 1)
            for way, to in ((0, X), (1, Y)):
                start(cond, functools.partial(
                    remote, ref, ref, send_o.at[way], recv_o.at[way, z // near_planes],
                    peer_device(to)))

    def to_sibling(source, first, count):
        ref = out_piece(source, first, count)
        remote(ref, ref, send_o.at[2], recv_s, sib_target).start()

    def wait_group(way, group):
        ref = out_piece(OWN, group * near_planes, near_planes)
        arrive(None, functools.partial(
            remote, ref, ref, send_o.at[0], recv_o.at[way, group], sib_target))

    def onward_out(group):
        for way, source, to in ((0, X, Y), (1, Y, X)):
            wait_group(way, group)
            ref = out_piece(source, group * near_planes, near_planes, way)
            remote(
                ref, ref, send_o.at[1 - way], recv_o.at[2, group], peer_device(to)).start()
            to_sibling(source, group * near_planes, near_planes)

    def diagonal_out(group):
        wait_group(2, group)
        to_sibling(DIAGONAL, group * near_planes, near_planes)

    def finish_out():
        ref = go_ref.at[0:planes]
        arrive(None, functools.partial(remote, ref, ref, send_o.at[2], recv_s, sib_target))

    pair_rows = 2 * tokens
    low = lax.broadcasted_iota(jnp.int32, (tokens, share), 1) < HEAD_DIM
    at_lane = lax.broadcasted_iota(jnp.int32, (tokens, share), 1)
    ones = jnp.ones((tokens, share), bf16)

    def keep_keys(slot, keys, values):
        table = tabs_ref[0].astype(f32)
        for p in range(1, PLANE):
            table = table + tabs_ref[p].astype(f32)
        which = lax.broadcasted_iota(jnp.int32, table.shape, 0)
        for r in (0, 1):
            absent = jnp.sum(
                jnp.where(which == slot * 2 + r, table, 0.0), axis=0, keepdims=True
            )
            absent = jnp.broadcast_to(absent, (tokens, share)).astype(bf16)
            rows = pl.ds(pl.multiple_of(slot * pair_rows + r * tokens, tokens), tokens)
            part = slice(r * tokens, (r + 1) * tokens)
            kl_ref[rows, :] = jnp.where(low, keys[part], absent)
            kh_ref[rows, :] = jnp.where(low, absent, keys[part])
            vl_ref[rows, :] = jnp.where(low, values[part], ones)
            vh_ref[rows, :] = jnp.where(low, ones, values[part])

    def project_step(i):
        late = i // 2
        a = i + late * (1 - 2 * (i % 2))
        project(a + row * (3 - 2 * a), row + late * (1 - 2 * row), i % 2 == 0)

    def project(j, edge, at_edge):
        rows = pl.ds(pl.multiple_of(j * pair_rows, pair_rows), pair_rows)
        part = jnp.dot(blocks_ref[rows, :], w_ref[...], preferred_element_type=f32).astype(bf16)
        queries = part[:, 0:share] * bf16(HEAD_DIM ** (-0.5))
        keys, values = part[:, share:2 * share], part[:, 2 * share:]

        @pl.when(at_edge)
        def _():
            edge_out_ref[edge, :, 0:share] = keys
            edge_out_ref[edge, :, share:] = values
            send_edge(edge)

        for r in (0, 1):
            q = 2 * j + r
            q_rows = pl.ds(pl.multiple_of(q * tokens, tokens), tokens)
            mark_low = jnp.where(at_lane == q, 1.0, 0.0).astype(bf16)
            mark_high = jnp.where(at_lane == q + HEAD_DIM, 1.0, 0.0).astype(bf16)
            piece = queries[r * tokens:(r + 1) * tokens]
            ql_ref[q_rows, :] = jnp.where(low, piece, mark_high)
            qh_ref[q_rows, :] = jnp.where(low, mark_low, piece)
        keep_keys(j + 1, keys, values)

    def send_edge(e):
        z = plane + 2 * e - 1

        @pl.when(jnp.logical_and(z >= 0, z < planes))
        def _():
            remote(
                edge_out_ref.at[e], edge_in_ref.at[1 - e], send_e.at[e], recv_e.at[1 - e],
                device(region, z, row, core)).start()

    sent(edge_out_ref.at[0], send_e.at[0], has_down)
    sent(edge_out_ref.at[1], send_e.at[1], has_up)

    def take_edge(e):
        z = plane + 2 * e - 1
        there = jnp.logical_and(z >= 0, z < planes)
        arrive(there, functools.partial(
            remote, edge_in_ref.at[e], edge_in_ref.at[e], send_e.at[e], recv_e.at[e], sib_target))

        @pl.when(jnp.logical_not(there))
        def _():
            edge_in_ref[e] = jnp.zeros(edge_in_ref.shape[1:], bf16)

        keep_keys(e * 5, edge_in_ref[e, :, 0:share], edge_in_ref[e, :, share:])

    def order(i):
        g = i // 2
        late = g // 2
        a = (1 - late) * (2 - g) + late * (9 - 3 * g)
        j = a + row * (3 - 2 * a)
        r = (i % 2) * region + (1 - i % 2) * (1 - region)
        return j, r

    def hand_over(i, out):
        j, r = order(i)
        q = 2 * j + r
        staged_ref[i] = out

        @pl.when(q == me)
        def _():
            mixed_ref[me] = out

        @pl.when(q != me)
        def _():
            remote(
                staged_ref.at[i], mixed_ref.at[me], send_m, recv_m,
                device(r, plane, j // 2, j % 2)).start()

    def attend_rows(j, start_row, count):
        rows = pl.ds(pl.multiple_of(start_row, count), count)
        keys = pl.ds(pl.multiple_of(j * pair_rows, pair_rows), 3 * pair_rows)
        heads = ((ql_ref, kl_ref, vl_ref), (qh_ref, kh_ref, vh_ref))
        scores = [
            lax.dot_general(
                q_ref[rows, :], k_ref[keys, :], (((1,), (1,)), ((), ())),
                preferred_element_type=f32,
            )
            for q_ref, k_ref, _ in heads
        ]
        mixes = []
        for score, (_, _, v_ref) in zip(scores, heads):
            shifted = jnp.exp(score - jnp.max(score, axis=-1, keepdims=True)).astype(bf16)
            mixes.append(jnp.dot(shifted, v_ref[keys, :], preferred_element_type=f32))
        lower = lax.broadcasted_iota(jnp.int32, (count, share), 1) < HEAD_DIM
        total = pltpu.roll(jnp.where(lower, mixes[1], mixes[0]), HEAD_DIM, 1)
        return (jnp.where(lower, mixes[0], mixes[1]) / total).astype(bf16)

    def attend_block(i):
        j, r = order(i)
        hand_over(i, attend_rows(j, j * pair_rows + r * tokens, tokens))

    blocks.own(range(CHUNKS))
    blocks.own_sib()
    own_w()
    own_out()
    blocks.direct(0)
    relay_w(1)
    relay_out(1)
    blocks.direct(1)
    spread_out(0)
    spread_out(1)
    relay_w(2)
    relay_out(2)
    spread_out(2)
    blocks.direct(2)
    blocks.direct(3)
    relay_w(planes - 1)
    wait_tables()
    blocks.finish([SIB, (1, 0, 1)])

    def drain(sends):
        for cond, wait, _ in sends:
            run(cond, wait)

    early = [entry for entry in pending if entry[2]]
    late = [entry for entry in pending if not entry[2]]
    pending.clear()

    def projections(i, carry):
        @pl.when(i == 2)
        def _():
            blocks.diagonal(0)
            drain(early)
            blocks.diagonal(1)
            blocks.finish([(0, 1, 1), (1, 1, 1)])

        project_step(i)
        return carry

    lax.fori_loop(0, PLANE // 2, projections, 0)
    relay_out(planes - 1)
    spread_out(planes - 1)
    to_sibling(OWN, 0, planes)
    for way in (0, 1):
        sent(go_ref.at[pl.ds(0, planes * 3 // 4), 0:2 * depth, :], send_o.at[way])
    sent(go_ref.at[0:planes], send_o.at[2])
    near = plane // near_planes

    HOOKS = {
        2: [lambda: onward_out(near)],
        4: [lambda: take_edge(1 - row), lambda: onward_out(1 - near)],
        6: [lambda: take_edge(row), lambda: diagonal_out(near)],
    }

    def attention(i, carry):
        for at, hooks in HOOKS.items():
            @pl.when(i == at)
            def _():
                for hook in hooks:
                    hook()

        attend_block(i)
        return carry

    lax.fori_loop(0, PLANE, attention, 0)
    diagonal_out(1 - near)
    finish_out()
    pieces = staged_ref.at[0:PLANE - 1]
    arrive(None, functools.partial(remote, pieces, pieces, send_m, recv_m, sib_target))
    sent(pieces, send_m)
    mixed = jnp.concatenate([mixed_ref[p] for p in range(PLANE)], axis=1)
    tile = min(512, width)
    for at in range(0, width, tile):
        weight = go_ref[:, :, at:at + tile].reshape(width, tile)
        projected = jnp.dot(mixed, weight, preferred_element_type=f32)
        out_ref[:, at:at + tile] = (
            x_ref[:, at:at + tile].astype(f32) + projected
        ).astype(out_ref.dtype)
    drain(late + pending)


def fused(block, qkv_weight, out_weight, norm_gain, near):
    owners = lax.axis_size("owner")
    devices = lax.axis_size("region") * owners
    planes = owners // 4
    tokens, width = block.shape
    depth = qkv_weight.shape[0]
    share = 2 * HEAD_DIM
    bf16 = jnp.bfloat16
    vmem = pl.BlockSpec(memory_space=pltpu.VMEM)
    dma = pltpu.SemaphoreType.DMA
    return pl.pallas_call(
        functools.partial(fused_kernel, owners),
        out_shape=pltpu.VMEM(block.shape, block.dtype),
        in_specs=[pl.BlockSpec(memory_space=pl.ANY)] * 3 + [vmem] + [pl.BlockSpec(memory_space=pltpu.SMEM)],
        out_specs=vmem,
        scratch_shapes=[
            pltpu.VMEM(block.shape, bf16),
            pltpu.VMEM(qkv_weight.shape, bf16),
            pltpu.VMEM((PLANE, depth, 3 * share), bf16),
            pltpu.VMEM((devices * depth, 3 * share), bf16),
            pltpu.VMEM((2 * planes, 4 * depth, width), bf16),
            pltpu.VMEM((PLANE * tokens, width), bf16),
            pltpu.VMEM((16, share), bf16),
            pltpu.VMEM((PLANE, 16, share), bf16),
        ] + [pltpu.VMEM((PLANE * tokens, share), bf16)] * 2
        + [pltpu.VMEM((12 * tokens, share), bf16)] * 4
        + [pltpu.VMEM((2, 2 * tokens, 2 * share), bf16)] * 2
        + [pltpu.VMEM((PLANE, tokens, share), bf16)] * 2
        + [
            dma, dma((2,)), dma, dma,
            dma((2, planes - 1)), dma((planes, 2)), dma((planes,)),
            dma((4,)), dma((5, CHUNKS)), dma((3,)), dma((3, 2)), dma,
            dma((2,)), dma((2,)), dma, dma, dma((3,)),
        ],
        compiler_params=pltpu.CompilerParams(
            collective_id=0, has_side_effects=True, vmem_limit_bytes=54 * 1024 * 1024
        ),
        name="fused",
    )(block, qkv_weight, out_weight, norm_gain, near)


def attend_kernel(listed_ref, x_ref, xs_ref, gain_ref, bias_ref, wq_ref, wo_ref, out_ref,
                  normed_ref, q_ref, kv_ref, mixed_ref):
    tokens, width = x_ref.shape
    others = xs_ref.shape[0]
    gain = gain_ref[...]
    normed_ref[0:tokens, :] = layer_norm(x_ref[...], gain)

    @pl.loop(0, others)
    def _(slot):
        rows = pl.ds(pl.multiple_of((slot + 1) * tokens, tokens), tokens)
        block = xs_ref[slot].astype(jnp.float32)
        block = jnp.where(listed_ref[slot] > 0, block, 0.0)
        normed_ref[rows, :] = layer_norm(block, gain)

    tile = min(512, width)

    @pl.loop(0, width // tile)
    def _(step):
        cols = pl.ds(pl.multiple_of(step * tile, tile), tile)
        part = jnp.dot(normed_ref[0:tokens, :], wq_ref[:, cols], preferred_element_type=jnp.float32)
        q_ref[:, cols] = part.astype(jnp.bfloat16) * jnp.bfloat16(HEAD_DIM ** (-0.5))

    @pl.loop(0, 2 * width // tile)
    def _(step):
        cols = pl.ds(pl.multiple_of(step * tile, tile), tile)
        from_cols = pl.ds(pl.multiple_of(width + step * tile, tile), tile)
        kv_ref[:, cols] = jnp.dot(
            normed_ref[...], wq_ref[:, from_cols], preferred_element_type=jnp.float32
        ).astype(jnp.bfloat16)

    pair = 2 * HEAD_DIM
    low = lax.broadcasted_iota(jnp.int32, (tokens, pair), 1) < HEAD_DIM
    bias = bias_ref[...]

    @pl.loop(0, width // pair)
    def _(group):
        cols = pl.ds(pl.multiple_of(group * pair, pair), pair)
        value_cols = pl.ds(pl.multiple_of(width + group * pair, pair), pair)
        queries = q_ref[:, cols]
        keys = kv_ref[:, cols]
        values = kv_ref[:, value_cols]
        halves = []
        for mine in (low, jnp.logical_not(low)):
            query = jnp.where(mine, queries, jnp.zeros_like(queries))
            scores = lax.dot_general(
                query, keys, (((1,), (1,)), ((), ())), preferred_element_type=jnp.float32
            ) + bias
            shifted = jnp.exp(scores - jnp.max(scores, axis=-1, keepdims=True))
            total = jnp.sum(shifted, axis=-1, keepdims=True)
            mixed = jnp.dot(shifted.astype(jnp.bfloat16), values, preferred_element_type=jnp.float32)
            halves.append(mixed / total)
        mixed_ref[:, cols] = jnp.where(low, halves[0], halves[1]).astype(jnp.bfloat16)

    @pl.loop(0, width // tile)
    def _(step):
        cols = pl.ds(pl.multiple_of(step * tile, tile), tile)
        projected = jnp.dot(mixed_ref[...], wo_ref[:, cols], preferred_element_type=jnp.float32)
        out_ref[:, cols] = (x_ref[:, cols].astype(jnp.float32) + projected).astype(out_ref.dtype)


def attend(listed, block, others, norm_gain, bias, qkv_weight, out_weight):
    tokens, width = block.shape
    count = (others.shape[0] + 1) * tokens
    vmem = pl.BlockSpec(memory_space=pltpu.VMEM)
    return pl.pallas_call(
        attend_kernel,
        out_shape=jax.ShapeDtypeStruct(block.shape, block.dtype),
        in_specs=[pl.BlockSpec(memory_space=pltpu.SMEM)] + [vmem] * 6,
        out_specs=vmem,
        scratch_shapes=[
            pltpu.VMEM((count, width), jnp.bfloat16),
            pltpu.VMEM((tokens, width), jnp.bfloat16),
            pltpu.VMEM((count, 2 * width), jnp.bfloat16),
            pltpu.VMEM((tokens, width), jnp.bfloat16),
        ],
        compiler_params=pltpu.CompilerParams(vmem_limit_bytes=60 * 1024 * 1024),
        name="attend",
    )(listed, block, others, norm_gain, bias, qkv_weight, out_weight)


def shards(voxels, norm_gain, qkv_weight, out_weight, neighbours):
    block_size, model_width = voxels.shape[-2:]
    block = voxels.reshape(block_size, model_width)
    regions, owners = (lax.axis_size("region"), lax.axis_size("owner"))
    region, owner = (lax.axis_index("region"), lax.axis_index("owner"))
    share = 2 * HEAD_DIM
    together = regions == 2 and owners % 8 == 0 and model_width == PLANE * share
    together = together and block_size % (16 * CHUNKS) == 0 and voxels.shape[2] == 1
    if together:
        out = fused(block, qkv_weight, out_weight, norm_gain[None, :], neighbours.reshape(1, -1))
        return out.reshape(voxels.shape)
    wide = padded(voxels[:, :, 0], (("owner", 1), ("region", 0)), 1)
    wide = wide.reshape(-1, block_size, model_width)
    middle = wide.shape[0] // 2
    others = jnp.concatenate([wide[:middle], wide[middle + 1:]], axis=0)
    full_qkv = lax.all_gather(qkv_weight, ("region", "owner"), axis=0, tiled=True)
    full_out = lax.all_gather(out_weight, ("region", "owner"), axis=0, tiled=True)
    offsets = [(i, j) for i in (-1, 0, 1) for j in (-1, 0, 1) if i or j]
    numbers = []
    for up, along in offsets:
        inside = (owner + along >= 0) & (owner + along < owners)
        number = (region + up) * owners + owner + along
        numbers.append(jnp.where(inside & (number >= 0), number, -2))
    listed = jnp.any(neighbours.reshape(1, -1) == jnp.stack(numbers)[:, None], axis=1)
    present = jnp.concatenate([jnp.ones((1,), bool), listed])
    bias = jnp.repeat(jnp.where(present, 0.0, MASKED).astype(jnp.float32), block_size)[None, :]
    out = attend(
        listed.astype(jnp.int32), block, others, norm_gain[None, :], bias, full_qkv, full_out
    )
    return out.reshape(voxels.shape)


def solution(mesh):
    return jax.shard_map(
        shards,
        mesh=mesh,
        in_specs=(
            P("region", "owner", None, None, None),
            P(),
            P(("region", "owner"), None),
            P(("region", "owner"), None),
            P("region", "owner", None, None),
        ),
        out_specs=P("region", "owner", None, None, None),
        check_vma=False,
    )
```

```python
import functools

import jax
import jax.numpy as jnp
from jax import lax
from jax.experimental import pallas as pl
from jax.experimental.pallas import tpu as pltpu
from jax.sharding import PartitionSpec as P

HEAD_DIM = 64
MESH = pl.DeviceIdType.MESH
PLANE = 8
CHUNKS = 4
MASKED = -1e30


def padded(value, sides, width):
    for axis, dim in sides:
        devices, length = (lax.axis_size(axis), value.shape[dim])
        up = [(i, (i + 1) % devices) for i in range(devices - 1)]
        down = [(j, i) for i, j in up]
        last = lax.slice_in_dim(value, length - width, length, axis=dim)
        first = lax.slice_in_dim(value, 0, width, axis=dim)
        before = lax.ppermute(last, axis, up)
        after = lax.ppermute(first, axis, down)
        value = jnp.concatenate([before, value, after], axis=dim)
    return value


def layer_norm(inputs, norm_gain):
    widened = inputs.astype(jnp.float32)
    average = jnp.mean(widened, axis=-1, keepdims=True)
    spread = jnp.mean((widened - average) ** 2, axis=-1, keepdims=True)
    return ((widened - average) * lax.rsqrt(spread + 1e-06) * norm_gain).astype(jnp.bfloat16)


def fused_kernel(owners, x_hbm, wq_hbm, wo_hbm, gain_hbm, near_hbm, out_ref,
                 x_ref, wq_ref, cut_ref, w_ref, go_ref, blocks_ref, own_tab_ref, tabs_ref,
                 ql_ref, qh_ref, kl_ref, kh_ref, vl_ref, vh_ref,
                 edge_out_ref, edge_in_ref, staged_ref, mixed_ref,
                 send_w, recv_w, send_t, recv_t, send_z, recv_z, recv_l, send_b, recv_b,
                 send_o, recv_o, recv_s, send_e, recv_e, send_m, recv_m, local_sem, gain_ref, near_ref):
    tokens, width = x_ref.shape
    depth = wo_hbm.shape[0]
    share = 2 * HEAD_DIM
    planes = owners // 4
    region = lax.axis_index("region")
    owner = lax.axis_index("owner")
    core = lax.rem(owner, 2)
    row = lax.rem(owner // 2, 2)
    plane = owner // 4
    bf16, f32 = jnp.bfloat16, jnp.float32

    def place(r, y, c):
        return (2 * y + c) * 2 + r

    def device(r, z, y, c):
        return (r, z * 4 + y * 2 + c)

    me = place(region, row, core)
    mine = region * owners + owner
    peers = [
        (dr, dy, dc) for dr in (1, 0) for dy in (1, 0) for dc in (1, 0) if dr or dy or dc
    ]

    def flip(value, change):
        return 1 - value if change else value

    def moved(change):
        dr, dy, dc = change
        return flip(region, dr), flip(row, dy), flip(core, dc)

    def peer_device(change):
        r, y, c = moved(change)
        return device(r, plane, y, c)

    X, Y, SIB = (1, 0, 0), (0, 1, 0), (0, 0, 1)
    has_up = plane < planes - 1
    has_down = plane > 0
    above = device(region, plane + 1, row, core)
    below = device(region, plane - 1, row, core)

    def run(cond, fn):
        if cond is None:
            fn()
        else:
            pl.when(cond)(fn)

    def both(a, b):
        if a is None:
            return b
        return a if b is None else jnp.logical_and(a, b)

    shard_rows = pl.ds(pl.multiple_of(mine * depth, depth), depth)
    local = [
        pltpu.make_async_copy(wq_hbm, wq_ref, local_sem.at[0]),
        pltpu.make_async_copy(x_hbm, x_ref, local_sem.at[1]),
        pltpu.make_async_copy(
            wo_hbm,
            go_ref.at[region * planes + plane, pl.ds(
                pl.multiple_of((2 * row + core) * depth, depth), depth), :],
            local_sem.at[2],
        ),
    ]
    local.append(pltpu.make_async_copy(gain_hbm, gain_ref, local_sem.at[3]))
    local.append(pltpu.make_async_copy(near_hbm, near_ref, local_sem.at[4]))
    for copy in local:
        copy.start()
    barrier = pltpu.get_barrier_semaphore()

    def greet(target):
        pl.semaphore_signal(barrier, inc=1, device_id=target, device_id_type=MESH)

    for change in peers:
        greet(peer_device(change))
    run(has_up, lambda: greet(above))
    run(has_down, lambda: greet(below))

    local[0].wait()
    for p in range(PLANE):
        for part in range(3):
            at = part * width + p * share
            cut_ref[p, :, part * share:(part + 1) * share] = wq_ref[:, at:at + share]
    w_ref[shard_rows, :] = cut_ref[me]
    local[1].wait()
    local[3].wait()
    local[4].wait()
    own_rows = pl.ds(pl.multiple_of(me * tokens, tokens), tokens)
    blocks_ref[own_rows, :] = layer_norm(x_ref[...], gain_ref[...])
    entries, lanes = own_tab_ref.shape
    entry = lax.broadcasted_iota(jnp.int32, (entries, lanes), 0)
    lane = lax.broadcasted_iota(jnp.int32, (entries, lanes), 1)
    far_region = entry % 2
    far_owner = plane * 4 - 1 + entry // 2
    number = far_region * owners + far_owner
    listed = number == mine
    for k in range(near_ref.shape[1]):
        listed = jnp.logical_or(listed, number == near_ref[0, k])
    inside = jnp.logical_and(far_owner >= 0, far_owner < owners)
    listed = jnp.logical_and(listed, inside)
    marked = jnp.logical_or(lane == me, lane == me + HEAD_DIM)
    own_tab_ref[...] = jnp.where(
        jnp.logical_and(marked, jnp.logical_not(listed)), MASKED, 0.0
    ).astype(bf16)
    tabs_ref[me] = own_tab_ref[...]
    local[2].wait()

    pl.semaphore_wait(
        barrier, len(peers) + has_up.astype(jnp.int32) + has_down.astype(jnp.int32)
    )

    pending = []
    sib_target = peer_device(SIB)

    def remote(src, dst, send_sem, recv_sem, target):
        return pltpu.make_async_remote_copy(
            src_ref=src, dst_ref=dst, send_sem=send_sem, recv_sem=recv_sem,
            device_id=target, device_id_type=MESH,
        )

    def start(cond, make):
        run(cond, lambda: make().start())

    def sent(ref, sem, cond=None, early=False):
        pending.append((cond, lambda: remote(ref, ref, sem, sem, sib_target).wait_send(), early))

    def arrive(cond, make):
        run(cond, lambda: make().wait_recv())

    for change in peers:
        to = place(*moved(change))
        start(None, functools.partial(
            remote, cut_ref.at[to], w_ref.at[shard_rows, :], send_w, recv_w.at[change[0]],
            peer_device(change)))
    sent(cut_ref.at[0:PLANE - 1], send_w, early=True)

    def wait_shards(flipped):
        count = sum(change[0] == flipped for change in peers)
        ref = cut_ref.at[0:count]
        arrive(None, functools.partial(
            remote, ref, ref, send_w, recv_w.at[flipped], sib_target))

    for change in peers:
        start(None, functools.partial(
            remote, own_tab_ref, tabs_ref.at[me], send_t, recv_t, peer_device(change)))
    sent(tabs_ref.at[0:PLANE - 1], send_t, early=True)

    def wait_tables():
        ref = tabs_ref.at[0:PLANE - 1]
        arrive(None, functools.partial(remote, ref, ref, send_t, recv_t, sib_target))

    OWN, DIAGONAL = (0, 0, 0), (1, 1, 0)
    LINE, BY_X, BY_Y, BY_BOTH, BY_SIB = range(5)

    def slot(sems, source, to, piece):
        way = tuple(int(a != b) for a, b in zip(source, to))
        if way[2]:
            return sems.at[BY_SIB, way[0] + 2 * way[1]]
        return sems.at[way[0] + 2 * way[1], piece]

    def lane_of(to, source):
        if to != SIB:
            return 0 if to == X else 1
        return 2 if source in (OWN, X) else 3

    class Gather:
        def __init__(self, pieces, view, send, recv):
            self.pieces, self.view, self.send_sem, self.recv = pieces, view, send, recv
            self.first = list(range(pieces // 2))
            self.second = list(range(pieces // 2, pieces))

        def send(self, change, piece, source):
            ref = self.view(source, piece)
            start(None, functools.partial(
                remote, ref, ref, self.send_sem.at[lane_of(change, source)],
                slot(self.recv, source, change, piece), peer_device(change)))

        def wait(self, source, piece):
            ref = self.view(source, piece)
            arrive(None, functools.partial(
                remote, ref, ref, self.send_sem.at[0], slot(self.recv, source, OWN, piece),
                sib_target))

        def own(self, ks):
            for k in ks:
                self.send(X, (self.first + self.second)[k], (0, 0, 0))
                self.send(Y, (self.second + self.first)[k], (0, 0, 0))

        def own_sib(self):
            for piece in range(self.pieces):
                self.send(SIB, piece, (0, 0, 0))

        def direct(self, k):
            a, b = (self.first + self.second)[k], (self.second + self.first)[k]
            onward = k < self.pieces // 2
            self.wait(X, a)
            if onward:
                self.send(Y, a, X)
            self.send(SIB, a, X)
            self.wait(Y, b)
            if onward:
                self.send(X, b, Y)
            self.send(SIB, b, Y)

        def diagonal(self, k):
            for piece in (self.first[k], self.second[k]):
                self.wait((1, 1, 0), piece)
                self.send(SIB, piece, (1, 1, 0))

        def finish(self, sources):
            for source in sources:
                at = pl.multiple_of(place(*moved(source)) * tokens, tokens)
                ref = blocks_ref.at[pl.ds(at, tokens), :]
                arrive(None, functools.partial(
                    remote, ref, ref, self.send_sem.at[0], slot(self.recv, source, OWN, None),
                    sib_target))

    piece_rows = tokens // CHUNKS

    def block_piece(source, piece):
        at = place(*moved(source)) * tokens + piece * piece_rows
        return blocks_ref.at[pl.ds(pl.multiple_of(at, piece_rows), piece_rows), :]

    blocks = Gather(CHUNKS, block_piece, send_b, recv_b)
    for way, count in ((0, 3), (1, 3), (2, 4), (3, 4)):
        sent(blocks_ref.at[0:count * tokens // 2, :], send_b.at[way])

    def line(d):
        return [(plane - d, plane - d >= 0), (plane + d, plane + d < planes)]

    def w_half(z, r):
        at = (r * owners + z * 4) * depth
        return w_ref.at[pl.ds(pl.multiple_of(at, 4 * depth), 4 * depth), :]

    def send_w_half(z, r, up, cond, d):
        ref = w_half(z, r)
        start(both(cond, has_up if up else has_down), functools.partial(
            remote, ref, ref, send_z.at[int(up), d], recv_z.at[z, r], above if up else below))

    def wait_w_half(z, r, cond):
        ref = w_half(z, r)
        arrive(cond, functools.partial(
            remote, ref, ref, send_z.at[0, 0], recv_z.at[z, r], sib_target))

    for d in range(planes - 1):
        for up, cond in ((1, plane - d >= 0), (0, plane + d < planes)):
            cond = jnp.logical_and(cond, has_up if up else has_down)
            sent(go_ref.at[0], send_z.at[up, d], cond, early=True)

    def own_w():
        for flipped in (0, 1):
            wait_shards(flipped)
            for up in (True, False):
                send_w_half(plane, flip(region, flipped), up, None, 0)

    def relay_w(d):
        for flipped in (0, 1):
            for (z, cond), up in zip(line(d), (True, False)):
                wait_w_half(z, flip(region, flipped), cond)
                if d < planes - 1:
                    send_w_half(z, flip(region, flipped), up, cond, d)

    near_planes = planes // 2

    def out_piece(source, first, count, half=None):
        r, y, c = moved(source)
        at, size = (2 * y + c) * depth, depth
        if half is not None:
            size = depth // 2
            at = at + half * size
        return go_ref.at[
            pl.ds(r * planes + first, count), pl.ds(pl.multiple_of(at, size), size), :]

    def line_out(z, up, cond, d):
        ref = out_piece(OWN, z, 1)
        start(both(cond, has_up if up else has_down), functools.partial(
            remote, ref, ref, send_z.at[int(up), d], recv_l.at[z], above if up else below))

    def own_out():
        for up in (True, False):
            line_out(plane, up, None, 0)

    def relay_out(d):
        for (z, cond), up in zip(line(d), (True, False)):
            ref = out_piece(OWN, z, 1)
            arrive(cond, functools.partial(
                remote, ref, ref, send_o.at[0], recv_l.at[z], sib_target))
            if d < planes - 1:
                line_out(z, up, cond, d)

    def ring(d):
        return [(plane, None)] if d == 0 else line(d)

    def spread_out(d):
        for z, cond in ring(d):
            ref = out_piece(OWN, z, 1)
            for way, to in ((0, X), (1, Y)):
                start(cond, functools.partial(
                    remote, ref, ref, send_o.at[way], recv_o.at[way, z // near_planes],
                    peer_device(to)))

    def to_sibling(source, first, count):
        ref = out_piece(source, first, count)
        remote(ref, ref, send_o.at[2], recv_s, sib_target).start()

    def wait_group(way, group):
        ref = out_piece(OWN, group * near_planes, near_planes)
        arrive(None, functools.partial(
            remote, ref, ref, send_o.at[0], recv_o.at[way, group], sib_target))

    def onward_out(group):
        for way, source, to in ((0, X, Y), (1, Y, X)):
            wait_group(way, group)
            ref = out_piece(source, group * near_planes, near_planes, way)
            remote(
                ref, ref, send_o.at[1 - way], recv_o.at[2, group], peer_device(to)).start()
            to_sibling(source, group * near_planes, near_planes)

    def diagonal_out(group):
        wait_group(2, group)
        to_sibling(DIAGONAL, group * near_planes, near_planes)

    def finish_out():
        ref = go_ref.at[0:planes]
        arrive(None, functools.partial(remote, ref, ref, send_o.at[2], recv_s, sib_target))

    pair_rows = 2 * tokens
    low = lax.broadcasted_iota(jnp.int32, (tokens, share), 1) < HEAD_DIM
    at_lane = lax.broadcasted_iota(jnp.int32, (tokens, share), 1)
    ones = jnp.ones((tokens, share), bf16)

    def keep_keys(slot, keys, values):
        table = tabs_ref[0].astype(f32)
        for p in range(1, PLANE):
            table = table + tabs_ref[p].astype(f32)
        which = lax.broadcasted_iota(jnp.int32, table.shape, 0)
        for r in (0, 1):
            absent = jnp.sum(
                jnp.where(which == slot * 2 + r, table, 0.0), axis=0, keepdims=True
            )
            absent = jnp.broadcast_to(absent, (tokens, share)).astype(bf16)
            rows = pl.ds(pl.multiple_of(slot * pair_rows + r * tokens, tokens), tokens)
            part = slice(r * tokens, (r + 1) * tokens)
            kl_ref[rows, :] = jnp.where(low, keys[part], absent)
            kh_ref[rows, :] = jnp.where(low, absent, keys[part])
            vl_ref[rows, :] = jnp.where(low, values[part], ones)
            vh_ref[rows, :] = jnp.where(low, ones, values[part])

    def project_step(i):
        late = i // 2
        a = i + late * (1 - 2 * (i % 2))
        project(a + row * (3 - 2 * a), row + late * (1 - 2 * row), i % 2 == 0)

    def project(j, edge, at_edge):
        rows = pl.ds(pl.multiple_of(j * pair_rows, pair_rows), pair_rows)
        part = jnp.dot(blocks_ref[rows, :], w_ref[...], preferred_element_type=f32).astype(bf16)
        queries = part[:, 0:share] * bf16(HEAD_DIM ** (-0.5))
        keys, values = part[:, share:2 * share], part[:, 2 * share:]

        @pl.when(at_edge)
        def _():
            edge_out_ref[edge, :, 0:share] = keys
            edge_out_ref[edge, :, share:] = values
            send_edge(edge)

        for r in (0, 1):
            q = 2 * j + r
            q_rows = pl.ds(pl.multiple_of(q * tokens, tokens), tokens)
            mark_low = jnp.where(at_lane == q, 1.0, 0.0).astype(bf16)
            mark_high = jnp.where(at_lane == q + HEAD_DIM, 1.0, 0.0).astype(bf16)
            piece = queries[r * tokens:(r + 1) * tokens]
            ql_ref[q_rows, :] = jnp.where(low, piece, mark_high)
            qh_ref[q_rows, :] = jnp.where(low, mark_low, piece)
        keep_keys(j + 1, keys, values)

    def send_edge(e):
        z = plane + 2 * e - 1

        @pl.when(jnp.logical_and(z >= 0, z < planes))
        def _():
            remote(
                edge_out_ref.at[e], edge_in_ref.at[1 - e], send_e.at[e], recv_e.at[1 - e],
                device(region, z, row, core)).start()

    sent(edge_out_ref.at[0], send_e.at[0], has_down)
    sent(edge_out_ref.at[1], send_e.at[1], has_up)

    def take_edge(e):
        z = plane + 2 * e - 1
        there = jnp.logical_and(z >= 0, z < planes)
        arrive(there, functools.partial(
            remote, edge_in_ref.at[e], edge_in_ref.at[e], send_e.at[e], recv_e.at[e], sib_target))

        @pl.when(jnp.logical_not(there))
        def _():
            edge_in_ref[e] = jnp.zeros(edge_in_ref.shape[1:], bf16)

        keep_keys(e * 5, edge_in_ref[e, :, 0:share], edge_in_ref[e, :, share:])

    def order(i):
        g = i // 2
        late = g // 2
        a = (1 - late) * (2 - g) + late * (9 - 3 * g)
        j = a + row * (3 - 2 * a)
        r = (i % 2) * region + (1 - i % 2) * (1 - region)
        return j, r

    def hand_over(i, out):
        j, r = order(i)
        q = 2 * j + r
        staged_ref[i] = out

        @pl.when(q == me)
        def _():
            mixed_ref[me] = out

        @pl.when(q != me)
        def _():
            remote(
                staged_ref.at[i], mixed_ref.at[me], send_m, recv_m,
                device(r, plane, j // 2, j % 2)).start()

    def attend_rows(j, start_row, count):
        rows = pl.ds(pl.multiple_of(start_row, count), count)
        keys = pl.ds(pl.multiple_of(j * pair_rows, pair_rows), 3 * pair_rows)
        heads = ((ql_ref, kl_ref, vl_ref), (qh_ref, kh_ref, vh_ref))
        scores = [
            lax.dot_general(
                q_ref[rows, :], k_ref[keys, :], (((1,), (1,)), ((), ())),
                preferred_element_type=f32,
            )
            for q_ref, k_ref, _ in heads
        ]
        mixes = []
        for score, (_, _, v_ref) in zip(scores, heads):
            shifted = jnp.exp(score - jnp.max(score, axis=-1, keepdims=True)).astype(bf16)
            mixes.append(jnp.dot(shifted, v_ref[keys, :], preferred_element_type=f32))
        lower = lax.broadcasted_iota(jnp.int32, (count, share), 1) < HEAD_DIM
        total = pltpu.roll(jnp.where(lower, mixes[1], mixes[0]), HEAD_DIM, 1)
        return (jnp.where(lower, mixes[0], mixes[1]) / total).astype(bf16)

    def attend_block(i):
        j, r = order(i)
        hand_over(i, attend_rows(j, j * pair_rows + r * tokens, tokens))

    blocks.own(range(CHUNKS))
    blocks.own_sib()
    own_w()
    own_out()
    blocks.direct(0)
    relay_w(1)
    relay_out(1)
    blocks.direct(1)
    spread_out(0)
    spread_out(1)
    relay_w(2)
    relay_out(2)
    spread_out(2)
    blocks.direct(2)
    blocks.direct(3)
    relay_w(planes - 1)
    wait_tables()
    blocks.finish([SIB, (1, 0, 1)])

    def drain(sends):
        for cond, wait, _ in sends:
            run(cond, wait)

    early = [entry for entry in pending if entry[2]]
    late = [entry for entry in pending if not entry[2]]
    pending.clear()

    def projections(i, carry):
        @pl.when(i == 2)
        def _():
            blocks.diagonal(0)
            drain(early)
            blocks.diagonal(1)
            blocks.finish([(0, 1, 1), (1, 1, 1)])

        project_step(i)
        return carry

    lax.fori_loop(0, PLANE // 2, projections, 0)
    relay_out(planes - 1)
    spread_out(planes - 1)
    to_sibling(OWN, 0, planes)
    for way in (0, 1):
        sent(go_ref.at[pl.ds(0, planes * 3 // 4), 0:2 * depth, :], send_o.at[way])
    sent(go_ref.at[0:planes], send_o.at[2])
    near = plane // near_planes

    HOOKS = {
        2: [lambda: onward_out(near)],
        4: [lambda: take_edge(1 - row), lambda: onward_out(1 - near)],
        6: [lambda: take_edge(row), lambda: diagonal_out(near)],
    }

    def attention(i, carry):
        for at, hooks in HOOKS.items():
            @pl.when(i == at)
            def _():
                for hook in hooks:
                    hook()

        attend_block(i)
        return carry

    lax.fori_loop(0, PLANE, attention, 0)
    diagonal_out(1 - near)
    finish_out()
    pieces = staged_ref.at[0:PLANE - 1]
    arrive(None, functools.partial(remote, pieces, pieces, send_m, recv_m, sib_target))
    sent(pieces, send_m)
    mixed = jnp.concatenate([mixed_ref[p] for p in range(PLANE)], axis=1)
    tile = min(512, width)
    for at in range(0, width, tile):
        weight = go_ref[:, :, at:at + tile].reshape(width, tile)
        projected = jnp.dot(mixed, weight, preferred_element_type=f32)
        out_ref[:, at:at + tile] = (
            x_ref[:, at:at + tile].astype(f32) + projected
        ).astype(out_ref.dtype)
    drain(late + pending)


def fused(block, qkv_weight, out_weight, norm_gain, near):
    owners = lax.axis_size("owner")
    devices = lax.axis_size("region") * owners
    planes = owners // 4
    tokens, width = block.shape
    depth = qkv_weight.shape[0]
    share = 2 * HEAD_DIM
    bf16 = jnp.bfloat16
    vmem = pl.BlockSpec(memory_space=pltpu.VMEM)
    dma = pltpu.SemaphoreType.DMA
    return pl.pallas_call(
        functools.partial(fused_kernel, owners),
        out_shape=pltpu.VMEM(block.shape, block.dtype),
        in_specs=[pl.BlockSpec(memory_space=pl.ANY)] * 5,
        out_specs=vmem,
        scratch_shapes=[
            pltpu.VMEM(block.shape, bf16),
            pltpu.VMEM(qkv_weight.shape, bf16),
            pltpu.VMEM((PLANE, depth, 3 * share), bf16),
            pltpu.VMEM((devices * depth, 3 * share), bf16),
            pltpu.VMEM((2 * planes, 4 * depth, width), bf16),
            pltpu.VMEM((PLANE * tokens, width), bf16),
            pltpu.VMEM((16, share), bf16),
            pltpu.VMEM((PLANE, 16, share), bf16),
        ] + [pltpu.VMEM((PLANE * tokens, share), bf16)] * 2
        + [pltpu.VMEM((12 * tokens, share), bf16)] * 4
        + [pltpu.VMEM((2, 2 * tokens, 2 * share), bf16)] * 2
        + [pltpu.VMEM((PLANE, tokens, share), bf16)] * 2
        + [
            dma, dma((2,)), dma, dma,
            dma((2, planes - 1)), dma((planes, 2)), dma((planes,)),
            dma((4,)), dma((5, CHUNKS)), dma((3,)), dma((3, 2)), dma,
            dma((2,)), dma((2,)), dma, dma, dma((5,)),
            pltpu.VMEM(norm_gain.shape, norm_gain.dtype), pltpu.SMEM(near.shape, near.dtype),
        ],
        compiler_params=pltpu.CompilerParams(
            collective_id=0, has_side_effects=True, vmem_limit_bytes=54 * 1024 * 1024
        ),
        name="fused",
    )(block, qkv_weight, out_weight, norm_gain, near)


def attend_kernel(listed_ref, x_ref, xs_ref, gain_ref, bias_ref, wq_ref, wo_ref, out_ref,
                  normed_ref, q_ref, kv_ref, mixed_ref):
    tokens, width = x_ref.shape
    others = xs_ref.shape[0]
    gain = gain_ref[...]
    normed_ref[0:tokens, :] = layer_norm(x_ref[...], gain)

    @pl.loop(0, others)
    def _(slot):
        rows = pl.ds(pl.multiple_of((slot + 1) * tokens, tokens), tokens)
        block = xs_ref[slot].astype(jnp.float32)
        block = jnp.where(listed_ref[slot] > 0, block, 0.0)
        normed_ref[rows, :] = layer_norm(block, gain)

    tile = min(512, width)

    @pl.loop(0, width // tile)
    def _(step):
        cols = pl.ds(pl.multiple_of(step * tile, tile), tile)
        part = jnp.dot(normed_ref[0:tokens, :], wq_ref[:, cols], preferred_element_type=jnp.float32)
        q_ref[:, cols] = part.astype(jnp.bfloat16) * jnp.bfloat16(HEAD_DIM ** (-0.5))

    @pl.loop(0, 2 * width // tile)
    def _(step):
        cols = pl.ds(pl.multiple_of(step * tile, tile), tile)
        from_cols = pl.ds(pl.multiple_of(width + step * tile, tile), tile)
        kv_ref[:, cols] = jnp.dot(
            normed_ref[...], wq_ref[:, from_cols], preferred_element_type=jnp.float32
        ).astype(jnp.bfloat16)

    pair = 2 * HEAD_DIM
    low = lax.broadcasted_iota(jnp.int32, (tokens, pair), 1) < HEAD_DIM
    bias = bias_ref[...]

    @pl.loop(0, width // pair)
    def _(group):
        cols = pl.ds(pl.multiple_of(group * pair, pair), pair)
        value_cols = pl.ds(pl.multiple_of(width + group * pair, pair), pair)
        queries = q_ref[:, cols]
        keys = kv_ref[:, cols]
        values = kv_ref[:, value_cols]
        halves = []
        for mine in (low, jnp.logical_not(low)):
            query = jnp.where(mine, queries, jnp.zeros_like(queries))
            scores = lax.dot_general(
                query, keys, (((1,), (1,)), ((), ())), preferred_element_type=jnp.float32
            ) + bias
            shifted = jnp.exp(scores - jnp.max(scores, axis=-1, keepdims=True))
            total = jnp.sum(shifted, axis=-1, keepdims=True)
            mixed = jnp.dot(shifted.astype(jnp.bfloat16), values, preferred_element_type=jnp.float32)
            halves.append(mixed / total)
        mixed_ref[:, cols] = jnp.where(low, halves[0], halves[1]).astype(jnp.bfloat16)

    @pl.loop(0, width // tile)
    def _(step):
        cols = pl.ds(pl.multiple_of(step * tile, tile), tile)
        projected = jnp.dot(mixed_ref[...], wo_ref[:, cols], preferred_element_type=jnp.float32)
        out_ref[:, cols] = (x_ref[:, cols].astype(jnp.float32) + projected).astype(out_ref.dtype)


def attend(listed, block, others, norm_gain, bias, qkv_weight, out_weight):
    tokens, width = block.shape
    count = (others.shape[0] + 1) * tokens
    vmem = pl.BlockSpec(memory_space=pltpu.VMEM)
    return pl.pallas_call(
        attend_kernel,
        out_shape=jax.ShapeDtypeStruct(block.shape, block.dtype),
        in_specs=[pl.BlockSpec(memory_space=pltpu.SMEM)] + [vmem] * 6,
        out_specs=vmem,
        scratch_shapes=[
            pltpu.VMEM((count, width), jnp.bfloat16),
            pltpu.VMEM((tokens, width), jnp.bfloat16),
            pltpu.VMEM((count, 2 * width), jnp.bfloat16),
            pltpu.VMEM((tokens, width), jnp.bfloat16),
        ],
        compiler_params=pltpu.CompilerParams(vmem_limit_bytes=60 * 1024 * 1024),
        name="attend",
    )(listed, block, others, norm_gain, bias, qkv_weight, out_weight)


def shards(voxels, norm_gain, qkv_weight, out_weight, neighbours):
    block_size, model_width = voxels.shape[-2:]
    block = voxels.reshape(block_size, model_width)
    regions, owners = (lax.axis_size("region"), lax.axis_size("owner"))
    region, owner = (lax.axis_index("region"), lax.axis_index("owner"))
    share = 2 * HEAD_DIM
    together = regions == 2 and owners % 8 == 0 and model_width == PLANE * share
    together = together and block_size % (16 * CHUNKS) == 0 and voxels.shape[2] == 1
    if together:
        out = fused(block, qkv_weight, out_weight, norm_gain[None, :], neighbours.reshape(1, -1))
        return out.reshape(voxels.shape)
    wide = padded(voxels[:, :, 0], (("owner", 1), ("region", 0)), 1)
    wide = wide.reshape(-1, block_size, model_width)
    middle = wide.shape[0] // 2
    others = jnp.concatenate([wide[:middle], wide[middle + 1:]], axis=0)
    full_qkv = lax.all_gather(qkv_weight, ("region", "owner"), axis=0, tiled=True)
    full_out = lax.all_gather(out_weight, ("region", "owner"), axis=0, tiled=True)
    offsets = [(i, j) for i in (-1, 0, 1) for j in (-1, 0, 1) if i or j]
    numbers = []
    for up, along in offsets:
        inside = (owner + along >= 0) & (owner + along < owners)
        number = (region + up) * owners + owner + along
        numbers.append(jnp.where(inside & (number >= 0), number, -2))
    listed = jnp.any(neighbours.reshape(1, -1) == jnp.stack(numbers)[:, None], axis=1)
    present = jnp.concatenate([jnp.ones((1,), bool), listed])
    bias = jnp.repeat(jnp.where(present, 0.0, MASKED).astype(jnp.float32), block_size)[None, :]
    out = attend(
        listed.astype(jnp.int32), block, others, norm_gain[None, :], bias, full_qkv, full_out
    )
    return out.reshape(voxels.shape)


def solution(mesh):
    return jax.shard_map(
        shards,
        mesh=mesh,
        in_specs=(
            P("region", "owner", None, None, None),
            P(),
            P(("region", "owner"), None),
            P(("region", "owner"), None),
            P("region", "owner", None, None),
        ),
        out_specs=P("region", "owner", None, None, None),
        check_vma=False,
    )
```

```python
import functools

import jax
import jax.numpy as jnp
from jax import lax
from jax.experimental import pallas as pl
from jax.experimental.pallas import tpu as pltpu
from jax.sharding import PartitionSpec as P

HEAD_DIM = 64
MESH = pl.DeviceIdType.MESH
PLANE = 8
CHUNKS = 4
MASKED = -1e30
STEP_OWNERS = (2, 2, 1, 3, 3, 0, 1, 0)
STEP_REGIONS = (0, 1, 0, 0, 1, 0, 1, 1)


def padded(value, sides, width):
    for axis, dim in sides:
        devices, length = (lax.axis_size(axis), value.shape[dim])
        up = [(i, (i + 1) % devices) for i in range(devices - 1)]
        down = [(j, i) for i, j in up]
        last = lax.slice_in_dim(value, length - width, length, axis=dim)
        first = lax.slice_in_dim(value, 0, width, axis=dim)
        before = lax.ppermute(last, axis, up)
        after = lax.ppermute(first, axis, down)
        value = jnp.concatenate([before, value, after], axis=dim)
    return value


def layer_norm(inputs, norm_gain):
    widened = inputs.astype(jnp.float32)
    average = jnp.mean(widened, axis=-1, keepdims=True)
    spread = jnp.mean((widened - average) ** 2, axis=-1, keepdims=True)
    return ((widened - average) * lax.rsqrt(spread + 1e-06) * norm_gain).astype(jnp.bfloat16)


def fused_kernel(owners, x_hbm, wq_hbm, wo_hbm, gain_hbm, near_hbm, out_ref,
                 x_ref, wq_ref, cut_ref, w_ref, go_ref, blocks_ref, own_tab_ref, tabs_ref,
                 ql_ref, qh_ref, kl_ref, kh_ref, vl_ref, vh_ref,
                 edge_out_ref, edge_in_ref, staged_ref, mixed_ref,
                 send_w, recv_w, send_t, recv_t, send_z, recv_z, recv_l, send_b, recv_b,
                 send_o, recv_o, recv_s, send_e, recv_e, send_m, recv_m, local_sem, gain_ref, near_ref):
    tokens, width = x_ref.shape
    depth = wo_hbm.shape[0]
    share = 2 * HEAD_DIM
    planes = owners // 4
    region = lax.axis_index("region")
    owner = lax.axis_index("owner")
    core = lax.rem(owner, 2)
    row = lax.rem(owner // 2, 2)
    plane = owner // 4
    bf16, f32 = jnp.bfloat16, jnp.float32

    def place(r, y, c):
        return (2 * y + c) * 2 + r

    def device(r, z, y, c):
        return (r, z * 4 + y * 2 + c)

    me = place(region, row, core)
    mine = region * owners + owner
    peers = [
        (dr, dy, dc) for dr in (1, 0) for dy in (1, 0) for dc in (1, 0) if dr or dy or dc
    ]

    def flip(value, change):
        return 1 - value if change else value

    def moved(change):
        dr, dy, dc = change
        return flip(region, dr), flip(row, dy), flip(core, dc)

    def peer_device(change):
        r, y, c = moved(change)
        return device(r, plane, y, c)

    X, Y, SIB = (1, 0, 0), (0, 1, 0), (0, 0, 1)
    has_up = plane < planes - 1
    has_down = plane > 0
    above = device(region, plane + 1, row, core)
    below = device(region, plane - 1, row, core)

    def run(cond, fn):
        if cond is None:
            fn()
        else:
            pl.when(cond)(fn)

    def both(a, b):
        if a is None:
            return b
        return a if b is None else jnp.logical_and(a, b)

    shard_rows = pl.ds(pl.multiple_of(mine * depth, depth), depth)
    local = [
        pltpu.make_async_copy(wq_hbm, wq_ref, local_sem.at[0]),
        pltpu.make_async_copy(x_hbm, x_ref, local_sem.at[1]),
        pltpu.make_async_copy(
            wo_hbm,
            go_ref.at[region * planes + plane, pl.ds(
                pl.multiple_of((2 * row + core) * depth, depth), depth), :],
            local_sem.at[2],
        ),
    ]
    local.append(pltpu.make_async_copy(gain_hbm, gain_ref, local_sem.at[3]))
    local.append(pltpu.make_async_copy(near_hbm, near_ref, local_sem.at[4]))
    for copy in local:
        copy.start()
    barrier = pltpu.get_barrier_semaphore()

    def greet(target):
        pl.semaphore_signal(barrier, inc=1, device_id=target, device_id_type=MESH)

    for change in peers:
        greet(peer_device(change))
    run(has_up, lambda: greet(above))
    run(has_down, lambda: greet(below))

    local[0].wait()
    for p in range(PLANE):
        for part in range(3):
            at = part * width + p * share
            cut_ref[p, :, part * share:(part + 1) * share] = wq_ref[:, at:at + share]
    w_ref[shard_rows, :] = cut_ref[me]

    pl.semaphore_wait(
        barrier, len(peers) + has_up.astype(jnp.int32) + has_down.astype(jnp.int32)
    )

    pending = []
    sib_target = peer_device(SIB)

    def remote(src, dst, send_sem, recv_sem, target):
        return pltpu.make_async_remote_copy(
            src_ref=src, dst_ref=dst, send_sem=send_sem, recv_sem=recv_sem,
            device_id=target, device_id_type=MESH,
        )

    def start(cond, make):
        run(cond, lambda: make().start())

    def sent(ref, sem, cond=None, early=False):
        pending.append((cond, lambda: remote(ref, ref, sem, sem, sib_target).wait_send(), early))

    def arrive(cond, make):
        run(cond, lambda: make().wait_recv())

    for change in peers:
        to = place(*moved(change))
        start(None, functools.partial(
            remote, cut_ref.at[to], w_ref.at[shard_rows, :], send_w, recv_w.at[change[0]],
            peer_device(change)))
    sent(cut_ref.at[0:PLANE - 1], send_w, early=True)

    def wait_shards(flipped):
        count = sum(change[0] == flipped for change in peers)
        ref = cut_ref.at[0:count]
        arrive(None, functools.partial(
            remote, ref, ref, send_w, recv_w.at[flipped], sib_target))

    local[1].wait()
    local[3].wait()
    local[4].wait()
    own_rows = pl.ds(pl.multiple_of(me * tokens, tokens), tokens)
    blocks_ref[own_rows, :] = layer_norm(x_ref[...], gain_ref[...])
    entries, lanes = own_tab_ref.shape
    entry = lax.broadcasted_iota(jnp.int32, (entries, lanes), 0)
    lane = lax.broadcasted_iota(jnp.int32, (entries, lanes), 1)
    far_region = entry % 2
    far_owner = plane * 4 - 1 + entry // 2
    number = far_region * owners + far_owner
    listed = number == mine
    for k in range(near_ref.shape[1]):
        listed = jnp.logical_or(listed, number == near_ref[0, k])
    inside = jnp.logical_and(far_owner >= 0, far_owner < owners)
    listed = jnp.logical_and(listed, inside)
    marked = jnp.logical_or(lane == me, lane == me + HEAD_DIM)
    own_tab_ref[...] = jnp.where(
        jnp.logical_and(marked, jnp.logical_not(listed)), MASKED, 0.0
    ).astype(bf16)
    tabs_ref[me] = own_tab_ref[...]
    local[2].wait()

    for change in peers:
        start(None, functools.partial(
            remote, own_tab_ref, tabs_ref.at[me], send_t, recv_t, peer_device(change)))
    sent(tabs_ref.at[0:PLANE - 1], send_t, early=True)

    def wait_tables():
        ref = tabs_ref.at[0:PLANE - 1]
        arrive(None, functools.partial(remote, ref, ref, send_t, recv_t, sib_target))

    OWN, DIAGONAL = (0, 0, 0), (1, 1, 0)
    LINE, BY_X, BY_Y, BY_BOTH, BY_SIB = range(5)

    def slot(sems, source, to, piece):
        way = tuple(int(a != b) for a, b in zip(source, to))
        if way[2]:
            return sems.at[BY_SIB, way[0] + 2 * way[1]]
        return sems.at[way[0] + 2 * way[1], piece]

    def lane_of(to, source):
        if to != SIB:
            return 0 if to == X else 1
        return 2 if source in (OWN, X) else 3

    class Gather:
        def __init__(self, pieces, view, send, recv):
            self.pieces, self.view, self.send_sem, self.recv = pieces, view, send, recv
            self.first = list(range(pieces // 2))
            self.second = list(range(pieces // 2, pieces))

        def send(self, change, piece, source):
            ref = self.view(source, piece)
            start(None, functools.partial(
                remote, ref, ref, self.send_sem.at[lane_of(change, source)],
                slot(self.recv, source, change, piece), peer_device(change)))

        def wait(self, source, piece):
            ref = self.view(source, piece)
            arrive(None, functools.partial(
                remote, ref, ref, self.send_sem.at[0], slot(self.recv, source, OWN, piece),
                sib_target))

        def own(self, ks):
            for k in ks:
                self.send(X, (self.first + self.second)[k], (0, 0, 0))
                self.send(Y, (self.second + self.first)[k], (0, 0, 0))

        def own_sib(self):
            for piece in range(self.pieces):
                self.send(SIB, piece, (0, 0, 0))

        def direct(self, k):
            a, b = (self.first + self.second)[k], (self.second + self.first)[k]
            onward = k < self.pieces // 2
            self.wait(X, a)
            if onward:
                self.send(Y, a, X)
            self.send(SIB, a, X)
            self.wait(Y, b)
            if onward:
                self.send(X, b, Y)
            self.send(SIB, b, Y)

        def diagonal(self, k):
            for piece in (self.first[k], self.second[k]):
                self.wait((1, 1, 0), piece)
                self.send(SIB, piece, (1, 1, 0))

        def finish(self, sources):
            for source in sources:
                at = pl.multiple_of(place(*moved(source)) * tokens, tokens)
                ref = blocks_ref.at[pl.ds(at, tokens), :]
                arrive(None, functools.partial(
                    remote, ref, ref, self.send_sem.at[0], slot(self.recv, source, OWN, None),
                    sib_target))

    piece_rows = tokens // CHUNKS

    def block_piece(source, piece):
        at = place(*moved(source)) * tokens + piece * piece_rows
        return blocks_ref.at[pl.ds(pl.multiple_of(at, piece_rows), piece_rows), :]

    blocks = Gather(CHUNKS, block_piece, send_b, recv_b)
    for way, count in ((0, 3), (1, 3), (2, 4), (3, 4)):
        sent(blocks_ref.at[0:count * tokens // 2, :], send_b.at[way])

    def line(d):
        return [(plane - d, plane - d >= 0), (plane + d, plane + d < planes)]

    def w_half(z, r):
        at = (r * owners + z * 4) * depth
        return w_ref.at[pl.ds(pl.multiple_of(at, 4 * depth), 4 * depth), :]

    def send_w_half(z, r, up, cond, d):
        ref = w_half(z, r)
        start(both(cond, has_up if up else has_down), functools.partial(
            remote, ref, ref, send_z.at[int(up), d], recv_z.at[z, r], above if up else below))

    def wait_w_half(z, r, cond):
        ref = w_half(z, r)
        arrive(cond, functools.partial(
            remote, ref, ref, send_z.at[0, 0], recv_z.at[z, r], sib_target))

    for d in range(planes - 1):
        for up, cond in ((1, plane - d >= 0), (0, plane + d < planes)):
            cond = jnp.logical_and(cond, has_up if up else has_down)
            sent(go_ref.at[0], send_z.at[up, d], cond, early=True)

    def own_w():
        for flipped in (0, 1):
            wait_shards(flipped)
            for up in (True, False):
                send_w_half(plane, flip(region, flipped), up, None, 0)

    def relay_w(d):
        for flipped in (0, 1):
            for (z, cond), up in zip(line(d), (True, False)):
                wait_w_half(z, flip(region, flipped), cond)
                if d < planes - 1:
                    send_w_half(z, flip(region, flipped), up, cond, d)

    near_planes = planes // 2

    def out_piece(source, first, count, half=None):
        r, y, c = moved(source)
        at, size = (2 * y + c) * depth, depth
        if half is not None:
            size = depth // 2
            at = at + half * size
        return go_ref.at[
            pl.ds(r * planes + first, count), pl.ds(pl.multiple_of(at, size), size), :]

    def line_out(z, up, cond, d):
        ref = out_piece(OWN, z, 1)
        start(both(cond, has_up if up else has_down), functools.partial(
            remote, ref, ref, send_z.at[int(up), d], recv_l.at[z], above if up else below))

    def own_out():
        for up in (True, False):
            line_out(plane, up, None, 0)

    def relay_out(d):
        for (z, cond), up in zip(line(d), (True, False)):
            ref = out_piece(OWN, z, 1)
            arrive(cond, functools.partial(
                remote, ref, ref, send_o.at[0], recv_l.at[z], sib_target))
            if d < planes - 1:
                line_out(z, up, cond, d)

    def ring(d):
        return [(plane, None)] if d == 0 else line(d)

    def spread_out(d):
        for z, cond in ring(d):
            ref = out_piece(OWN, z, 1)
            for way, to in ((0, X), (1, Y)):
                start(cond, functools.partial(
                    remote, ref, ref, send_o.at[way], recv_o.at[way, z // near_planes],
                    peer_device(to)))

    def to_sibling(source, first, count):
        ref = out_piece(source, first, count)
        remote(ref, ref, send_o.at[2], recv_s, sib_target).start()

    def wait_group(way, group):
        ref = out_piece(OWN, group * near_planes, near_planes)
        arrive(None, functools.partial(
            remote, ref, ref, send_o.at[0], recv_o.at[way, group], sib_target))

    def onward_out(group):
        for way, source, to in ((0, X, Y), (1, Y, X)):
            wait_group(way, group)
            ref = out_piece(source, group * near_planes, near_planes, way)
            remote(
                ref, ref, send_o.at[1 - way], recv_o.at[2, group], peer_device(to)).start()
            to_sibling(source, group * near_planes, near_planes)

    def diagonal_out(group):
        wait_group(2, group)
        to_sibling(DIAGONAL, group * near_planes, near_planes)

    def finish_out():
        ref = go_ref.at[0:planes]
        arrive(None, functools.partial(remote, ref, ref, send_o.at[2], recv_s, sib_target))

    pair_rows = 2 * tokens
    low = lax.broadcasted_iota(jnp.int32, (tokens, share), 1) < HEAD_DIM
    at_lane = lax.broadcasted_iota(jnp.int32, (tokens, share), 1)
    ones = jnp.ones((tokens, share), bf16)

    def keep_keys(slot, keys, values):
        table = tabs_ref[0].astype(f32)
        for p in range(1, PLANE):
            table = table + tabs_ref[p].astype(f32)
        which = lax.broadcasted_iota(jnp.int32, table.shape, 0)
        for r in (0, 1):
            absent = jnp.sum(
                jnp.where(which == slot * 2 + r, table, 0.0), axis=0, keepdims=True
            )
            absent = jnp.broadcast_to(absent, (tokens, share)).astype(bf16)
            rows = pl.ds(pl.multiple_of(slot * pair_rows + r * tokens, tokens), tokens)
            part = slice(r * tokens, (r + 1) * tokens)
            kl_ref[rows, :] = jnp.where(low, keys[part], absent)
            kh_ref[rows, :] = jnp.where(low, absent, keys[part])
            vl_ref[rows, :] = jnp.where(low, values[part], ones)
            vh_ref[rows, :] = jnp.where(low, ones, values[part])

    def project_step(i):
        late = i // 2
        a = i + late * (1 - 2 * (i % 2))
        project(a + row * (3 - 2 * a), row + late * (1 - 2 * row), i % 2 == 0)

    def project(j, edge, at_edge):
        rows = pl.ds(pl.multiple_of(j * pair_rows, pair_rows), pair_rows)
        part = jnp.dot(blocks_ref[rows, :], w_ref[...], preferred_element_type=f32).astype(bf16)
        queries = part[:, 0:share] * bf16(HEAD_DIM ** (-0.5))
        keys, values = part[:, share:2 * share], part[:, 2 * share:]

        @pl.when(at_edge)
        def _():
            edge_out_ref[edge, :, 0:share] = keys
            edge_out_ref[edge, :, share:] = values
            send_edge(edge)

        for r in (0, 1):
            q = 2 * j + r
            q_rows = pl.ds(pl.multiple_of(q * tokens, tokens), tokens)
            mark_low = jnp.where(at_lane == q, 1.0, 0.0).astype(bf16)
            mark_high = jnp.where(at_lane == q + HEAD_DIM, 1.0, 0.0).astype(bf16)
            piece = queries[r * tokens:(r + 1) * tokens]
            ql_ref[q_rows, :] = jnp.where(low, piece, mark_high)
            qh_ref[q_rows, :] = jnp.where(low, mark_low, piece)
        keep_keys(j + 1, keys, values)

    def send_edge(e):
        z = plane + 2 * e - 1

        @pl.when(jnp.logical_and(z >= 0, z < planes))
        def _():
            remote(
                edge_out_ref.at[e], edge_in_ref.at[1 - e], send_e.at[e], recv_e.at[1 - e],
                device(region, z, row, core)).start()

    sent(edge_out_ref.at[0], send_e.at[0], has_down)
    sent(edge_out_ref.at[1], send_e.at[1], has_up)

    def take_edge(e):
        z = plane + 2 * e - 1
        there = jnp.logical_and(z >= 0, z < planes)
        arrive(there, functools.partial(
            remote, edge_in_ref.at[e], edge_in_ref.at[e], send_e.at[e], recv_e.at[e], sib_target))

        @pl.when(jnp.logical_not(there))
        def _():
            edge_in_ref[e] = jnp.zeros(edge_in_ref.shape[1:], bf16)

        keep_keys(e * 5, edge_in_ref[e, :, 0:share], edge_in_ref[e, :, share:])

    def digit(numbers, base, i):
        packed = sum(n << (base * k) for k, n in enumerate(numbers))
        return lax.rem(lax.shift_right_logical(i * 0 + packed, i * base), 1 << base)

    def order(i):
        a = digit(STEP_OWNERS, 2, i)
        same = digit(STEP_REGIONS, 1, i)
        return a + row * (3 - 2 * a), same * region + (1 - same) * (1 - region)

    def hand_over(i, out):
        j, r = order(i)
        q = 2 * j + r
        staged_ref[i] = out

        @pl.when(q == me)
        def _():
            mixed_ref[me] = out

        @pl.when(q != me)
        def _():
            remote(
                staged_ref.at[i], mixed_ref.at[me], send_m, recv_m,
                device(r, plane, j // 2, j % 2)).start()

    def attend_rows(j, start_row, count):
        rows = pl.ds(pl.multiple_of(start_row, count), count)
        keys = pl.ds(pl.multiple_of(j * pair_rows, pair_rows), 3 * pair_rows)
        heads = ((ql_ref, kl_ref, vl_ref), (qh_ref, kh_ref, vh_ref))
        scores = [
            lax.dot_general(
                q_ref[rows, :], k_ref[keys, :], (((1,), (1,)), ((), ())),
                preferred_element_type=f32,
            )
            for q_ref, k_ref, _ in heads
        ]
        mixes = []
        for score, (_, _, v_ref) in zip(scores, heads):
            shifted = jnp.exp(score - jnp.max(score, axis=-1, keepdims=True)).astype(bf16)
            mixes.append(jnp.dot(shifted, v_ref[keys, :], preferred_element_type=f32))
        lower = lax.broadcasted_iota(jnp.int32, (count, share), 1) < HEAD_DIM
        total = pltpu.roll(jnp.where(lower, mixes[1], mixes[0]), HEAD_DIM, 1)
        return (jnp.where(lower, mixes[0], mixes[1]) / total).astype(bf16)

    def attend_block(i):
        j, r = order(i)
        hand_over(i, attend_rows(j, j * pair_rows + r * tokens, tokens))

    blocks.own(range(CHUNKS))
    blocks.own_sib()
    own_w()
    own_out()
    blocks.direct(0)
    relay_w(1)
    relay_out(1)
    blocks.direct(1)
    spread_out(0)
    spread_out(1)
    relay_w(2)
    relay_out(2)
    spread_out(2)
    blocks.direct(2)
    blocks.direct(3)
    relay_w(planes - 1)
    wait_tables()
    blocks.finish([SIB, (1, 0, 1)])

    def drain(sends):
        for cond, wait, _ in sends:
            run(cond, wait)

    early = [entry for entry in pending if entry[2]]
    late = [entry for entry in pending if not entry[2]]
    pending.clear()

    def projections(i, carry):
        @pl.when(i == 2)
        def _():
            blocks.diagonal(0)
            drain(early)
            blocks.diagonal(1)
            blocks.finish([(0, 1, 1), (1, 1, 1)])

        project_step(i)
        return carry

    lax.fori_loop(0, PLANE // 2, projections, 0)
    relay_out(planes - 1)
    spread_out(planes - 1)
    to_sibling(OWN, 0, planes)
    for way in (0, 1):
        sent(go_ref.at[pl.ds(0, planes * 3 // 4), 0:2 * depth, :], send_o.at[way])
    sent(go_ref.at[0:planes], send_o.at[2])
    near = plane // near_planes

    HOOKS = {
        2: [lambda: onward_out(near)],
        3: [lambda: take_edge(1 - row)],
        4: [lambda: onward_out(1 - near)],
        5: [lambda: take_edge(row)],
    }

    def attention(i, carry):
        for at, hooks in HOOKS.items():
            @pl.when(i == at)
            def _():
                for hook in hooks:
                    hook()

        attend_block(i)
        return carry

    lax.fori_loop(0, PLANE, attention, 0)
    diagonal_out(near)
    diagonal_out(1 - near)
    finish_out()
    pieces = staged_ref.at[0:PLANE - 1]
    arrive(None, functools.partial(remote, pieces, pieces, send_m, recv_m, sib_target))
    sent(pieces, send_m)
    mixed = jnp.concatenate([mixed_ref[p] for p in range(PLANE)], axis=1)
    tile = min(512, width)
    for at in range(0, width, tile):
        weight = go_ref[:, :, at:at + tile].reshape(width, tile)
        projected = jnp.dot(mixed, weight, preferred_element_type=f32)
        out_ref[:, at:at + tile] = (
            x_ref[:, at:at + tile].astype(f32) + projected
        ).astype(out_ref.dtype)
    drain(late + pending)


def fused(block, qkv_weight, out_weight, norm_gain, near):
    owners = lax.axis_size("owner")
    devices = lax.axis_size("region") * owners
    planes = owners // 4
    tokens, width = block.shape
    depth = qkv_weight.shape[0]
    share = 2 * HEAD_DIM
    bf16 = jnp.bfloat16
    vmem = pl.BlockSpec(memory_space=pltpu.VMEM)
    dma = pltpu.SemaphoreType.DMA
    return pl.pallas_call(
        functools.partial(fused_kernel, owners),
        out_shape=pltpu.VMEM(block.shape, block.dtype),
        in_specs=[pl.BlockSpec(memory_space=pl.ANY)] * 5,
        out_specs=vmem,
        scratch_shapes=[
            pltpu.VMEM(block.shape, bf16),
            pltpu.VMEM(qkv_weight.shape, bf16),
            pltpu.VMEM((PLANE, depth, 3 * share), bf16),
            pltpu.VMEM((devices * depth, 3 * share), bf16),
            pltpu.VMEM((2 * planes, 4 * depth, width), bf16),
            pltpu.VMEM((PLANE * tokens, width), bf16),
            pltpu.VMEM((16, share), bf16),
            pltpu.VMEM((PLANE, 16, share), bf16),
        ] + [pltpu.VMEM((PLANE * tokens, share), bf16)] * 2
        + [pltpu.VMEM((12 * tokens, share), bf16)] * 4
        + [pltpu.VMEM((2, 2 * tokens, 2 * share), bf16)] * 2
        + [pltpu.VMEM((PLANE, tokens, share), bf16)] * 2
        + [
            dma, dma((2,)), dma, dma,
            dma((2, planes - 1)), dma((planes, 2)), dma((planes,)),
            dma((4,)), dma((5, CHUNKS)), dma((3,)), dma((3, 2)), dma,
            dma((2,)), dma((2,)), dma, dma, dma((5,)),
            pltpu.VMEM(norm_gain.shape, norm_gain.dtype), pltpu.SMEM(near.shape, near.dtype),
        ],
        compiler_params=pltpu.CompilerParams(
            collective_id=0, has_side_effects=True, vmem_limit_bytes=54 * 1024 * 1024
        ),
        name="fused",
    )(block, qkv_weight, out_weight, norm_gain, near)


def attend_kernel(listed_ref, x_ref, xs_ref, gain_ref, bias_ref, wq_ref, wo_ref, out_ref,
                  normed_ref, q_ref, kv_ref, mixed_ref):
    tokens, width = x_ref.shape
    others = xs_ref.shape[0]
    gain = gain_ref[...]
    normed_ref[0:tokens, :] = layer_norm(x_ref[...], gain)

    @pl.loop(0, others)
    def _(slot):
        rows = pl.ds(pl.multiple_of((slot + 1) * tokens, tokens), tokens)
        block = xs_ref[slot].astype(jnp.float32)
        block = jnp.where(listed_ref[slot] > 0, block, 0.0)
        normed_ref[rows, :] = layer_norm(block, gain)

    tile = min(512, width)

    @pl.loop(0, width // tile)
    def _(step):
        cols = pl.ds(pl.multiple_of(step * tile, tile), tile)
        part = jnp.dot(normed_ref[0:tokens, :], wq_ref[:, cols], preferred_element_type=jnp.float32)
        q_ref[:, cols] = part.astype(jnp.bfloat16) * jnp.bfloat16(HEAD_DIM ** (-0.5))

    @pl.loop(0, 2 * width // tile)
    def _(step):
        cols = pl.ds(pl.multiple_of(step * tile, tile), tile)
        from_cols = pl.ds(pl.multiple_of(width + step * tile, tile), tile)
        kv_ref[:, cols] = jnp.dot(
            normed_ref[...], wq_ref[:, from_cols], preferred_element_type=jnp.float32
        ).astype(jnp.bfloat16)

    pair = 2 * HEAD_DIM
    low = lax.broadcasted_iota(jnp.int32, (tokens, pair), 1) < HEAD_DIM
    bias = bias_ref[...]

    @pl.loop(0, width // pair)
    def _(group):
        cols = pl.ds(pl.multiple_of(group * pair, pair), pair)
        value_cols = pl.ds(pl.multiple_of(width + group * pair, pair), pair)
        queries = q_ref[:, cols]
        keys = kv_ref[:, cols]
        values = kv_ref[:, value_cols]
        halves = []
        for mine in (low, jnp.logical_not(low)):
            query = jnp.where(mine, queries, jnp.zeros_like(queries))
            scores = lax.dot_general(
                query, keys, (((1,), (1,)), ((), ())), preferred_element_type=jnp.float32
            ) + bias
            shifted = jnp.exp(scores - jnp.max(scores, axis=-1, keepdims=True))
            total = jnp.sum(shifted, axis=-1, keepdims=True)
            mixed = jnp.dot(shifted.astype(jnp.bfloat16), values, preferred_element_type=jnp.float32)
            halves.append(mixed / total)
        mixed_ref[:, cols] = jnp.where(low, halves[0], halves[1]).astype(jnp.bfloat16)

    @pl.loop(0, width // tile)
    def _(step):
        cols = pl.ds(pl.multiple_of(step * tile, tile), tile)
        projected = jnp.dot(mixed_ref[...], wo_ref[:, cols], preferred_element_type=jnp.float32)
        out_ref[:, cols] = (x_ref[:, cols].astype(jnp.float32) + projected).astype(out_ref.dtype)


def attend(listed, block, others, norm_gain, bias, qkv_weight, out_weight):
    tokens, width = block.shape
    count = (others.shape[0] + 1) * tokens
    vmem = pl.BlockSpec(memory_space=pltpu.VMEM)
    return pl.pallas_call(
        attend_kernel,
        out_shape=jax.ShapeDtypeStruct(block.shape, block.dtype),
        in_specs=[pl.BlockSpec(memory_space=pltpu.SMEM)] + [vmem] * 6,
        out_specs=vmem,
        scratch_shapes=[
            pltpu.VMEM((count, width), jnp.bfloat16),
            pltpu.VMEM((tokens, width), jnp.bfloat16),
            pltpu.VMEM((count, 2 * width), jnp.bfloat16),
            pltpu.VMEM((tokens, width), jnp.bfloat16),
        ],
        compiler_params=pltpu.CompilerParams(vmem_limit_bytes=60 * 1024 * 1024),
        name="attend",
    )(listed, block, others, norm_gain, bias, qkv_weight, out_weight)


def shards(voxels, norm_gain, qkv_weight, out_weight, neighbours):
    block_size, model_width = voxels.shape[-2:]
    block = voxels.reshape(block_size, model_width)
    regions, owners = (lax.axis_size("region"), lax.axis_size("owner"))
    region, owner = (lax.axis_index("region"), lax.axis_index("owner"))
    share = 2 * HEAD_DIM
    together = regions == 2 and owners % 8 == 0 and model_width == PLANE * share
    together = together and block_size % (16 * CHUNKS) == 0 and voxels.shape[2] == 1
    if together:
        out = fused(block, qkv_weight, out_weight, norm_gain[None, :], neighbours.reshape(1, -1))
        return out.reshape(voxels.shape)
    wide = padded(voxels[:, :, 0], (("owner", 1), ("region", 0)), 1)
    wide = wide.reshape(-1, block_size, model_width)
    middle = wide.shape[0] // 2
    others = jnp.concatenate([wide[:middle], wide[middle + 1:]], axis=0)
    full_qkv = lax.all_gather(qkv_weight, ("region", "owner"), axis=0, tiled=True)
    full_out = lax.all_gather(out_weight, ("region", "owner"), axis=0, tiled=True)
    offsets = [(i, j) for i in (-1, 0, 1) for j in (-1, 0, 1) if i or j]
    numbers = []
    for up, along in offsets:
        inside = (owner + along >= 0) & (owner + along < owners)
        number = (region + up) * owners + owner + along
        numbers.append(jnp.where(inside & (number >= 0), number, -2))
    listed = jnp.any(neighbours.reshape(1, -1) == jnp.stack(numbers)[:, None], axis=1)
    present = jnp.concatenate([jnp.ones((1,), bool), listed])
    bias = jnp.repeat(jnp.where(present, 0.0, MASKED).astype(jnp.float32), block_size)[None, :]
    out = attend(
        listed.astype(jnp.int32), block, others, norm_gain[None, :], bias, full_qkv, full_out
    )
    return out.reshape(voxels.shape)


def solution(mesh):
    return jax.shard_map(
        shards,
        mesh=mesh,
        in_specs=(
            P("region", "owner", None, None, None),
            P(),
            P(("region", "owner"), None),
            P(("region", "owner"), None),
            P("region", "owner", None, None),
        ),
        out_specs=P("region", "owner", None, None, None),
        check_vma=False,
    )
```

```python
import functools

import jax
import jax.numpy as jnp
from jax import lax
from jax.experimental import pallas as pl
from jax.experimental.pallas import tpu as pltpu
from jax.sharding import PartitionSpec as P

HEAD_DIM = 64
MESH = pl.DeviceIdType.MESH
PLANE = 8
CHUNKS = 4
MASKED = -1e30
STEP_OWNERS = (2, 2, 1, 3, 3, 0, 1, 0)
STEP_REGIONS = (0, 1, 0, 0, 1, 0, 1, 1)


def padded(value, sides, width):
    for axis, dim in sides:
        devices, length = (lax.axis_size(axis), value.shape[dim])
        up = [(i, (i + 1) % devices) for i in range(devices - 1)]
        down = [(j, i) for i, j in up]
        last = lax.slice_in_dim(value, length - width, length, axis=dim)
        first = lax.slice_in_dim(value, 0, width, axis=dim)
        before = lax.ppermute(last, axis, up)
        after = lax.ppermute(first, axis, down)
        value = jnp.concatenate([before, value, after], axis=dim)
    return value


def layer_norm(inputs, norm_gain):
    widened = inputs.astype(jnp.float32)
    average = jnp.mean(widened, axis=-1, keepdims=True)
    spread = jnp.mean((widened - average) ** 2, axis=-1, keepdims=True)
    return ((widened - average) * lax.rsqrt(spread + 1e-06) * norm_gain).astype(jnp.bfloat16)


def fused_kernel(owners, x_hbm, wq_hbm, wo_hbm, gain_hbm, near_hbm, out_ref,
                 x_ref, wq_ref, cut_ref, w_ref, go_ref, blocks_ref, own_tab_ref, tabs_ref,
                 ql_ref, qh_ref, kl_ref, kh_ref, vl_ref, vh_ref,
                 edge_out_ref, edge_in_ref, staged_ref, mixed_ref,
                 send_w, recv_w, send_t, recv_t, send_z, recv_z, recv_l, send_b, recv_b,
                 send_o, recv_o, recv_s, send_e, recv_e, send_m, recv_m, local_sem, gain_ref, near_ref):
    tokens, width = x_ref.shape
    depth = wo_hbm.shape[0]
    share = 2 * HEAD_DIM
    planes = owners // 4
    region = lax.axis_index("region")
    owner = lax.axis_index("owner")
    core = lax.rem(owner, 2)
    row = lax.rem(owner // 2, 2)
    plane = owner // 4
    bf16, f32 = jnp.bfloat16, jnp.float32

    def place(r, y, c):
        return (2 * y + c) * 2 + r

    def device(r, z, y, c):
        return (r, z * 4 + y * 2 + c)

    me = place(region, row, core)
    mine = region * owners + owner
    peers = [
        (dr, dy, dc) for dr in (1, 0) for dy in (1, 0) for dc in (1, 0) if dr or dy or dc
    ]

    def flip(value, change):
        return 1 - value if change else value

    def moved(change):
        dr, dy, dc = change
        return flip(region, dr), flip(row, dy), flip(core, dc)

    def peer_device(change):
        r, y, c = moved(change)
        return device(r, plane, y, c)

    X, Y, SIB = (1, 0, 0), (0, 1, 0), (0, 0, 1)
    has_up = plane < planes - 1
    has_down = plane > 0
    above = device(region, plane + 1, row, core)
    below = device(region, plane - 1, row, core)

    def run(cond, fn):
        if cond is None:
            fn()
        else:
            pl.when(cond)(fn)

    def both(a, b):
        if a is None:
            return b
        return a if b is None else jnp.logical_and(a, b)

    shard_rows = pl.ds(pl.multiple_of(mine * depth, depth), depth)
    local = [
        pltpu.make_async_copy(wq_hbm, wq_ref, local_sem.at[0]),
        pltpu.make_async_copy(x_hbm, x_ref, local_sem.at[1]),
        pltpu.make_async_copy(
            wo_hbm,
            go_ref.at[region * planes + plane, pl.ds(
                pl.multiple_of((2 * row + core) * depth, depth), depth), :],
            local_sem.at[2],
        ),
    ]
    local.append(pltpu.make_async_copy(gain_hbm, gain_ref, local_sem.at[3]))
    local.append(pltpu.make_async_copy(near_hbm, near_ref, local_sem.at[4]))
    for copy in local:
        copy.start()
    barrier = pltpu.get_barrier_semaphore()

    def greet(target):
        pl.semaphore_signal(barrier, inc=1, device_id=target, device_id_type=MESH)

    for change in peers:
        greet(peer_device(change))
    run(has_up, lambda: greet(above))
    run(has_down, lambda: greet(below))

    local[0].wait()
    for p in range(PLANE):
        for part in range(3):
            at = part * width + p * share
            cut_ref[p, :, part * share:(part + 1) * share] = wq_ref[:, at:at + share]
    w_ref[shard_rows, :] = cut_ref[me]

    pl.semaphore_wait(
        barrier, len(peers) + has_up.astype(jnp.int32) + has_down.astype(jnp.int32)
    )

    pending = []
    sib_target = peer_device(SIB)

    def remote(src, dst, send_sem, recv_sem, target):
        return pltpu.make_async_remote_copy(
            src_ref=src, dst_ref=dst, send_sem=send_sem, recv_sem=recv_sem,
            device_id=target, device_id_type=MESH,
        )

    def start(cond, make):
        run(cond, lambda: make().start())

    def sent(ref, sem, cond=None, early=False):
        pending.append((cond, lambda: remote(ref, ref, sem, sem, sib_target).wait_send(), early))

    def arrive(cond, make):
        run(cond, lambda: make().wait_recv())

    for change in peers:
        to = place(*moved(change))
        start(None, functools.partial(
            remote, cut_ref.at[to], w_ref.at[shard_rows, :], send_w, recv_w.at[change[0]],
            peer_device(change)))
    sent(cut_ref.at[0:PLANE - 1], send_w, early=True)

    def wait_shards(flipped):
        count = sum(change[0] == flipped for change in peers)
        ref = cut_ref.at[0:count]
        arrive(None, functools.partial(
            remote, ref, ref, send_w, recv_w.at[flipped], sib_target))

    local[1].wait()
    local[3].wait()
    local[4].wait()
    own_rows = pl.ds(pl.multiple_of(me * tokens, tokens), tokens)
    blocks_ref[own_rows, :] = layer_norm(x_ref[...], gain_ref[...])
    entries, lanes = own_tab_ref.shape
    entry = lax.broadcasted_iota(jnp.int32, (entries, lanes), 0)
    lane = lax.broadcasted_iota(jnp.int32, (entries, lanes), 1)
    far_region = entry % 2
    far_owner = plane * 4 - 1 + entry // 2
    number = far_region * owners + far_owner
    listed = number == mine
    for k in range(near_ref.shape[1]):
        listed = jnp.logical_or(listed, number == near_ref[0, k])
    inside = jnp.logical_and(far_owner >= 0, far_owner < owners)
    listed = jnp.logical_and(listed, inside)
    marked = jnp.logical_or(lane == me, lane == me + HEAD_DIM)
    own_tab_ref[...] = jnp.where(
        jnp.logical_and(marked, jnp.logical_not(listed)), MASKED, 0.0
    ).astype(bf16)
    tabs_ref[me] = own_tab_ref[...]
    local[2].wait()

    for change in peers:
        start(None, functools.partial(
            remote, own_tab_ref, tabs_ref.at[me], send_t, recv_t, peer_device(change)))
    sent(tabs_ref.at[0:PLANE - 1], send_t, early=True)

    def wait_tables():
        ref = tabs_ref.at[0:PLANE - 1]
        arrive(None, functools.partial(remote, ref, ref, send_t, recv_t, sib_target))

    OWN, DIAGONAL = (0, 0, 0), (1, 1, 0)
    LINE, BY_X, BY_Y, BY_BOTH, BY_SIB = range(5)

    def slot(sems, source, to, piece):
        way = tuple(int(a != b) for a, b in zip(source, to))
        if way[2]:
            return sems.at[BY_SIB, way[0] + 2 * way[1]]
        return sems.at[way[0] + 2 * way[1], piece]

    def lane_of(to, source):
        if to != SIB:
            return 0 if to == X else 1
        return 2 if source in (OWN, X) else 3

    class Gather:
        def __init__(self, pieces, view, send, recv):
            self.pieces, self.view, self.send_sem, self.recv = pieces, view, send, recv
            self.first = list(range(pieces // 2))
            self.second = list(range(pieces // 2, pieces))

        def send(self, change, piece, source):
            ref = self.view(source, piece)
            start(None, functools.partial(
                remote, ref, ref, self.send_sem.at[lane_of(change, source)],
                slot(self.recv, source, change, piece), peer_device(change)))

        def wait(self, source, piece):
            ref = self.view(source, piece)
            arrive(None, functools.partial(
                remote, ref, ref, self.send_sem.at[0], slot(self.recv, source, OWN, piece),
                sib_target))

        def own(self, ks):
            for k in ks:
                self.send(X, (self.first + self.second)[k], (0, 0, 0))
                self.send(Y, (self.second + self.first)[k], (0, 0, 0))

        def own_sib(self):
            for piece in range(self.pieces):
                self.send(SIB, piece, (0, 0, 0))

        def direct(self, k):
            a, b = (self.first + self.second)[k], (self.second + self.first)[k]
            onward = k < self.pieces // 2
            self.wait(X, a)
            if onward:
                self.send(Y, a, X)
            self.send(SIB, a, X)
            self.wait(Y, b)
            if onward:
                self.send(X, b, Y)
            self.send(SIB, b, Y)

        def diagonal(self, k):
            for piece in (self.first[k], self.second[k]):
                self.wait((1, 1, 0), piece)
                self.send(SIB, piece, (1, 1, 0))

        def finish(self, sources):
            for source in sources:
                at = pl.multiple_of(place(*moved(source)) * tokens, tokens)
                ref = blocks_ref.at[pl.ds(at, tokens), :]
                arrive(None, functools.partial(
                    remote, ref, ref, self.send_sem.at[0], slot(self.recv, source, OWN, None),
                    sib_target))

    piece_rows = tokens // CHUNKS

    def block_piece(source, piece):
        at = place(*moved(source)) * tokens + piece * piece_rows
        return blocks_ref.at[pl.ds(pl.multiple_of(at, piece_rows), piece_rows), :]

    blocks = Gather(CHUNKS, block_piece, send_b, recv_b)
    for way, count in ((0, 3), (1, 3), (2, 4), (3, 4)):
        sent(blocks_ref.at[0:count * tokens // 2, :], send_b.at[way])

    def line(d):
        return [(plane - d, plane - d >= 0), (plane + d, plane + d < planes)]

    def w_half(z, r):
        at = (r * owners + z * 4) * depth
        return w_ref.at[pl.ds(pl.multiple_of(at, 4 * depth), 4 * depth), :]

    def send_w_half(z, r, up, cond, d):
        ref = w_half(z, r)
        start(both(cond, has_up if up else has_down), functools.partial(
            remote, ref, ref, send_z.at[int(up), d], recv_z.at[z, r], above if up else below))

    def wait_w_half(z, r, cond):
        ref = w_half(z, r)
        arrive(cond, functools.partial(
            remote, ref, ref, send_z.at[0, 0], recv_z.at[z, r], sib_target))

    for d in range(planes - 1):
        for up, cond in ((1, plane - d >= 0), (0, plane + d < planes)):
            cond = jnp.logical_and(cond, has_up if up else has_down)
            sent(go_ref.at[0], send_z.at[up, d], cond, early=True)

    def own_w():
        for flipped in (0, 1):
            wait_shards(flipped)
            for up in (True, False):
                send_w_half(plane, flip(region, flipped), up, None, 0)

    def relay_w(d):
        for flipped in (0, 1):
            for (z, cond), up in zip(line(d), (True, False)):
                wait_w_half(z, flip(region, flipped), cond)
                if d < planes - 1:
                    send_w_half(z, flip(region, flipped), up, cond, d)

    near_planes = planes // 2

    def out_piece(source, first, count, half=None):
        r, y, c = moved(source)
        at, size = (2 * y + c) * depth, depth
        if half is not None:
            size = depth // 2
            at = at + half * size
        return go_ref.at[
            pl.ds(r * planes + first, count), pl.ds(pl.multiple_of(at, size), size), :]

    def line_out(z, up, cond, d):
        ref = out_piece(OWN, z, 1)
        start(both(cond, has_up if up else has_down), functools.partial(
            remote, ref, ref, send_z.at[int(up), d], recv_l.at[z], above if up else below))

    def own_out():
        for up in (True, False):
            line_out(plane, up, None, 0)

    def relay_out(d):
        for (z, cond), up in zip(line(d), (True, False)):
            ref = out_piece(OWN, z, 1)
            arrive(cond, functools.partial(
                remote, ref, ref, send_o.at[0], recv_l.at[z], sib_target))
            if d < planes - 1:
                line_out(z, up, cond, d)

    def ring(d):
        return [(plane, None)] if d == 0 else line(d)

    def spread_out(d):
        for z, cond in ring(d):
            ref = out_piece(OWN, z, 1)
            for way, to in ((0, X), (1, Y)):
                start(cond, functools.partial(
                    remote, ref, ref, send_o.at[way], recv_o.at[way, z // near_planes],
                    peer_device(to)))

    def to_sibling(source, first, count):
        ref = out_piece(source, first, count)
        remote(ref, ref, send_o.at[2], recv_s, sib_target).start()

    def wait_group(way, group):
        ref = out_piece(OWN, group * near_planes, near_planes)
        arrive(None, functools.partial(
            remote, ref, ref, send_o.at[0], recv_o.at[way, group], sib_target))

    def onward_out(group):
        for way, source, to in ((0, X, Y), (1, Y, X)):
            wait_group(way, group)
            ref = out_piece(source, group * near_planes, near_planes, way)
            remote(
                ref, ref, send_o.at[1 - way], recv_o.at[2, group], peer_device(to)).start()
            to_sibling(source, group * near_planes, near_planes)

    def diagonal_out(group):
        wait_group(2, group)
        to_sibling(DIAGONAL, group * near_planes, near_planes)

    def finish_out():
        ref = go_ref.at[0:planes]
        arrive(None, functools.partial(remote, ref, ref, send_o.at[2], recv_s, sib_target))

    pair_rows = 2 * tokens
    low = lax.broadcasted_iota(jnp.int32, (tokens, share), 1) < HEAD_DIM
    at_lane = lax.broadcasted_iota(jnp.int32, (tokens, share), 1)
    ones = jnp.ones((tokens, share), bf16)

    def keep_keys(slot, keys, values):
        table = tabs_ref[0].astype(f32)
        for p in range(1, PLANE):
            table = table + tabs_ref[p].astype(f32)
        which = lax.broadcasted_iota(jnp.int32, table.shape, 0)
        for r in (0, 1):
            absent = jnp.sum(
                jnp.where(which == slot * 2 + r, table, 0.0), axis=0, keepdims=True
            )
            absent = jnp.broadcast_to(absent, (tokens, share)).astype(bf16)
            rows = pl.ds(pl.multiple_of(slot * pair_rows + r * tokens, tokens), tokens)
            part = slice(r * tokens, (r + 1) * tokens)
            kl_ref[rows, :] = jnp.where(low, keys[part], absent)
            kh_ref[rows, :] = jnp.where(low, absent, keys[part])
            vl_ref[rows, :] = jnp.where(low, values[part], ones)
            vh_ref[rows, :] = jnp.where(low, ones, values[part])

    def project_step(i):
        late = i // 2
        a = i + late * (1 - 2 * (i % 2))
        project(a + row * (3 - 2 * a), row + late * (1 - 2 * row), i % 2 == 0)

    def project(j, edge, at_edge):
        rows = pl.ds(pl.multiple_of(j * pair_rows, pair_rows), pair_rows)
        part = jnp.dot(blocks_ref[rows, :], w_ref[...], preferred_element_type=f32).astype(bf16)
        queries = part[:, 0:share] * bf16(HEAD_DIM ** (-0.5))
        keys, values = part[:, share:2 * share], part[:, 2 * share:]

        @pl.when(at_edge)
        def _():
            edge_out_ref[edge, :, 0:share] = keys
            edge_out_ref[edge, :, share:] = values
            send_edge(edge)

        for r in (0, 1):
            q = 2 * j + r
            q_rows = pl.ds(pl.multiple_of(q * tokens, tokens), tokens)
            mark_low = jnp.where(at_lane == q, 1.0, 0.0).astype(bf16)
            mark_high = jnp.where(at_lane == q + HEAD_DIM, 1.0, 0.0).astype(bf16)
            piece = queries[r * tokens:(r + 1) * tokens]
            ql_ref[q_rows, :] = jnp.where(low, piece, mark_high)
            qh_ref[q_rows, :] = jnp.where(low, mark_low, piece)
        keep_keys(j + 1, keys, values)

    def send_edge(e):
        z = plane + 2 * e - 1

        @pl.when(jnp.logical_and(z >= 0, z < planes))
        def _():
            remote(
                edge_out_ref.at[e], edge_in_ref.at[1 - e], send_e.at[e], recv_e.at[1 - e],
                device(region, z, row, core)).start()

    sent(edge_out_ref.at[0], send_e.at[0], has_down)
    sent(edge_out_ref.at[1], send_e.at[1], has_up)

    def take_edge(e):
        z = plane + 2 * e - 1
        there = jnp.logical_and(z >= 0, z < planes)
        arrive(there, functools.partial(
            remote, edge_in_ref.at[e], edge_in_ref.at[e], send_e.at[e], recv_e.at[e], sib_target))

        @pl.when(jnp.logical_not(there))
        def _():
            edge_in_ref[e] = jnp.zeros(edge_in_ref.shape[1:], bf16)

        keep_keys(e * 5, edge_in_ref[e, :, 0:share], edge_in_ref[e, :, share:])

    def digit(numbers, base, i):
        packed = sum(n << (base * k) for k, n in enumerate(numbers))
        return lax.rem(lax.shift_right_logical(i * 0 + packed, i * base), 1 << base)

    def order(i):
        a = digit(STEP_OWNERS, 2, i)
        same = digit(STEP_REGIONS, 1, i)
        return a + row * (3 - 2 * a), same * region + (1 - same) * (1 - region)

    def hand_over(i, out):
        j, r = order(i)
        q = 2 * j + r
        staged_ref[i] = out

        @pl.when(q == me)
        def _():
            mixed_ref[me] = out

        @pl.when(q != me)
        def _():
            remote(
                staged_ref.at[i], mixed_ref.at[me], send_m, recv_m,
                device(r, plane, j // 2, j % 2)).start()

    def attend_rows(j, start_row, count):
        rows = pl.ds(pl.multiple_of(start_row, count), count)
        keys = pl.ds(pl.multiple_of(j * pair_rows, pair_rows), 3 * pair_rows)
        heads = ((ql_ref, kl_ref, vl_ref), (qh_ref, kh_ref, vh_ref))
        scores = [
            lax.dot_general(
                q_ref[rows, :], k_ref[keys, :], (((1,), (1,)), ((), ())),
                preferred_element_type=f32,
            )
            for q_ref, k_ref, _ in heads
        ]
        mixes = []
        for score, (_, _, v_ref) in zip(scores, heads):
            shifted = jnp.exp(score - jnp.max(score, axis=-1, keepdims=True)).astype(bf16)
            mixes.append(jnp.dot(shifted, v_ref[keys, :], preferred_element_type=f32))
        lower = lax.broadcasted_iota(jnp.int32, (count, share), 1) < HEAD_DIM
        total = pltpu.roll(jnp.where(lower, mixes[1], mixes[0]), HEAD_DIM, 1)
        return (jnp.where(lower, mixes[0], mixes[1]) / total).astype(bf16)

    def attend_block(i):
        j, r = order(i)
        hand_over(i, attend_rows(j, j * pair_rows + r * tokens, tokens))

    blocks.own(range(CHUNKS))
    blocks.own_sib()
    own_w()
    own_out()
    blocks.direct(0)
    relay_w(1)
    relay_out(1)
    blocks.direct(1)
    spread_out(0)
    spread_out(1)
    relay_w(2)
    relay_out(2)
    spread_out(2)
    blocks.direct(2)
    blocks.direct(3)
    relay_w(planes - 1)
    wait_tables()
    blocks.finish([SIB, (1, 0, 1)])

    def drain(sends):
        for cond, wait, _ in sends:
            run(cond, wait)

    early = [entry for entry in pending if entry[2]]
    late = [entry for entry in pending if not entry[2]]
    pending.clear()

    def projections(i, carry):
        @pl.when(i == 2)
        def _():
            blocks.diagonal(0)
            drain(early)
            relay_out(planes - 1)
            spread_out(planes - 1)
            blocks.diagonal(1)
            blocks.finish([(0, 1, 1), (1, 1, 1)])

        project_step(i)
        return carry

    lax.fori_loop(0, PLANE // 2, projections, 0)
    to_sibling(OWN, 0, planes)
    for way in (0, 1):
        sent(go_ref.at[pl.ds(0, planes * 3 // 4), 0:2 * depth, :], send_o.at[way])
    sent(go_ref.at[0:planes], send_o.at[2])
    near = plane // near_planes

    HOOKS = {
        2: [lambda: onward_out(near)],
        3: [lambda: take_edge(1 - row)],
        4: [lambda: onward_out(1 - near)],
        5: [lambda: take_edge(row)],
    }

    def attention(i, carry):
        for at, hooks in HOOKS.items():
            @pl.when(i == at)
            def _():
                for hook in hooks:
                    hook()

        attend_block(i)
        return carry

    lax.fori_loop(0, PLANE, attention, 0)
    diagonal_out(near)
    diagonal_out(1 - near)
    finish_out()
    pieces = staged_ref.at[0:PLANE - 1]
    arrive(None, functools.partial(remote, pieces, pieces, send_m, recv_m, sib_target))
    sent(pieces, send_m)
    mixed = jnp.concatenate([mixed_ref[p] for p in range(PLANE)], axis=1)
    tile = min(512, width)
    for at in range(0, width, tile):
        weight = go_ref[:, :, at:at + tile].reshape(width, tile)
        projected = jnp.dot(mixed, weight, preferred_element_type=f32)
        out_ref[:, at:at + tile] = (
            x_ref[:, at:at + tile].astype(f32) + projected
        ).astype(out_ref.dtype)
    drain(late + pending)


def fused(block, qkv_weight, out_weight, norm_gain, near):
    owners = lax.axis_size("owner")
    devices = lax.axis_size("region") * owners
    planes = owners // 4
    tokens, width = block.shape
    depth = qkv_weight.shape[0]
    share = 2 * HEAD_DIM
    bf16 = jnp.bfloat16
    vmem = pl.BlockSpec(memory_space=pltpu.VMEM)
    dma = pltpu.SemaphoreType.DMA
    return pl.pallas_call(
        functools.partial(fused_kernel, owners),
        out_shape=pltpu.VMEM(block.shape, block.dtype),
        in_specs=[pl.BlockSpec(memory_space=pl.ANY)] * 5,
        out_specs=vmem,
        scratch_shapes=[
            pltpu.VMEM(block.shape, bf16),
            pltpu.VMEM(qkv_weight.shape, bf16),
            pltpu.VMEM((PLANE, depth, 3 * share), bf16),
            pltpu.VMEM((devices * depth, 3 * share), bf16),
            pltpu.VMEM((2 * planes, 4 * depth, width), bf16),
            pltpu.VMEM((PLANE * tokens, width), bf16),
            pltpu.VMEM((16, share), bf16),
            pltpu.VMEM((PLANE, 16, share), bf16),
        ] + [pltpu.VMEM((PLANE * tokens, share), bf16)] * 2
        + [pltpu.VMEM((12 * tokens, share), bf16)] * 4
        + [pltpu.VMEM((2, 2 * tokens, 2 * share), bf16)] * 2
        + [pltpu.VMEM((PLANE, tokens, share), bf16)] * 2
        + [
            dma, dma((2,)), dma, dma,
            dma((2, planes - 1)), dma((planes, 2)), dma((planes,)),
            dma((4,)), dma((5, CHUNKS)), dma((3,)), dma((3, 2)), dma,
            dma((2,)), dma((2,)), dma, dma, dma((5,)),
            pltpu.VMEM(norm_gain.shape, norm_gain.dtype), pltpu.SMEM(near.shape, near.dtype),
        ],
        compiler_params=pltpu.CompilerParams(
            collective_id=0, has_side_effects=True, vmem_limit_bytes=54 * 1024 * 1024
        ),
        name="fused",
    )(block, qkv_weight, out_weight, norm_gain, near)


def attend_kernel(listed_ref, x_ref, xs_ref, gain_ref, bias_ref, wq_ref, wo_ref, out_ref,
                  normed_ref, q_ref, kv_ref, mixed_ref):
    tokens, width = x_ref.shape
    others = xs_ref.shape[0]
    gain = gain_ref[...]
    normed_ref[0:tokens, :] = layer_norm(x_ref[...], gain)

    @pl.loop(0, others)
    def _(slot):
        rows = pl.ds(pl.multiple_of((slot + 1) * tokens, tokens), tokens)
        block = xs_ref[slot].astype(jnp.float32)
        block = jnp.where(listed_ref[slot] > 0, block, 0.0)
        normed_ref[rows, :] = layer_norm(block, gain)

    tile = min(512, width)

    @pl.loop(0, width // tile)
    def _(step):
        cols = pl.ds(pl.multiple_of(step * tile, tile), tile)
        part = jnp.dot(normed_ref[0:tokens, :], wq_ref[:, cols], preferred_element_type=jnp.float32)
        q_ref[:, cols] = part.astype(jnp.bfloat16) * jnp.bfloat16(HEAD_DIM ** (-0.5))

    @pl.loop(0, 2 * width // tile)
    def _(step):
        cols = pl.ds(pl.multiple_of(step * tile, tile), tile)
        from_cols = pl.ds(pl.multiple_of(width + step * tile, tile), tile)
        kv_ref[:, cols] = jnp.dot(
            normed_ref[...], wq_ref[:, from_cols], preferred_element_type=jnp.float32
        ).astype(jnp.bfloat16)

    pair = 2 * HEAD_DIM
    low = lax.broadcasted_iota(jnp.int32, (tokens, pair), 1) < HEAD_DIM
    bias = bias_ref[...]

    @pl.loop(0, width // pair)
    def _(group):
        cols = pl.ds(pl.multiple_of(group * pair, pair), pair)
        value_cols = pl.ds(pl.multiple_of(width + group * pair, pair), pair)
        queries = q_ref[:, cols]
        keys = kv_ref[:, cols]
        values = kv_ref[:, value_cols]
        halves = []
        for mine in (low, jnp.logical_not(low)):
            query = jnp.where(mine, queries, jnp.zeros_like(queries))
            scores = lax.dot_general(
                query, keys, (((1,), (1,)), ((), ())), preferred_element_type=jnp.float32
            ) + bias
            shifted = jnp.exp(scores - jnp.max(scores, axis=-1, keepdims=True))
            total = jnp.sum(shifted, axis=-1, keepdims=True)
            mixed = jnp.dot(shifted.astype(jnp.bfloat16), values, preferred_element_type=jnp.float32)
            halves.append(mixed / total)
        mixed_ref[:, cols] = jnp.where(low, halves[0], halves[1]).astype(jnp.bfloat16)

    @pl.loop(0, width // tile)
    def _(step):
        cols = pl.ds(pl.multiple_of(step * tile, tile), tile)
        projected = jnp.dot(mixed_ref[...], wo_ref[:, cols], preferred_element_type=jnp.float32)
        out_ref[:, cols] = (x_ref[:, cols].astype(jnp.float32) + projected).astype(out_ref.dtype)


def attend(listed, block, others, norm_gain, bias, qkv_weight, out_weight):
    tokens, width = block.shape
    count = (others.shape[0] + 1) * tokens
    vmem = pl.BlockSpec(memory_space=pltpu.VMEM)
    return pl.pallas_call(
        attend_kernel,
        out_shape=jax.ShapeDtypeStruct(block.shape, block.dtype),
        in_specs=[pl.BlockSpec(memory_space=pltpu.SMEM)] + [vmem] * 6,
        out_specs=vmem,
        scratch_shapes=[
            pltpu.VMEM((count, width), jnp.bfloat16),
            pltpu.VMEM((tokens, width), jnp.bfloat16),
            pltpu.VMEM((count, 2 * width), jnp.bfloat16),
            pltpu.VMEM((tokens, width), jnp.bfloat16),
        ],
        compiler_params=pltpu.CompilerParams(vmem_limit_bytes=60 * 1024 * 1024),
        name="attend",
    )(listed, block, others, norm_gain, bias, qkv_weight, out_weight)


def shards(voxels, norm_gain, qkv_weight, out_weight, neighbours):
    block_size, model_width = voxels.shape[-2:]
    block = voxels.reshape(block_size, model_width)
    regions, owners = (lax.axis_size("region"), lax.axis_size("owner"))
    region, owner = (lax.axis_index("region"), lax.axis_index("owner"))
    share = 2 * HEAD_DIM
    together = regions == 2 and owners % 8 == 0 and model_width == PLANE * share
    together = together and block_size % (16 * CHUNKS) == 0 and voxels.shape[2] == 1
    if together:
        out = fused(block, qkv_weight, out_weight, norm_gain[None, :], neighbours.reshape(1, -1))
        return out.reshape(voxels.shape)
    wide = padded(voxels[:, :, 0], (("owner", 1), ("region", 0)), 1)
    wide = wide.reshape(-1, block_size, model_width)
    middle = wide.shape[0] // 2
    others = jnp.concatenate([wide[:middle], wide[middle + 1:]], axis=0)
    full_qkv = lax.all_gather(qkv_weight, ("region", "owner"), axis=0, tiled=True)
    full_out = lax.all_gather(out_weight, ("region", "owner"), axis=0, tiled=True)
    offsets = [(i, j) for i in (-1, 0, 1) for j in (-1, 0, 1) if i or j]
    numbers = []
    for up, along in offsets:
        inside = (owner + along >= 0) & (owner + along < owners)
        number = (region + up) * owners + owner + along
        numbers.append(jnp.where(inside & (number >= 0), number, -2))
    listed = jnp.any(neighbours.reshape(1, -1) == jnp.stack(numbers)[:, None], axis=1)
    present = jnp.concatenate([jnp.ones((1,), bool), listed])
    bias = jnp.repeat(jnp.where(present, 0.0, MASKED).astype(jnp.float32), block_size)[None, :]
    out = attend(
        listed.astype(jnp.int32), block, others, norm_gain[None, :], bias, full_qkv, full_out
    )
    return out.reshape(voxels.shape)


def solution(mesh):
    return jax.shard_map(
        shards,
        mesh=mesh,
        in_specs=(
            P("region", "owner", None, None, None),
            P(),
            P(("region", "owner"), None),
            P(("region", "owner"), None),
            P("region", "owner", None, None),
        ),
        out_specs=P("region", "owner", None, None, None),
        check_vma=False,
    )
```

```python
import functools

import jax
import jax.numpy as jnp
from jax import lax
from jax.experimental import pallas as pl
from jax.experimental.pallas import tpu as pltpu
from jax.sharding import PartitionSpec as P

HEAD_DIM = 64
MESH = pl.DeviceIdType.MESH
PLANE = 8
CHUNKS = 4
MASKED = -1e30
STEP_OWNERS = (2, 2, 1, 3, 3, 0, 1, 0)
STEP_REGIONS = (0, 1, 0, 0, 1, 0, 1, 1)


def padded(value, sides, width):
    for axis, dim in sides:
        devices, length = (lax.axis_size(axis), value.shape[dim])
        up = [(i, (i + 1) % devices) for i in range(devices - 1)]
        down = [(j, i) for i, j in up]
        last = lax.slice_in_dim(value, length - width, length, axis=dim)
        first = lax.slice_in_dim(value, 0, width, axis=dim)
        before = lax.ppermute(last, axis, up)
        after = lax.ppermute(first, axis, down)
        value = jnp.concatenate([before, value, after], axis=dim)
    return value


def layer_norm(inputs, norm_gain):
    widened = inputs.astype(jnp.float32)
    average = jnp.mean(widened, axis=-1, keepdims=True)
    spread = jnp.mean((widened - average) ** 2, axis=-1, keepdims=True)
    return ((widened - average) * lax.rsqrt(spread + 1e-06) * norm_gain).astype(jnp.bfloat16)


def fused_kernel(owners, x_hbm, wq_hbm, wo_hbm, gain_hbm, near_hbm, out_ref,
                 x_ref, wq_ref, cut_ref, w_ref, go_ref, blocks_ref, own_tab_ref, tabs_ref,
                 ql_ref, qh_ref, kl_ref, kh_ref, vl_ref, vh_ref,
                 edge_out_ref, edge_in_ref, staged_ref, mixed_ref,
                 send_w, recv_w, send_t, recv_t, send_z, recv_z, recv_l, send_b, recv_b,
                 send_o, recv_o, recv_s, send_e, recv_e, send_m, recv_m, local_sem, gain_ref, near_ref):
    tokens, width = x_ref.shape
    depth = wo_hbm.shape[0]
    share = 2 * HEAD_DIM
    planes = owners // 4
    region = lax.axis_index("region")
    owner = lax.axis_index("owner")
    core = lax.rem(owner, 2)
    row = lax.rem(owner // 2, 2)
    plane = owner // 4
    bf16, f32 = jnp.bfloat16, jnp.float32

    def place(r, y, c):
        return (2 * y + c) * 2 + r

    def device(r, z, y, c):
        return (r, z * 4 + y * 2 + c)

    me = place(region, row, core)
    mine = region * owners + owner
    peers = [
        (dr, dy, dc) for dr in (1, 0) for dy in (1, 0) for dc in (1, 0) if dr or dy or dc
    ]

    def flip(value, change):
        return 1 - value if change else value

    def moved(change):
        dr, dy, dc = change
        return flip(region, dr), flip(row, dy), flip(core, dc)

    def peer_device(change):
        r, y, c = moved(change)
        return device(r, plane, y, c)

    X, Y, SIB = (1, 0, 0), (0, 1, 0), (0, 0, 1)
    has_up = plane < planes - 1
    has_down = plane > 0
    above = device(region, plane + 1, row, core)
    below = device(region, plane - 1, row, core)

    def run(cond, fn):
        if cond is None:
            fn()
        else:
            pl.when(cond)(fn)

    def both(a, b):
        if a is None:
            return b
        return a if b is None else jnp.logical_and(a, b)

    shard_rows = pl.ds(pl.multiple_of(mine * depth, depth), depth)
    local = [
        pltpu.make_async_copy(wq_hbm, wq_ref, local_sem.at[0]),
        pltpu.make_async_copy(x_hbm, x_ref, local_sem.at[1]),
        pltpu.make_async_copy(
            wo_hbm,
            go_ref.at[region * planes + plane, pl.ds(
                pl.multiple_of((2 * row + core) * depth, depth), depth), :],
            local_sem.at[2],
        ),
    ]
    local.append(pltpu.make_async_copy(gain_hbm, gain_ref, local_sem.at[3]))
    local.append(pltpu.make_async_copy(near_hbm, near_ref, local_sem.at[4]))
    for copy in local:
        copy.start()
    barrier = pltpu.get_barrier_semaphore()

    def greet(target):
        pl.semaphore_signal(barrier, inc=1, device_id=target, device_id_type=MESH)

    for change in peers:
        greet(peer_device(change))
    run(has_up, lambda: greet(above))
    run(has_down, lambda: greet(below))

    local[0].wait()
    for p in range(PLANE):
        for part in range(3):
            at = part * width + p * share
            cut_ref[p, :, part * share:(part + 1) * share] = wq_ref[:, at:at + share]
    w_ref[shard_rows, :] = cut_ref[me]

    pl.semaphore_wait(
        barrier, len(peers) + has_up.astype(jnp.int32) + has_down.astype(jnp.int32)
    )

    pending = []
    sib_target = peer_device(SIB)

    def remote(src, dst, send_sem, recv_sem, target):
        return pltpu.make_async_remote_copy(
            src_ref=src, dst_ref=dst, send_sem=send_sem, recv_sem=recv_sem,
            device_id=target, device_id_type=MESH,
        )

    def start(cond, make):
        run(cond, lambda: make().start())

    def sent(ref, sem, cond=None, early=False):
        pending.append((cond, lambda: remote(ref, ref, sem, sem, sib_target).wait_send(), early))

    def arrive(cond, make):
        run(cond, lambda: make().wait_recv())

    for change in peers:
        to = place(*moved(change))
        start(None, functools.partial(
            remote, cut_ref.at[to], w_ref.at[shard_rows, :], send_w, recv_w.at[change[0]],
            peer_device(change)))
    sent(cut_ref.at[0:PLANE - 1], send_w, early=True)

    def wait_shards(flipped):
        count = sum(change[0] == flipped for change in peers)
        ref = cut_ref.at[0:count]
        arrive(None, functools.partial(
            remote, ref, ref, send_w, recv_w.at[flipped], sib_target))

    local[1].wait()
    local[3].wait()
    local[4].wait()
    own_rows = pl.ds(pl.multiple_of(me * tokens, tokens), tokens)
    blocks_ref[own_rows, :] = layer_norm(x_ref[...], gain_ref[...])
    entries, lanes = own_tab_ref.shape
    entry = lax.broadcasted_iota(jnp.int32, (entries, lanes), 0)
    lane = lax.broadcasted_iota(jnp.int32, (entries, lanes), 1)
    far_region = entry % 2
    far_owner = plane * 4 - 1 + entry // 2
    number = far_region * owners + far_owner
    listed = number == mine
    for k in range(near_ref.shape[1]):
        listed = jnp.logical_or(listed, number == near_ref[0, k])
    inside = jnp.logical_and(far_owner >= 0, far_owner < owners)
    listed = jnp.logical_and(listed, inside)
    marked = jnp.logical_or(lane == me, lane == me + HEAD_DIM)
    own_tab_ref[...] = jnp.where(
        jnp.logical_and(marked, jnp.logical_not(listed)), MASKED, 0.0
    ).astype(bf16)
    tabs_ref[me] = own_tab_ref[...]
    local[2].wait()

    for change in peers:
        start(None, functools.partial(
            remote, own_tab_ref, tabs_ref.at[me], send_t, recv_t, peer_device(change)))
    sent(tabs_ref.at[0:PLANE - 1], send_t, early=True)

    def wait_tables():
        ref = tabs_ref.at[0:PLANE - 1]
        arrive(None, functools.partial(remote, ref, ref, send_t, recv_t, sib_target))

    OWN, DIAGONAL = (0, 0, 0), (1, 1, 0)
    LINE, BY_X, BY_Y, BY_BOTH, BY_SIB = range(5)

    def slot(sems, source, to, piece):
        way = tuple(int(a != b) for a, b in zip(source, to))
        if way[2]:
            return sems.at[BY_SIB, way[0] + 2 * way[1]]
        return sems.at[way[0] + 2 * way[1], piece]

    def lane_of(to, source):
        if to != SIB:
            return 0 if to == X else 1
        return 2 if source in (OWN, X) else 3

    class Gather:
        def __init__(self, pieces, view, send, recv):
            self.pieces, self.view, self.send_sem, self.recv = pieces, view, send, recv
            self.first = list(range(pieces // 2))
            self.second = list(range(pieces // 2, pieces))

        def send(self, change, piece, source):
            ref = self.view(source, piece)
            start(None, functools.partial(
                remote, ref, ref, self.send_sem.at[lane_of(change, source)],
                slot(self.recv, source, change, piece), peer_device(change)))

        def wait(self, source, piece):
            ref = self.view(source, piece)
            arrive(None, functools.partial(
                remote, ref, ref, self.send_sem.at[0], slot(self.recv, source, OWN, piece),
                sib_target))

        def own(self, ks):
            for k in ks:
                self.send(X, (self.first + self.second)[k], (0, 0, 0))
                self.send(Y, (self.second + self.first)[k], (0, 0, 0))

        def own_sib(self):
            for piece in range(self.pieces):
                self.send(SIB, piece, (0, 0, 0))

        def direct(self, k):
            a, b = (self.first + self.second)[k], (self.second + self.first)[k]
            onward = k < self.pieces // 2
            self.wait(X, a)
            if onward:
                self.send(Y, a, X)
            self.send(SIB, a, X)
            self.wait(Y, b)
            if onward:
                self.send(X, b, Y)
            self.send(SIB, b, Y)

        def diagonal(self, k):
            for piece in (self.first[k], self.second[k]):
                self.wait((1, 1, 0), piece)
                self.send(SIB, piece, (1, 1, 0))

        def finish(self, sources):
            for source in sources:
                at = pl.multiple_of(place(*moved(source)) * tokens, tokens)
                ref = blocks_ref.at[pl.ds(at, tokens), :]
                arrive(None, functools.partial(
                    remote, ref, ref, self.send_sem.at[0], slot(self.recv, source, OWN, None),
                    sib_target))

    piece_rows = tokens // CHUNKS

    def block_piece(source, piece):
        at = place(*moved(source)) * tokens + piece * piece_rows
        return blocks_ref.at[pl.ds(pl.multiple_of(at, piece_rows), piece_rows), :]

    blocks = Gather(CHUNKS, block_piece, send_b, recv_b)
    for way, count in ((0, 3), (1, 3), (2, 4), (3, 4)):
        sent(blocks_ref.at[0:count * tokens // 2, :], send_b.at[way])

    def line(d):
        return [(plane - d, plane - d >= 0), (plane + d, plane + d < planes)]

    def w_half(z, r):
        at = (r * owners + z * 4) * depth
        return w_ref.at[pl.ds(pl.multiple_of(at, 4 * depth), 4 * depth), :]

    def send_w_half(z, r, up, cond, d):
        ref = w_half(z, r)
        start(both(cond, has_up if up else has_down), functools.partial(
            remote, ref, ref, send_z.at[int(up), d], recv_z.at[z, r], above if up else below))

    def wait_w_half(z, r, cond):
        ref = w_half(z, r)
        arrive(cond, functools.partial(
            remote, ref, ref, send_z.at[0, 0], recv_z.at[z, r], sib_target))

    for d in range(planes - 1):
        for up, cond in ((1, plane - d >= 0), (0, plane + d < planes)):
            cond = jnp.logical_and(cond, has_up if up else has_down)
            sent(go_ref.at[0], send_z.at[up, d], cond, early=True)

    def own_w():
        for flipped in (0, 1):
            wait_shards(flipped)
            for up in (True, False):
                send_w_half(plane, flip(region, flipped), up, None, 0)

    def relay_w(d):
        for flipped in (0, 1):
            for (z, cond), up in zip(line(d), (True, False)):
                wait_w_half(z, flip(region, flipped), cond)
                if d < planes - 1:
                    send_w_half(z, flip(region, flipped), up, cond, d)

    near_planes = planes // 2

    def out_piece(source, first, count, half=None):
        r, y, c = moved(source)
        at, size = (2 * y + c) * depth, depth
        if half is not None:
            size = depth // 2
            at = at + half * size
        return go_ref.at[
            pl.ds(r * planes + first, count), pl.ds(pl.multiple_of(at, size), size), :]

    def line_out(z, up, cond, d):
        ref = out_piece(OWN, z, 1)
        start(both(cond, has_up if up else has_down), functools.partial(
            remote, ref, ref, send_z.at[int(up), d], recv_l.at[z], above if up else below))

    def own_out():
        for up in (True, False):
            line_out(plane, up, None, 0)

    def relay_out(d):
        for (z, cond), up in zip(line(d), (True, False)):
            ref = out_piece(OWN, z, 1)
            arrive(cond, functools.partial(
                remote, ref, ref, send_o.at[0], recv_l.at[z], sib_target))
            if d < planes - 1:
                line_out(z, up, cond, d)

    def ring(d):
        return [(plane, None)] if d == 0 else line(d)

    def spread_out(d):
        for z, cond in ring(d):
            ref = out_piece(OWN, z, 1)
            for way, to in ((0, X), (1, Y)):
                start(cond, functools.partial(
                    remote, ref, ref, send_o.at[way], recv_o.at[way, z // near_planes],
                    peer_device(to)))

    def to_sibling(source, first, count):
        ref = out_piece(source, first, count)
        remote(ref, ref, send_o.at[2], recv_s, sib_target).start()

    def wait_group(way, group):
        ref = out_piece(OWN, group * near_planes, near_planes)
        arrive(None, functools.partial(
            remote, ref, ref, send_o.at[0], recv_o.at[way, group], sib_target))

    def onward_out(group):
        for way, source, to in ((0, X, Y), (1, Y, X)):
            wait_group(way, group)
            ref = out_piece(source, group * near_planes, near_planes, way)
            remote(
                ref, ref, send_o.at[1 - way], recv_o.at[2, group], peer_device(to)).start()
            to_sibling(source, group * near_planes, near_planes)

    def diagonal_out(group):
        wait_group(2, group)
        to_sibling(DIAGONAL, group * near_planes, near_planes)

    def finish_out():
        ref = go_ref.at[0:planes]
        arrive(None, functools.partial(remote, ref, ref, send_o.at[2], recv_s, sib_target))

    pair_rows = 2 * tokens
    low = lax.broadcasted_iota(jnp.int32, (tokens, share), 1) < HEAD_DIM
    at_lane = lax.broadcasted_iota(jnp.int32, (tokens, share), 1)
    ones = jnp.ones((tokens, share), bf16)

    def keep_keys(slot, keys, values):
        table = tabs_ref[0].astype(f32)
        for p in range(1, PLANE):
            table = table + tabs_ref[p].astype(f32)
        which = lax.broadcasted_iota(jnp.int32, table.shape, 0)
        for r in (0, 1):
            absent = jnp.sum(
                jnp.where(which == slot * 2 + r, table, 0.0), axis=0, keepdims=True
            )
            absent = jnp.broadcast_to(absent, (tokens, share)).astype(bf16)
            rows = pl.ds(pl.multiple_of(slot * pair_rows + r * tokens, tokens), tokens)
            part = slice(r * tokens, (r + 1) * tokens)
            kl_ref[rows, :] = jnp.where(low, keys[part], absent)
            kh_ref[rows, :] = jnp.where(low, absent, keys[part])
            vl_ref[rows, :] = jnp.where(low, values[part], ones)
            vh_ref[rows, :] = jnp.where(low, ones, values[part])

    def project_step(i):
        late = i // 2
        a = i + late * (1 - 2 * (i % 2))
        project(a + row * (3 - 2 * a), row + late * (1 - 2 * row), i % 2 == 0)

    def project(j, edge, at_edge):
        rows = pl.ds(pl.multiple_of(j * pair_rows, pair_rows), pair_rows)
        part = jnp.dot(blocks_ref[rows, :], w_ref[...], preferred_element_type=f32).astype(bf16)
        queries = part[:, 0:share] * bf16(HEAD_DIM ** (-0.5))
        keys, values = part[:, share:2 * share], part[:, 2 * share:]

        @pl.when(at_edge)
        def _():
            edge_out_ref[edge, :, 0:share] = keys
            edge_out_ref[edge, :, share:] = values
            send_edge(edge)

        for r in (0, 1):
            q = 2 * j + r
            q_rows = pl.ds(pl.multiple_of(q * tokens, tokens), tokens)
            mark_low = jnp.where(at_lane == q, 1.0, 0.0).astype(bf16)
            mark_high = jnp.where(at_lane == q + HEAD_DIM, 1.0, 0.0).astype(bf16)
            piece = queries[r * tokens:(r + 1) * tokens]
            ql_ref[q_rows, :] = jnp.where(low, piece, mark_high)
            qh_ref[q_rows, :] = jnp.where(low, mark_low, piece)
        keep_keys(j + 1, keys, values)

    def send_edge(e):
        z = plane + 2 * e - 1

        @pl.when(jnp.logical_and(z >= 0, z < planes))
        def _():
            remote(
                edge_out_ref.at[e], edge_in_ref.at[1 - e], send_e.at[e], recv_e.at[1 - e],
                device(region, z, row, core)).start()

    sent(edge_out_ref.at[0], send_e.at[0], has_down)
    sent(edge_out_ref.at[1], send_e.at[1], has_up)

    def take_edge(e):
        z = plane + 2 * e - 1
        there = jnp.logical_and(z >= 0, z < planes)
        arrive(there, functools.partial(
            remote, edge_in_ref.at[e], edge_in_ref.at[e], send_e.at[e], recv_e.at[e], sib_target))

        @pl.when(jnp.logical_not(there))
        def _():
            edge_in_ref[e] = jnp.zeros(edge_in_ref.shape[1:], bf16)

        keep_keys(e * 5, edge_in_ref[e, :, 0:share], edge_in_ref[e, :, share:])

    def digit(numbers, base, i):
        packed = sum(n << (base * k) for k, n in enumerate(numbers))
        return lax.rem(lax.shift_right_logical(i * 0 + packed, i * base), 1 << base)

    def order(i):
        a = digit(STEP_OWNERS, 2, i)
        same = digit(STEP_REGIONS, 1, i)
        return a + row * (3 - 2 * a), same * region + (1 - same) * (1 - region)

    def hand_over(i, out):
        j, r = order(i)
        q = 2 * j + r
        staged_ref[i] = out

        @pl.when(q == me)
        def _():
            mixed_ref[me] = out

        @pl.when(q != me)
        def _():
            remote(
                staged_ref.at[i], mixed_ref.at[me], send_m, recv_m,
                device(r, plane, j // 2, j % 2)).start()

    def attend_rows(j, start_row, count):
        rows = pl.ds(pl.multiple_of(start_row, count), count)
        keys = pl.ds(pl.multiple_of(j * pair_rows, pair_rows), 3 * pair_rows)
        heads = ((ql_ref, kl_ref, vl_ref), (qh_ref, kh_ref, vh_ref))
        scores = [
            lax.dot_general(
                q_ref[rows, :], k_ref[keys, :], (((1,), (1,)), ((), ())),
                preferred_element_type=f32,
            )
            for q_ref, k_ref, _ in heads
        ]
        mixes = []
        for score, (_, _, v_ref) in zip(scores, heads):
            shifted = jnp.exp(score - jnp.max(score, axis=-1, keepdims=True)).astype(bf16)
            mixes.append(jnp.dot(shifted, v_ref[keys, :], preferred_element_type=f32))
        lower = lax.broadcasted_iota(jnp.int32, (count, share), 1) < HEAD_DIM
        total = pltpu.roll(jnp.where(lower, mixes[1], mixes[0]), HEAD_DIM, 1)
        return (jnp.where(lower, mixes[0], mixes[1]) / total).astype(bf16)

    def attend_block(i):
        j, r = order(i)
        hand_over(i, attend_rows(j, j * pair_rows + r * tokens, tokens))

    blocks.own(range(CHUNKS))
    blocks.own_sib()
    own_w()
    own_out()
    blocks.direct(0)
    relay_w(1)
    relay_out(1)
    blocks.direct(1)
    spread_out(0)
    spread_out(1)
    relay_w(2)
    relay_out(2)
    spread_out(2)
    blocks.direct(2)
    blocks.direct(3)
    relay_w(planes - 1)
    wait_tables()
    blocks.finish([SIB, (1, 0, 1)])

    def drain(sends):
        for cond, wait, _ in sends:
            run(cond, wait)

    early = [entry for entry in pending if entry[2]]
    late = [entry for entry in pending if not entry[2]]
    pending.clear()

    def projections(i, carry):
        @pl.when(i == 2)
        def _():
            blocks.diagonal(0)
            drain(early)
            relay_out(planes - 1)
            spread_out(planes - 1)
            blocks.diagonal(1)
            to_sibling(OWN, 0, planes)
            blocks.finish([(0, 1, 1), (1, 1, 1)])

        project_step(i)
        return carry

    lax.fori_loop(0, PLANE // 2, projections, 0)
    for way in (0, 1):
        sent(go_ref.at[pl.ds(0, planes * 3 // 4), 0:2 * depth, :], send_o.at[way])
    sent(go_ref.at[0:planes], send_o.at[2])
    near = plane // near_planes

    HOOKS = {
        2: [lambda: onward_out(near)],
        3: [lambda: take_edge(1 - row)],
        4: [lambda: onward_out(1 - near)],
        5: [lambda: take_edge(row)],
    }

    def attention(i, carry):
        for at, hooks in HOOKS.items():
            @pl.when(i == at)
            def _():
                for hook in hooks:
                    hook()

        attend_block(i)
        return carry

    lax.fori_loop(0, PLANE, attention, 0)
    diagonal_out(near)
    diagonal_out(1 - near)
    finish_out()
    pieces = staged_ref.at[0:PLANE - 1]
    arrive(None, functools.partial(remote, pieces, pieces, send_m, recv_m, sib_target))
    sent(pieces, send_m)
    mixed = jnp.concatenate([mixed_ref[p] for p in range(PLANE)], axis=1)
    tile = min(512, width)
    for at in range(0, width, tile):
        weight = go_ref[:, :, at:at + tile].reshape(width, tile)
        projected = jnp.dot(mixed, weight, preferred_element_type=f32)
        out_ref[:, at:at + tile] = (
            x_ref[:, at:at + tile].astype(f32) + projected
        ).astype(out_ref.dtype)
    drain(late + pending)


def fused(block, qkv_weight, out_weight, norm_gain, near):
    owners = lax.axis_size("owner")
    devices = lax.axis_size("region") * owners
    planes = owners // 4
    tokens, width = block.shape
    depth = qkv_weight.shape[0]
    share = 2 * HEAD_DIM
    bf16 = jnp.bfloat16
    vmem = pl.BlockSpec(memory_space=pltpu.VMEM)
    dma = pltpu.SemaphoreType.DMA
    return pl.pallas_call(
        functools.partial(fused_kernel, owners),
        out_shape=pltpu.VMEM(block.shape, block.dtype),
        in_specs=[pl.BlockSpec(memory_space=pl.ANY)] * 5,
        out_specs=vmem,
        scratch_shapes=[
            pltpu.VMEM(block.shape, bf16),
            pltpu.VMEM(qkv_weight.shape, bf16),
            pltpu.VMEM((PLANE, depth, 3 * share), bf16),
            pltpu.VMEM((devices * depth, 3 * share), bf16),
            pltpu.VMEM((2 * planes, 4 * depth, width), bf16),
            pltpu.VMEM((PLANE * tokens, width), bf16),
            pltpu.VMEM((16, share), bf16),
            pltpu.VMEM((PLANE, 16, share), bf16),
        ] + [pltpu.VMEM((PLANE * tokens, share), bf16)] * 2
        + [pltpu.VMEM((12 * tokens, share), bf16)] * 4
        + [pltpu.VMEM((2, 2 * tokens, 2 * share), bf16)] * 2
        + [pltpu.VMEM((PLANE, tokens, share), bf16)] * 2
        + [
            dma, dma((2,)), dma, dma,
            dma((2, planes - 1)), dma((planes, 2)), dma((planes,)),
            dma((4,)), dma((5, CHUNKS)), dma((3,)), dma((3, 2)), dma,
            dma((2,)), dma((2,)), dma, dma, dma((5,)),
            pltpu.VMEM(norm_gain.shape, norm_gain.dtype), pltpu.SMEM(near.shape, near.dtype),
        ],
        compiler_params=pltpu.CompilerParams(
            collective_id=0, has_side_effects=True, vmem_limit_bytes=54 * 1024 * 1024
        ),
        name="fused",
    )(block, qkv_weight, out_weight, norm_gain, near)


def attend_kernel(listed_ref, x_ref, xs_ref, gain_ref, bias_ref, wq_ref, wo_ref, out_ref,
                  normed_ref, q_ref, kv_ref, mixed_ref):
    tokens, width = x_ref.shape
    others = xs_ref.shape[0]
    gain = gain_ref[...]
    normed_ref[0:tokens, :] = layer_norm(x_ref[...], gain)

    @pl.loop(0, others)
    def _(slot):
        rows = pl.ds(pl.multiple_of((slot + 1) * tokens, tokens), tokens)
        block = xs_ref[slot].astype(jnp.float32)
        block = jnp.where(listed_ref[slot] > 0, block, 0.0)
        normed_ref[rows, :] = layer_norm(block, gain)

    tile = min(512, width)

    @pl.loop(0, width // tile)
    def _(step):
        cols = pl.ds(pl.multiple_of(step * tile, tile), tile)
        part = jnp.dot(normed_ref[0:tokens, :], wq_ref[:, cols], preferred_element_type=jnp.float32)
        q_ref[:, cols] = part.astype(jnp.bfloat16) * jnp.bfloat16(HEAD_DIM ** (-0.5))

    @pl.loop(0, 2 * width // tile)
    def _(step):
        cols = pl.ds(pl.multiple_of(step * tile, tile), tile)
        from_cols = pl.ds(pl.multiple_of(width + step * tile, tile), tile)
        kv_ref[:, cols] = jnp.dot(
            normed_ref[...], wq_ref[:, from_cols], preferred_element_type=jnp.float32
        ).astype(jnp.bfloat16)

    pair = 2 * HEAD_DIM
    low = lax.broadcasted_iota(jnp.int32, (tokens, pair), 1) < HEAD_DIM
    bias = bias_ref[...]

    @pl.loop(0, width // pair)
    def _(group):
        cols = pl.ds(pl.multiple_of(group * pair, pair), pair)
        value_cols = pl.ds(pl.multiple_of(width + group * pair, pair), pair)
        queries = q_ref[:, cols]
        keys = kv_ref[:, cols]
        values = kv_ref[:, value_cols]
        halves = []
        for mine in (low, jnp.logical_not(low)):
            query = jnp.where(mine, queries, jnp.zeros_like(queries))
            scores = lax.dot_general(
                query, keys, (((1,), (1,)), ((), ())), preferred_element_type=jnp.float32
            ) + bias
            shifted = jnp.exp(scores - jnp.max(scores, axis=-1, keepdims=True))
            total = jnp.sum(shifted, axis=-1, keepdims=True)
            mixed = jnp.dot(shifted.astype(jnp.bfloat16), values, preferred_element_type=jnp.float32)
            halves.append(mixed / total)
        mixed_ref[:, cols] = jnp.where(low, halves[0], halves[1]).astype(jnp.bfloat16)

    @pl.loop(0, width // tile)
    def _(step):
        cols = pl.ds(pl.multiple_of(step * tile, tile), tile)
        projected = jnp.dot(mixed_ref[...], wo_ref[:, cols], preferred_element_type=jnp.float32)
        out_ref[:, cols] = (x_ref[:, cols].astype(jnp.float32) + projected).astype(out_ref.dtype)


def attend(listed, block, others, norm_gain, bias, qkv_weight, out_weight):
    tokens, width = block.shape
    count = (others.shape[0] + 1) * tokens
    vmem = pl.BlockSpec(memory_space=pltpu.VMEM)
    return pl.pallas_call(
        attend_kernel,
        out_shape=jax.ShapeDtypeStruct(block.shape, block.dtype),
        in_specs=[pl.BlockSpec(memory_space=pltpu.SMEM)] + [vmem] * 6,
        out_specs=vmem,
        scratch_shapes=[
            pltpu.VMEM((count, width), jnp.bfloat16),
            pltpu.VMEM((tokens, width), jnp.bfloat16),
            pltpu.VMEM((count, 2 * width), jnp.bfloat16),
            pltpu.VMEM((tokens, width), jnp.bfloat16),
        ],
        compiler_params=pltpu.CompilerParams(vmem_limit_bytes=60 * 1024 * 1024),
        name="attend",
    )(listed, block, others, norm_gain, bias, qkv_weight, out_weight)


def shards(voxels, norm_gain, qkv_weight, out_weight, neighbours):
    block_size, model_width = voxels.shape[-2:]
    block = voxels.reshape(block_size, model_width)
    regions, owners = (lax.axis_size("region"), lax.axis_size("owner"))
    region, owner = (lax.axis_index("region"), lax.axis_index("owner"))
    share = 2 * HEAD_DIM
    together = regions == 2 and owners % 8 == 0 and model_width == PLANE * share
    together = together and block_size % (16 * CHUNKS) == 0 and voxels.shape[2] == 1
    if together:
        out = fused(block, qkv_weight, out_weight, norm_gain[None, :], neighbours.reshape(1, -1))
        return out.reshape(voxels.shape)
    wide = padded(voxels[:, :, 0], (("owner", 1), ("region", 0)), 1)
    wide = wide.reshape(-1, block_size, model_width)
    middle = wide.shape[0] // 2
    others = jnp.concatenate([wide[:middle], wide[middle + 1:]], axis=0)
    full_qkv = lax.all_gather(qkv_weight, ("region", "owner"), axis=0, tiled=True)
    full_out = lax.all_gather(out_weight, ("region", "owner"), axis=0, tiled=True)
    offsets = [(i, j) for i in (-1, 0, 1) for j in (-1, 0, 1) if i or j]
    numbers = []
    for up, along in offsets:
        inside = (owner + along >= 0) & (owner + along < owners)
        number = (region + up) * owners + owner + along
        numbers.append(jnp.where(inside & (number >= 0), number, -2))
    listed = jnp.any(neighbours.reshape(1, -1) == jnp.stack(numbers)[:, None], axis=1)
    present = jnp.concatenate([jnp.ones((1,), bool), listed])
    bias = jnp.repeat(jnp.where(present, 0.0, MASKED).astype(jnp.float32), block_size)[None, :]
    out = attend(
        listed.astype(jnp.int32), block, others, norm_gain[None, :], bias, full_qkv, full_out
    )
    return out.reshape(voxels.shape)


def solution(mesh):
    return jax.shard_map(
        shards,
        mesh=mesh,
        in_specs=(
            P("region", "owner", None, None, None),
            P(),
            P(("region", "owner"), None),
            P(("region", "owner"), None),
            P("region", "owner", None, None),
        ),
        out_specs=P("region", "owner", None, None, None),
        check_vma=False,
    )
```
